32 devices in a mesh: ctx: 2 (over x), tp: 4 (over z), fsdp: 4 (over y, core).
Axes of the slice: x: 2, y: 2, z: 4, core: 2. Of those that a mesh axis runs over, the one named last changes fastest.
Arguments:
- x_in: bfloat16 [2, 4, 1024, 2048], P(None, 'fsdp', 'ctx', 'tp'), may hold values from -6 to 6
- cotangent: bfloat16 [2, 4, 1024, 2048], P(None, 'fsdp', 'ctx', 'tp'), may hold values from -6 to 6
- offsets: int32 [2, 4, 4], P(None, 'fsdp'), may hold values from 0 to 960, as said below
- in_gain: float32 [2048], replicated, may hold values from 0.1 to 1.9
- w_z: bfloat16 [2048, 4096], P('fsdp', 'tp'), may hold values from -0.125 to 0.125
- w_x: bfloat16 [2048, 4096], P('fsdp', 'tp'), may hold values from -0.125 to 0.125
- w_dt: bfloat16 [2048, 64], P('fsdp', 'tp'), may hold values from -0.125 to 0.125
- w_bc: bfloat16 [2048, 256], P('fsdp', 'tp'), may hold values from -0.125 to 0.125
- conv_w: float32 [4, 4352], replicated, may hold values from -3 to 3
- conv_b: float32 [4352], replicated, may hold values from -0.5 to 0.5
- dt_bias: float32 [64], replicated, may hold values from -3 to -1
- a_log: float32 [64], replicated, may hold values from -9 to -1
- d_skip: float32 [64], replicated, may hold values from 0.5 to 1.5
- norm_gain: float32 [4096], replicated, may hold values from 0.1 to 1.9
- w_out: bfloat16 [4096, 2048], P('tp', 'fsdp'), may hold values from -0.09375 to 0.09375
Outputs:
- out: float32 [2, 4, 1024, 2048], P(None, 'fsdp', 'ctx', 'tp')
- d_x_in: float32 [2, 4, 1024, 2048], P(None, 'fsdp', 'ctx', 'tp')
- g_in_gain: float32 [2048], replicated
- g_w_z: float32 [2048, 4096], P(('ctx', 'fsdp'), 'tp')
- g_w_x: float32 [2048, 4096], P(('ctx', 'fsdp'), 'tp')
- g_w_dt: float32 [2048, 64], P(('ctx', 'fsdp'), 'tp')
- g_w_bc: float32 [2048, 256], P(('ctx', 'fsdp'), 'tp')
- g_conv_w: float32 [4, 4352], replicated
- g_conv_b: float32 [4352], replicated
- g_dt_bias: float32 [64], replicated
- g_a_log: float32 [64], replicated
- g_d_skip: float32 [64], replicated
- g_norm_gain: float32 [4096], replicated
- g_w_out: float32 [4096, 2048], P('tp', ('ctx', 'fsdp'))
The draws below stay inside these ranges and needn't reach their ends.
Inputs may be any that keep to these rules, and one draw needn't show every extreme that they name: Each row of offsets starts at 0 and rises strictly; one document of every sequence begins within its first 512 positions and ends within its last 512; the last document of every sequence begins at 1024 - 512 // (2 * 4).
All inputs are finite; a program needn't handle non-finite values.
Results may differ from the reference program's by a relative error of at most 0.011.
Values may be sent and summed in bfloat16 or wider, within the bound.
A program may use at most 256 MiB of HBM per device.

```python
import jax
import jax.numpy as jnp
from jax import lax

D = 2048
INNER = 4096
HEADS = 64
HEAD = 64
STATE = 128
CONV = 4
STRETCH = 256
L_DEV = 512
MB = 2
DOCS = 4
SEQS = 4
LEN = 1024
XBC = 4352


def draw_offsets(key, part):
    spacing = L_DEV // (2 * DOCS)
    key_pick, key_early, key_late = jax.random.split(key, 3)
    long_doc = jax.random.randint(key_pick, (MB, SEQS, 1), 0, DOCS - 1)
    doc_index = jnp.arange(DOCS, dtype=jnp.int32)[None, None, :]
    early_start = doc_index * spacing + jax.random.randint(key_early, (MB, SEQS, DOCS), 0, spacing)
    late_start = LEN - L_DEV // 2 + doc_index * spacing + jax.random.randint(key_late, (MB, SEQS, DOCS), 0, spacing)
    last_start = jnp.full((MB, SEQS, DOCS), LEN - spacing, jnp.int32)
    late_start = jnp.where(doc_index == DOCS - 1, last_start, late_start)
    starts = jnp.where(doc_index <= long_doc, early_start, late_start)
    return jnp.where(doc_index == 0, 0, starts).astype(jnp.int32)


def steps_of(own_key, extent, pieces, smallest, high):
    factor_of = 1.0
    for dim, blocks in pieces:
        draws = jax.random.uniform(jax.random.fold_in(jax.random.fold_in(own_key, 6), dim), (blocks,), jnp.float32, smallest / len(pieces), high / len(pieces))
        factor_of = factor_of * jnp.repeat(jnp.exp(draws), extent[dim] // blocks).reshape((-1,) + (1,) * (len(extent) - 1 - dim))
    return factor_of


def centred(own_key, shape, spread, limit, pieces=(), kind=jnp.bfloat16):
    values = spread * jax.random.normal(own_key, shape, jnp.float32)
    if pieces:
        values = values * steps_of(own_key, shape, pieces, -0.22, 0.18)
    return jnp.clip(values, -limit, limit).astype(kind)


def setup_inputs(seed: int = 0) -> dict:
    splits = jax.random.split(jax.random.key(seed), 16)
    x_in = centred(splits[0], (MB, SEQS, LEN, D), 1.0, 6.0, ((1, 4), (2, 2), (3, 4)))
    cotangent = centred(splits[1], (MB, SEQS, LEN, D), 1.0, 6.0, ((1, 4), (2, 2), (3, 4)))
    offsets = draw_offsets(jax.random.fold_in(splits[15], 71), 0)
    in_gain = jnp.clip(1.0 + 0.18 * jax.random.normal(splits[3], (D,), jnp.float32), 0.1, 1.9)
    w_z = centred(splits[4], (D, INNER), D ** -0.5, 0.125, ((0, 4), (1, 4)))
    w_x = centred(splits[5], (D, INNER), D ** -0.5, 0.125, ((0, 4), (1, 4)))
    w_dt = centred(splits[6], (D, HEADS), D ** -0.5, 0.125, ((0, 4), (1, 4)))
    w_bc = centred(splits[7], (D, 2 * STATE), D ** -0.5, 0.125, ((0, 4), (1, 4)))
    conv_w = centred(splits[8], (CONV, XBC), CONV ** -0.5, 3.0, (), jnp.float32)
    conv_b = jnp.clip(jax.random.uniform(splits[9], (XBC,), jnp.float32, -0.5, 0.5), -0.5, 0.5)
    dt_bias = jnp.clip(jax.random.uniform(splits[10], (HEADS,), jnp.float32, -3.0, -1.0), -3.0, -1.0)
    a_log = jnp.clip(jax.random.uniform(splits[11], (HEADS,), jnp.float32, -9.0, -1.0), -9.0, -1.0)
    d_skip = jnp.clip(jax.random.uniform(splits[12], (HEADS,), jnp.float32, 0.5, 1.5), 0.5, 1.5)
    norm_gain = jnp.clip(1.0 + 0.18 * jax.random.normal(splits[13], (INNER,), jnp.float32), 0.1, 1.9)
    w_out = centred(splits[14], (INNER, D), INNER ** -0.5, 0.09375, ((0, 4), (1, 4)))
    return {"x_in": x_in, "cotangent": cotangent, "offsets": offsets, "in_gain": in_gain, "w_z": w_z, "w_x": w_x, "w_dt": w_dt, "w_bc": w_bc, "conv_w": conv_w, "conv_b": conv_b, "dt_bias": dt_bias, "a_log": a_log, "d_skip": d_skip, "norm_gain": norm_gain, "w_out": w_out}


@jax.custom_vjp
def low(v):
    return lax.optimization_barrier(v.astype(jnp.bfloat16)).astype(jnp.float32)

@jax.custom_vjp
def low_back(v):
    return v

def low_keep(v):
    return (low(v), None)

def low_pass(kept, grad):
    return (grad,)

def back_keep(v):
    return (v, None)

def back_low(kept, grad):
    return (low(grad),)
low.defvjp(low_keep, low_pass)
low_back.defvjp(back_keep, back_low)
EPSILON = 1e-05
PRECISE = lax.Precision.HIGHEST

def exact_dot(first_op, second_op):
    return jnp.dot(first_op, second_op, precision=PRECISE, preferred_element_type=jnp.float32)

def doc_numbers(starts, places):
    return lax.optimization_barrier(jnp.sum((starts[..., None, :] <= places[..., :, None]).astype(jnp.int32), axis=-1)) - 1

def stretch_step(carry_state, inputs):
    values, write_vec, read_vec, log_decay, step_size, doc_ids, before = inputs
    span_len = doc_ids.shape[0]
    running = jnp.cumsum(log_decay, axis=0)
    places = jnp.arange(span_len)
    same_doc = (doc_ids[:, None] == doc_ids[None, :]) & (places[:, None] >= places[None, :])
    scores = exact_dot(read_vec, write_vec.T)
    by_head = running.T
    spread_log = by_head[:, :, None] - by_head[:, None, :]
    allowed = same_doc[None, :, :]
    weights = jnp.where(allowed, jnp.exp(jnp.where(allowed, spread_log, 0.0)), 0.0)
    weights = weights * scores[None, :, :] * step_size.T[:, None, :]
    result = jnp.einsum('hts,shp->thp', weights, values, precision=PRECISE)
    kept_mask = (doc_ids == before).astype(jnp.float32)
    lead_decay = jnp.exp(running) * kept_mask[:, None]
    result = result + lead_decay[:, :, None] * jnp.einsum('tn,hpn->thp', read_vec, carry_state, precision=PRECISE)
    tail_decay = jnp.exp(running[-1][None, :] - running) * (doc_ids == doc_ids[-1]).astype(jnp.float32)[:, None] * step_size
    fresh_state = jnp.einsum('shp,sn->hpn', tail_decay[:, :, None] * values, write_vec, precision=PRECISE)
    return (lead_decay[-1][:, None, None] * carry_state + fresh_state, result)

def local_scan(values, write_vec, read_vec, log_decay, step_size, doc_ids):
    length = doc_ids.shape[0]
    blocks = length // STRETCH
    before = jnp.concatenate([jnp.full((1,), -1, jnp.int32), doc_ids[STRETCH - 1:length - 1:STRETCH].astype(jnp.int32)])

    def blocked(tensor):
        return tensor.reshape((blocks, STRETCH) + tensor.shape[1:])
    start_state = jnp.zeros((values.shape[1], values.shape[2], write_vec.shape[1]), jnp.float32)
    final_state, results = lax.scan(jax.checkpoint(stretch_step), start_state, (blocked(values), blocked(write_vec), blocked(read_vec), blocked(log_decay), blocked(step_size), blocked(doc_ids), before))
    return (results.reshape(values.shape), final_state)

def layer(resid, doc_ids, in_gain, w_z, w_x, w_dt, w_bc, conv_w, conv_b, dt_bias, a_log, d_skip, norm_gain, w_out):
    length = resid.shape[0]
    inv_rms = lax.rsqrt(lax.optimization_barrier(jnp.mean(resid * resid, axis=1, keepdims=True)) + EPSILON)
    normed = low(resid * inv_rms * in_gain)
    gate_raw = low_back(exact_dot(normed, w_z))
    conv_x = low(low_back(exact_dot(normed, w_x)))
    conv_bc = low(exact_dot(normed, w_bc))
    step_raw = low_back(exact_dot(normed, w_dt))
    conv_in = jnp.concatenate([conv_x, conv_bc], axis=1)
    conv_out = jnp.broadcast_to(conv_b[None, :], conv_in.shape)
    for k in range(CONV):
        lag_rows = CONV - 1 - k
        shifted_in = jnp.pad(conv_in, ((lag_rows, 0), (0, 0)))[:length]
        shifted_doc = jnp.pad(doc_ids, (lag_rows, 0), constant_values=-1)[:length]
        same_doc = (shifted_doc == doc_ids).astype(jnp.float32)
        conv_out = conv_out + conv_w[k][None, :] * shifted_in * same_doc[:, None]
    activ = jax.nn.silu(conv_out)
    values = activ[:, :INNER].reshape(length, HEADS, HEAD)
    write_vec = activ[:, INNER:INNER + STATE]
    read_vec = activ[:, INNER + STATE:]
    step_size = jax.nn.softplus(step_raw + dt_bias)
    log_decay = -step_size * jnp.exp(a_log)
    core_out, ending = local_scan(values, write_vec, read_vec, log_decay, step_size, doc_ids)
    mixed = core_out + d_skip[:, None] * values
    gated = mixed.reshape(length, INNER) * jax.nn.silu(gate_raw)
    gate_rms = lax.rsqrt(lax.optimization_barrier(jnp.mean(gated * gated, axis=1, keepdims=True)) + EPSILON)
    gate_norm = low(gated * gate_rms * norm_gain)
    return resid + exact_dot(gate_norm, w_out)

def reference(x_in, cotangent, offsets, in_gain, w_z, w_x, w_dt, w_bc, conv_w, conv_b, dt_bias, a_log, d_skip, norm_gain, w_out):
    params = (in_gain, w_z.astype(jnp.float32), w_x.astype(jnp.float32), w_dt.astype(jnp.float32), w_bc.astype(jnp.float32), conv_w, conv_b, dt_bias, a_log, d_skip, norm_gain, w_out.astype(jnp.float32))
    rows_in = x_in.astype(jnp.float32).reshape(MB * SEQS, LEN, D)
    rows_back = cotangent.astype(jnp.float32).reshape(MB * SEQS, LEN, D)
    rows_doc = offsets.reshape(MB * SEQS, DOCS)
    places = jnp.arange(LEN, dtype=jnp.int32)

    def one_row(totals, row_data):
        resid, cot_row, starts = row_data
        doc_ids = doc_numbers(starts, places)

        def forward(resid_in, *weights):
            return layer(resid_in, doc_ids, *weights)
        output, pullback = jax.vjp(forward, resid, *params)
        gradients = pullback(cot_row)
        return (tuple((running_sum + piece_grad for running_sum, piece_grad in zip(totals, gradients[1:]))), (output, gradients[0]))
    zero_init = tuple((jnp.zeros_like(param_item) for param_item in params))
    totals, (outputs, in_grads) = lax.scan(one_row, zero_init, (rows_in, rows_back, rows_doc))
    full_shape = (MB, SEQS, LEN, D)
    return (outputs.reshape(full_shape), in_grads.reshape(full_shape), totals[0], totals[1], totals[2], totals[3], totals[4], totals[5], totals[6], totals[7], totals[8], totals[9], totals[10], totals[11])
```

```python
import functools

import jax
import jax.numpy as jnp
from jax import lax
from jax.experimental import pallas as pl
from jax.experimental.pallas import tpu as pltpu
from jax.sharding import PartitionSpec as P

EPSILON = 1e-05
PRECISE = lax.Precision.HIGHEST
LANES = 128
CHUNK = 128
FAR = -1e30
F32 = jnp.float32
BF16 = jnp.bfloat16


def mm(a, b, dims=((1,), (0,)), precision=None):
    return lax.dot_general(a, b, (dims, ((), ())), precision=precision, preferred_element_type=F32)


NN = ((1,), (0,))
NT = ((1,), (1,))
TN = ((0,), (0,))


def softplus(v):
    return jnp.maximum(v, 0.0) + jnp.log1p(jnp.exp(-jnp.abs(v)))


def silu_slope(v, sig):
    return sig * (1.0 + v * (1.0 - sig))


def doc_of(off_ref, seq, pos):
    count = jnp.zeros_like(pos)
    for j in range(off_ref.shape[1]):
        count = count + (off_ref[seq, j] <= pos).astype(jnp.int32)
    return count


def widen(cols, head, lane, width):
    out = cols[:, head : head + 1]
    for i in range(1, LANES // width):
        out = jnp.where(lane >= i * width, cols[:, head + i : head + i + 1], out)
    return jnp.broadcast_to(out, (cols.shape[0], LANES))


class Span:
    def __init__(self, off_ref, pos_ref, seq, start, q, dtr, dtb, rate, taps):
        first = pos_ref[0]
        at = first + start
        col = at + lax.broadcasted_iota(jnp.int32, (q, 1), 0)
        row = at + lax.broadcasted_iota(jnp.int32, (1, q), 1)
        dcol = doc_of(off_ref, seq, col)
        drow = doc_of(off_ref, seq, row)
        before = doc_of(off_ref, seq, at - 1)
        before_dev = doc_of(off_ref, seq, first - 1)
        last = doc_of(off_ref, seq, at + q - 1)
        self.match = [
            (doc_of(off_ref, seq, col - (taps - 1 - k)) == dcol).astype(F32) for k in range(taps - 1)
        ]
        self.far = jnp.where((dcol == drow) & (col >= row), 0.0, FAR)
        self.kept = (dcol == before).astype(F32)
        self.kept_dev = (dcol == before_dev).astype(F32)
        self.carry_dev = (before == before_dev).astype(F32)
        self.dt_in = dtr + dtb
        self.dt = softplus(self.dt_in)
        decay = self.dt * rate
        tri = (
            lax.broadcasted_iota(jnp.int32, (q, q), 0) >= lax.broadcasted_iota(jnp.int32, (q, q), 1)
        ).astype(F32)
        self.tri = tri
        self.cum = mm(tri, decay, precision=PRECISE)
        self.cum_t = self.cum.T
        self.lead = jnp.exp(self.cum) * self.kept
        end = self.cum[q - 1 : q, :]
        self.tail = jnp.exp(end - self.cum) * (dcol == last).astype(F32)
        self.end = end

    def fade(self, head):
        return jnp.exp(self.cum[:, head : head + 1] - self.cum_t[head : head + 1, :] + self.far)


def conv_block(pre, halo, cw, cb, match):
    taps = len(match) + 1
    ext = jnp.concatenate([halo, pre], axis=0)
    shifted = [
        pltpu.roll(ext, taps - 1 - k, 0)[8:] * match[k] for k in range(taps - 1)
    ] + [pre]
    conv = cb
    for k in range(taps):
        conv = conv + cw[k : k + 1] * shifted[k]
    return conv, shifted


def scan_kernel(dims, off, pos, pre, rim, dtr, cw, cb, dtb, rate, dsk, y, rd, lead, st, lead0, fin, halo, state, run):
    q, inner, width, n = dims
    b, c = pl.program_id(0), pl.program_id(1)

    @pl.when(c == 0)
    def _():
        halo[...] = rim[0]
        state[...] = jnp.zeros_like(state)
        run[...] = jnp.zeros_like(run)

    taps = cw.shape[0]
    sp = Span(off, pos, b, c * q, q, dtr[0], dtb[...], rate[...], taps)
    total = run[...] + sp.cum
    lead[0] = jnp.exp(total) * sp.kept_dev
    lead0[0, 0] = jnp.broadcast_to(jnp.exp(run[...]) * sp.carry_dev, (8, LANES))
    run[...] = total[q - 1 : q]

    def act(lo, hi):
        conv, _ = conv_block(
            pre[0, :, lo:hi].astype(F32), halo[:, lo:hi], cw[:, lo:hi], cb[:, lo:hi], sp.match
        )
        return conv * jax.nn.sigmoid(conv)

    write = act(inner, inner + n).astype(BF16)
    read = act(inner + n, inner + 2 * n).astype(BF16)
    rd[0] = read
    scores = mm(read, write, NT)
    write_t = write.astype(F32).T.astype(BF16)
    lane = lax.broadcasted_iota(jnp.int32, (1, LANES), 1)
    per = LANES // width
    for j in range(inner // LANES):
        lo, hi = j * LANES, (j + 1) * LANES
        h = j * per
        xs = act(lo, hi)
        xdt = xs * widen(sp.dt, h, lane, width)
        xdt_low = xdt.astype(BF16)
        mixed = None
        for i in range(per):
            part = mm((sp.fade(h + i) * scores).astype(BF16), xdt_low)
            mixed = part if mixed is None else jnp.where(lane >= i * width, part, mixed)
        old = state[:, lo:hi]
        st[0, 0, :, lo:hi] = old
        mixed = mixed + widen(sp.lead, h, lane, width) * mm(read, old.astype(BF16))
        y[0, :, lo:hi] = mixed + dsk[:, lo:hi] * xs
        fresh = mm(write_t, (xdt * widen(sp.tail, h, lane, width)).astype(BF16))
        new = widen(sp.lead[q - 1 : q], h, lane, width) * old + fresh
        state[:, lo:hi] = new
        fin[0, :, lo:hi] = new
    halo[...] = pre[0, q - 8 : q].astype(F32)


def gate_kernel(dims, y_in, rd, lead, lead0, st, s_in, z, gain, y, ygg, sq, st_full):
    q, inner, width, n = dims
    lane = lax.broadcasted_iota(jnp.int32, (1, LANES), 1)
    per = LANES // width
    total = jnp.zeros((q, LANES), F32)
    for j in range(inner // LANES):
        lo, hi = j * LANES, (j + 1) * LANES
        h = j * per
        came = s_in[0, :, lo:hi]
        st_full[0, 0, :, lo:hi] = st[0, 0, :, lo:hi] + widen(lead0[0, 0, 0:1], h, lane, width) * came
        val = y_in[0, :, lo:hi] + widen(lead[0], h, lane, width) * mm(rd[0], came.astype(BF16))
        y[0, :, lo:hi] = val
        gate = z[0, :, lo:hi]
        gated = val * gate * jax.nn.sigmoid(gate)
        total = total + gated * gated
        ygg[0, :, lo:hi] = (gated * gain[:, lo:hi]).astype(BF16)
    sq[0] = jnp.broadcast_to(jnp.sum(total, axis=1, keepdims=True), (q, LANES))


def ungate_kernel(dims, count, dyn, y, z, stat, gain, rd, lead, dy, dz, yn, g_gain, g_state):
    q, inner, width, n = dims
    b, c = pl.program_id(0), pl.program_id(1)

    @pl.when((b == 0) & (c == 0))
    def _():
        g_gain[...] = jnp.zeros_like(g_gain)

    @pl.when(c == 0)
    def _():
        g_state[...] = jnp.zeros_like(g_state)

    lane = lax.broadcasted_iota(jnp.int32, (1, LANES), 1)
    per = LANES // width
    r2 = stat[0, :, 0:1]
    coef = r2 * r2 * r2 * stat[0, :, 1:2] * (1.0 / count)
    read_t = rd[0].astype(F32).T.astype(BF16)
    for j in range(inner // LANES):
        lo, hi = j * LANES, (j + 1) * LANES
        h = j * per
        gate = z[0, :, lo:hi]
        sig = jax.nn.sigmoid(gate)
        act = gate * sig
        val = y[0, :, lo:hi]
        gated = val * act
        dn = dyn[0, :, lo:hi]
        g = gain[:, lo:hi]
        norm = gated * r2
        g_gain[0:1, lo:hi] += jnp.sum(dn * norm, axis=0, keepdims=True)
        yn[0, :, lo:hi] = (norm * g).astype(BF16)
        d_gated = r2 * (dn * g) - gated * coef
        d_core = d_gated * act
        dy[0, :, lo:hi] = d_core
        dz[0, :, lo:hi] = (d_gated * val * silu_slope(gate, sig)).astype(BF16)
        g_state[0, :, lo:hi] += mm(read_t, (d_core * widen(lead[0], h, lane, width)).astype(BF16))


def back_kernel(dims, off, pos, pre, prev, rim, dtr, y, dy, st, d_in, cw, cb, dtb, rate, dsk,
                dcat, ddt_out, edge, rim_grad, acc, acc_head, d_state, carry):
    q, inner, width, n = dims
    b, c = pl.program_id(0), pl.program_id(1)
    chunks = pl.num_programs(1)
    at = chunks - 1 - c

    @pl.when((b == 0) & (c == 0))
    def _():
        acc[...] = jnp.zeros_like(acc)
        acc_head[...] = jnp.zeros_like(acc_head)

    @pl.when(c == 0)
    def _():
        d_state[...] = d_in[0]
        carry[...] = jnp.zeros_like(carry)

    taps = cw.shape[0]
    sp = Span(off, pos, b, at * q, q, dtr[0], dtb[...], rate[...], taps)
    lane = lax.broadcasted_iota(jnp.int32, (1, LANES), 1)
    per = LANES // width

    def conv(lo, hi):
        ahead = jnp.where(at == 0, rim[0, :, lo:hi], prev[0, 8:16, lo:hi].astype(F32))
        return conv_block(pre[0, :, lo:hi].astype(F32), ahead, cw[:, lo:hi], cb[:, lo:hi], sp.match)

    def unconv(lo, hi, d_act, out, shifted, sig):
        d_conv = d_act * silu_slope(out, sig)
        acc[taps : taps + 1, lo:hi] += jnp.sum(d_conv, axis=0, keepdims=True)
        d_ext = None
        zeros = jnp.zeros((8, hi - lo), F32)
        for k in range(taps):
            acc[k : k + 1, lo:hi] += jnp.sum(d_conv * shifted[k], axis=0, keepdims=True)
            masked = cw[k : k + 1, lo:hi] * d_conv
            if k < taps - 1:
                masked = masked * sp.match[k]
            part = jnp.concatenate([zeros, masked], axis=0)
            if k < taps - 1:
                part = pltpu.roll(part, q + 8 - (taps - 1 - k), 0)
            d_ext = part if d_ext is None else d_ext + part
        d_pre = jnp.concatenate([d_ext[8:q], d_ext[q:] + carry[:, lo:hi]], axis=0)
        carry[:, lo:hi] = d_ext[0:8]
        rim_grad[0, :, lo:hi] = d_ext[0:8]
        dcat[0, :, lo:hi] = d_pre.astype(BF16)

        @pl.when(c == 0)
        def _():
            edge[0, :, lo:hi] = d_pre[q - 8 : q]

    w_conv, w_shift = conv(inner, inner + n)
    w_sig = jax.nn.sigmoid(w_conv)
    write = (w_conv * w_sig).astype(BF16)
    r_conv, r_shift = conv(inner + n, inner + 2 * n)
    r_sig = jax.nn.sigmoid(r_conv)
    read = (r_conv * r_sig).astype(BF16)
    scores = mm(read, write, NT)
    read_t = read.astype(F32).T.astype(BF16)
    d_scores = jnp.zeros((q, q), F32)
    d_write = jnp.zeros((q, n), F32)
    d_read = jnp.zeros((q, n), F32)
    d_cum = jnp.zeros((q, LANES), F32)
    d_step = jnp.zeros((q, LANES), F32)
    d_end = jnp.zeros((8, LANES), F32)
    for j in range(inner // LANES):
        lo, hi = j * LANES, (j + 1) * LANES
        h = j * per
        x_conv, x_shift = conv(lo, hi)
        x_sig = jax.nn.sigmoid(x_conv)
        xs = x_conv * x_sig
        step = widen(sp.dt, h, lane, width)
        xdt = xs * step
        xdt_low = xdt.astype(BF16)
        grad = dy[0, :, lo:hi]
        grad_low = grad.astype(BF16)
        core = y[0, :, lo:hi] - dsk[:, lo:hi] * xs
        late = d_state[:, lo:hi]
        late_low = late.astype(BF16)
        early = st[0, 0, :, lo:hi]
        tail = widen(sp.tail, h, lane, width)
        lead = widen(sp.lead, h, lane, width)
        u = None
        for i in range(per):
            fade = sp.fade(h + i)
            here = (lane >= i * width) & (lane < (i + 1) * width)
            own = jnp.where(here, grad, 0.0).astype(BF16)
            d_scores = d_scores + mm(own, xdt_low, NT) * fade
            part = mm((fade * scores).astype(BF16), grad_low, TN)
            u = part if u is None else jnp.where(lane >= i * width, part, u)
        from_end = tail * mm(write, late_low)
        u = u + from_end
        weighted = (lead * grad).astype(BF16)
        d_read = d_read + mm(weighted, early.astype(BF16), NT)
        d_write = d_write + mm((xdt * tail).astype(BF16), late_low, NT)
        end_lead = widen(sp.lead[q - 1 : q], h, lane, width)
        d_state[:, lo:hi] = end_lead * late + mm(read_t, weighted)
        head_of = (
            lax.broadcasted_iota(jnp.int32, (LANES, LANES), 0) // width + h
            == lax.broadcasted_iota(jnp.int32, (LANES, LANES), 1)
        ).astype(F32)
        d_cum = d_cum + mm(grad * core - xdt * u, head_of, precision=PRECISE)
        d_step = d_step + mm(xs * u, head_of, precision=PRECISE)
        end_row = end_lead * jnp.sum(late * early, axis=0, keepdims=True) + jnp.sum(
            xdt * from_end, axis=0, keepdims=True
        )
        d_end = d_end + mm(jnp.broadcast_to(end_row, (8, LANES)), head_of, precision=PRECISE)
        acc[taps + 1 : taps + 2, lo:hi] += jnp.sum(grad * xs, axis=0, keepdims=True)
        unconv(lo, hi, step * u + dsk[:, lo:hi] * grad, x_conv, x_shift, x_sig)
    d_low = d_scores.astype(BF16)
    d_read = d_read + mm(d_low, write)
    d_write = d_write + mm(d_low, read, TN)
    unconv(inner, inner + n, d_write, w_conv, w_shift, w_sig)
    unconv(inner + n, inner + 2 * n, d_read, r_conv, r_shift, r_sig)
    d_decay = mm(sp.tri, d_cum, TN, precision=PRECISE) + d_end[0:1]
    acc_head[0:1] += jnp.sum(d_decay * sp.dt, axis=0, keepdims=True) * rate[...]
    d_dt = (d_step + d_decay * rate[...]) * jax.nn.sigmoid(sp.dt_in)
    acc_head[1:2] += jnp.sum(d_dt, axis=0, keepdims=True)
    ddt_out[0] = d_dt.astype(BF16)


def whole(shape):
    return pl.BlockSpec(shape, lambda *_: (0,) * len(shape))


def params():
    return pltpu.CompilerParams(vmem_limit_bytes=48 << 20)


def scan_forward(offs, pos, pre, rim, dtr, cw, cb, dtb, rate, dsk, width, n):
    nb, length, chans = pre.shape
    inner = dsk.shape[1]
    q = min(CHUNK, length)
    chunks = length // q
    dims = (q, inner, width, n)

    def rows(size):
        return pl.BlockSpec((1, q, size), lambda b, c, *_: (b, c, 0))

    return pl.pallas_call(
        functools.partial(scan_kernel, dims),
        grid_spec=pltpu.PrefetchScalarGridSpec(
            num_scalar_prefetch=2,
            grid=(nb, chunks),
            in_specs=[
                rows(chans),
                pl.BlockSpec((1, 8, chans), lambda b, c, *_: (b, 0, 0)),
                rows(LANES),
                whole(cw.shape),
                whole(cb.shape),
                whole(dtb.shape),
                whole(rate.shape),
                whole(dsk.shape),
            ],
            out_specs=[
                rows(inner),
                rows(n),
                rows(LANES),
                pl.BlockSpec((1, 1, n, inner), lambda b, c, *_: (b, c, 0, 0)),
                pl.BlockSpec((1, 1, 8, LANES), lambda b, c, *_: (b, c, 0, 0)),
                pl.BlockSpec((1, n, inner), lambda b, c, *_: (b, 0, 0)),
            ],
            scratch_shapes=[
                pltpu.VMEM((8, chans), F32),
                pltpu.VMEM((n, inner), F32),
                pltpu.VMEM((1, LANES), F32),
            ],
        ),
        out_shape=[
            jax.ShapeDtypeStruct((nb, length, inner), F32),
            jax.ShapeDtypeStruct((nb, length, n), BF16),
            jax.ShapeDtypeStruct((nb, length, LANES), F32),
            jax.ShapeDtypeStruct((nb, chunks, n, inner), F32),
            jax.ShapeDtypeStruct((nb, chunks, 8, LANES), F32),
            jax.ShapeDtypeStruct((nb, n, inner), F32),
        ],
        compiler_params=params(),
        name="scan_forward",
    )(offs, pos, pre, rim, dtr, cw, cb, dtb, rate, dsk)


def gate_forward(y_in, rd, lead, lead0, st, s_in, z, gain, width):
    nb, length, inner = y_in.shape
    chunks, n = st.shape[1], st.shape[2]
    q = length // chunks
    dims = (q, inner, width, n)

    def rows(size):
        return pl.BlockSpec((1, q, size), lambda b, c: (b, c, 0))

    def per_chunk(r, size):
        return pl.BlockSpec((1, 1, r, size), lambda b, c: (b, c, 0, 0))

    return pl.pallas_call(
        functools.partial(gate_kernel, dims),
        grid=(nb, chunks),
        in_specs=[
            rows(inner),
            rows(n),
            rows(LANES),
            per_chunk(8, LANES),
            per_chunk(n, inner),
            pl.BlockSpec((1, n, inner), lambda b, c: (b, 0, 0)),
            rows(inner),
            whole(gain.shape),
        ],
        out_specs=[rows(inner), rows(inner), rows(LANES), per_chunk(n, inner)],
        out_shape=[
            jax.ShapeDtypeStruct((nb, length, inner), F32),
            jax.ShapeDtypeStruct((nb, length, inner), BF16),
            jax.ShapeDtypeStruct((nb, length, LANES), F32),
            jax.ShapeDtypeStruct(st.shape, F32),
        ],
        compiler_params=params(),
        name="gate_forward",
    )(y_in, rd, lead, lead0, st, s_in, z, gain)


def gate_backward(dyn, y, z, stat, gain, rd, lead, width, count):
    nb, length, inner = y.shape
    n = rd.shape[2]
    q = min(CHUNK, length)
    chunks = length // q
    dims = (q, inner, width, n)

    def rows(size):
        return pl.BlockSpec((1, q, size), lambda b, c: (b, c, 0))

    return pl.pallas_call(
        functools.partial(ungate_kernel, dims, count),
        grid=(nb, chunks),
        in_specs=[
            rows(inner),
            rows(inner),
            rows(inner),
            rows(LANES),
            whole(gain.shape),
            rows(n),
            rows(LANES),
        ],
        out_specs=[
            rows(inner),
            rows(inner),
            rows(inner),
            whole((8, inner)),
            pl.BlockSpec((1, n, inner), lambda b, c: (b, 0, 0)),
        ],
        out_shape=[
            jax.ShapeDtypeStruct((nb, length, inner), F32),
            jax.ShapeDtypeStruct((nb, length, inner), BF16),
            jax.ShapeDtypeStruct((nb, length, inner), BF16),
            jax.ShapeDtypeStruct((8, inner), F32),
            jax.ShapeDtypeStruct((nb, n, inner), F32),
        ],
        compiler_params=params(),
        name="gate_backward",
    )(dyn, y, z, stat, gain, rd, lead)


def scan_backward(offs, pos, pre, rim, dtr, y, dy, st, d_in, cw, cb, dtb, rate, dsk, width):
    nb, length, chans = pre.shape
    inner = dsk.shape[1]
    chunks, n = st.shape[1], st.shape[2]
    q = length // chunks
    dims = (q, inner, width, n)
    per = q // 16

    def rows(size):
        return pl.BlockSpec((1, q, size), lambda b, c, *_: (b, chunks - 1 - c, 0))

    def per_seq(r, size):
        return pl.BlockSpec((1, r, size), lambda b, c, *_: (b, 0, 0))

    return pl.pallas_call(
        functools.partial(back_kernel, dims),
        grid_spec=pltpu.PrefetchScalarGridSpec(
            num_scalar_prefetch=2,
            grid=(nb, chunks),
            in_specs=[
                rows(chans),
                pl.BlockSpec(
                    (1, 16, chans), lambda b, c, *_: (b, jnp.maximum((chunks - 1 - c) * per - 1, 0), 0)
                ),
                per_seq(8, chans),
                rows(LANES),
                rows(inner),
                rows(inner),
                pl.BlockSpec((1, 1, n, inner), lambda b, c, *_: (b, chunks - 1 - c, 0, 0)),
                per_seq(n, inner),
                whole(cw.shape),
                whole(cb.shape),
                whole(dtb.shape),
                whole(rate.shape),
                whole(dsk.shape),
            ],
            out_specs=[
                rows(chans),
                rows(LANES),
                per_seq(8, chans),
                per_seq(8, chans),
                whole((8, chans)),
                whole((8, LANES)),
            ],
            scratch_shapes=[pltpu.VMEM((n, inner), F32), pltpu.VMEM((8, chans), F32)],
        ),
        out_shape=[
            jax.ShapeDtypeStruct((nb, length, chans), BF16),
            jax.ShapeDtypeStruct((nb, length, LANES), BF16),
            jax.ShapeDtypeStruct((nb, 8, chans), F32),
            jax.ShapeDtypeStruct((nb, 8, chans), F32),
            jax.ShapeDtypeStruct((8, chans), F32),
            jax.ShapeDtypeStruct((8, LANES), F32),
        ],
        compiler_params=params(),
        name="scan_backward",
    )(offs, pos, pre, pre, rim, dtr, y, dy, st, d_in, cw, cb, dtb, rate, dsk)


def shift(arr, axis, by):
    peers = lax.axis_size(axis)
    pairs = [(i, i + by) for i in range(peers) if 0 <= i + by < peers]
    return lax.ppermute(arr, axis, pairs)


def heads_row(vec, width=LANES):
    return jnp.pad(vec[None], ((0, 0), (0, width - vec.shape[0])))


def on_device(
    x_in,
    cotangent,
    offsets,
    in_gain,
    w_z,
    w_x,
    w_dt,
    w_bc,
    conv_w,
    conv_b,
    dt_bias,
    a_log,
    d_skip,
    norm_gain,
    w_out,
):
    batches, seq_count, length, width_dev = x_in.shape
    nb = batches * seq_count
    tokens = nb * length
    tp_rank = lax.axis_index("tp")
    ctx_rank = lax.axis_index("ctx")
    peers = lax.axis_size("ctx")
    inner = w_z.shape[1]
    heads = w_dt.shape[1]
    width = inner // heads
    model = in_gain.shape[0]
    inner_all = norm_gain.shape[0]
    pair = conv_w.shape[1] - inner_all
    n = pair // 2
    taps = conv_w.shape[0]

    def mine(arr, size, axis):
        return lax.dynamic_slice_in_dim(arr, tp_rank * size, size, axis)

    cw = jnp.concatenate([mine(conv_w, inner, 1), conv_w[:, inner_all:]], axis=1)
    cb = jnp.concatenate([mine(conv_b, inner, 0), conv_b[inner_all:]])[None]
    gain = mine(norm_gain, inner, 0)[None]
    gain_in = mine(in_gain, width_dev, 0)
    dtb = heads_row(mine(dt_bias, heads, 0))
    rate = heads_row(-jnp.exp(mine(a_log, heads, 0)))
    dsk = jnp.repeat(mine(d_skip, heads, 0), width)[None]
    pos = (ctx_rank * length).astype(jnp.int32)[None]
    offs = offsets.reshape(nb, offsets.shape[-1])

    x_own = x_in.reshape(tokens, width_dev)
    cot_own = cotangent.reshape(tokens, width_dev)
    x_all = lax.all_gather(x_own, "tp", axis=1, tiled=True)
    small = jnp.concatenate([w_bc, w_dt], axis=1)
    small = lax.all_gather(small, "fsdp", axis=0, tiled=True)
    wdt = jnp.pad(small[:, pair // lax.axis_size("tp") :], ((0, 0), (0, LANES - heads)))
    wbc = lax.all_gather(small[:, : pair // lax.axis_size("tp")], "tp", axis=1, tiled=True)
    wx = lax.all_gather(w_x, "fsdp", axis=0, tiled=True)
    wz = lax.all_gather(w_z, "fsdp", axis=0, tiled=True)
    wo = lax.all_gather(w_out, "fsdp", axis=1, tiled=True)
    cot_all = lax.all_gather(cot_own, "tp", axis=1, tiled=True)
    wxbc = jnp.concatenate([wx, wbc], axis=1)

    resid = x_all.astype(F32)
    r1 = lax.rsqrt(jnp.mean(resid * resid, axis=1, keepdims=True) + EPSILON)
    xn = (resid * r1 * in_gain).astype(BF16)
    pre = mm(xn, wxbc).astype(BF16).reshape(nb, length, inner + pair)
    dtr = mm(xn, wdt).reshape(nb, length, LANES)
    z = mm(xn, wz).reshape(nb, length, inner)
    rim = shift(pre[:, length - 8 :], "ctx", 1).astype(F32)
    y, rd, lead, st, lead0, fin = scan_forward(
        offs, pos, pre, rim, dtr, cw, cb, dtb, rate, dsk, width, n
    )
    lend = jnp.repeat(lead[:, length - 1, :heads], width, axis=-1)[:, None]

    def chained(start, by):
        came = jnp.zeros_like(start)
        for k in range(peers - 1):
            sent = start if k == 0 else start + lend * came
            came = shift(sent.astype(BF16), "ctx", by).astype(F32)
        return came

    s_in = chained(fin, 1)
    y, ygg, sq, st = gate_forward(y, rd, lead, lead0, st, s_in, z, gain, width)
    part = mm(ygg.reshape(tokens, inner), wo).astype(BF16)
    share = lax.psum_scatter(part, "tp", scatter_dimension=1, tiled=True)
    dyn = mm(cot_all, wo, NT).reshape(nb, length, inner)
    dot = jnp.sum(dyn * gain * y * jax.nn.silu(z), axis=2)
    stat = jnp.stack([sq[..., 0], dot])
    stat = jnp.sum(lax.all_gather(stat, "tp"), axis=0)
    r2 = lax.rsqrt(stat[0] / inner_all + EPSILON)
    out = x_own.astype(F32) + r2.reshape(tokens, 1) * share.astype(F32)
    stat = jnp.pad(jnp.stack([r2, stat[1]], axis=-1), ((0, 0), (0, 0), (0, LANES - 2)))
    dy, dz, yn, g_gain, g_state = gate_backward(dyn, y, z, stat, gain, rd, lead, width, inner_all)
    dz = dz.reshape(tokens, inner)
    yn = yn.reshape(tokens, inner)
    d_in = chained(g_state, -1)
    rows = ("ctx", "fsdp")

    def scattered(grad):
        return lax.psum_scatter(grad.astype(BF16), rows, scatter_dimension=0, tiled=True)

    g_out = scattered(mm(cot_all, yn, TN)).astype(F32).T
    g_z = scattered(mm(xn, dz, TN)).astype(F32)
    dcat, ddt, edge, rim_grad, acc, acc_head = scan_backward(
        offs, pos, pre, rim, dtr, y, dy, st, d_in, cw, cb, dtb, rate, dsk, width
    )
    edge = (edge + shift(rim_grad, "ctx", -1)).astype(BF16)
    dcat = lax.dynamic_update_slice(dcat, edge, (0, length - 8, 0)).reshape(tokens, inner + pair)
    ddt = ddt.reshape(tokens, LANES)
    dxn = mm(dz, wz, NT) + mm(dcat, wxbc, NT) + mm(ddt, wdt, NT)
    dxn = lax.psum_scatter(dxn.astype(BF16), "tp", scatter_dimension=1, tiled=True).astype(F32)
    g_xbc = scattered(jnp.concatenate([mm(xn, dcat, TN), mm(xn, ddt, TN)[:, :heads]], axis=1))
    g_x = g_xbc[:, :inner].astype(F32)
    g_dt = g_xbc[:, inner + pair :].astype(F32)
    g_bc = lax.psum_scatter(
        g_xbc[:, inner : inner + pair].astype(F32), "tp", scatter_dimension=1, tiled=True
    )
    h_own = x_own.astype(F32)
    scaled = dxn * gain_in
    in_dot = jnp.sum(lax.all_gather(jnp.sum(scaled * h_own, axis=1), "tp"), axis=0)[:, None]
    g_in = jnp.sum(dxn * h_own * r1, axis=0)
    d_x = cot_own.astype(F32) + r1 * scaled - h_own * r1**3 * in_dot / model
    pieces = [
        g_in,
        acc[:taps, :inner].reshape(-1),
        acc[taps, :inner],
        g_gain[0],
        acc_head[1, :heads],
        acc_head[0, :heads],
        acc[taps + 1, :inner].reshape(heads, width).sum(axis=1),
        acc[:taps, inner:].reshape(-1),
        acc[taps, inner:],
    ]
    sizes = [p.shape[0] for p in pieces]
    packed = jnp.sum(lax.all_gather(jnp.concatenate(pieces), rows), axis=0)
    packed = lax.all_gather(packed, "tp")
    parts, start = [], 0
    for size in sizes:
        parts.append(packed[:, start : start + size])
        start += size
    tp = packed.shape[0]
    g_cw = jnp.concatenate(
        [
            parts[1].reshape(tp, taps, inner).transpose(1, 0, 2).reshape(taps, inner_all),
            jnp.sum(parts[7], axis=0).reshape(taps, pair),
        ],
        axis=1,
    )
    g_cb = jnp.concatenate([parts[2].reshape(-1), jnp.sum(parts[8], axis=0)])
    shape = (batches, seq_count, length, width_dev)
    return (
        out.reshape(shape),
        d_x.reshape(shape),
        parts[0].reshape(-1),
        g_z,
        g_x,
        g_dt,
        g_bc,
        g_cw,
        g_cb,
        parts[4].reshape(-1),
        parts[5].reshape(-1),
        parts[6].reshape(-1),
        parts[3].reshape(-1),
        g_out,
    )


def solution(mesh):
    stream = P(None, "fsdp", "ctx", "tp")
    weight = P("fsdp", "tp")
    grad = P(("ctx", "fsdp"), "tp")
    in_specs = (
        (stream, stream, P(None, "fsdp", None), P())
        + (weight,) * 4
        + (P(),) * 6
        + (P("tp", "fsdp"),)
    )
    out_specs = (
        (stream, stream, P()) + (grad,) * 4 + (P(),) * 6 + (P("tp", ("ctx", "fsdp")),)
    )
    return jax.shard_map(
        on_device, mesh=mesh, in_specs=in_specs, out_specs=out_specs, check_vma=False
    )
```

```python
import functools

import jax
import jax.numpy as jnp
from jax import lax
from jax.experimental import pallas as pl
from jax.experimental.pallas import tpu as pltpu
from jax.sharding import PartitionSpec as P

EPSILON = 1e-05
PRECISE = lax.Precision.HIGHEST
LANES = 128
CHUNK = 128
FAR = -1e30
F32 = jnp.float32
BF16 = jnp.bfloat16


def mm(a, b, dims=((1,), (0,)), precision=None):
    return lax.dot_general(a, b, (dims, ((), ())), precision=precision, preferred_element_type=F32)


NN = ((1,), (0,))
NT = ((1,), (1,))
TN = ((0,), (0,))


def softplus(v):
    return jnp.maximum(v, 0.0) + jnp.log1p(jnp.exp(-jnp.abs(v)))


def silu_slope(v, sig):
    return sig * (1.0 + v * (1.0 - sig))


def doc_of(off_ref, seq, pos):
    count = jnp.zeros_like(pos)
    for j in range(off_ref.shape[1]):
        count = count + (off_ref[seq, j] <= pos).astype(jnp.int32)
    return count


def widen(cols, head, lane, width):
    out = cols[:, head : head + 1]
    for i in range(1, LANES // width):
        out = jnp.where(lane >= i * width, cols[:, head + i : head + i + 1], out)
    return jnp.broadcast_to(out, (cols.shape[0], LANES))


class Span:
    def __init__(self, off_ref, first, seq, start, q, dtr, dtb, rate, taps):
        at = first + start
        col = at + lax.broadcasted_iota(jnp.int32, (q, 1), 0)
        row = at + lax.broadcasted_iota(jnp.int32, (1, q), 1)
        dcol = doc_of(off_ref, seq, col)
        drow = doc_of(off_ref, seq, row)
        before = doc_of(off_ref, seq, at - 1)
        before_dev = doc_of(off_ref, seq, first - 1)
        last = doc_of(off_ref, seq, at + q - 1)
        self.match = [
            (doc_of(off_ref, seq, col - (taps - 1 - k)) == dcol).astype(F32) for k in range(taps - 1)
        ]
        self.far = jnp.where((dcol == drow) & (col >= row), 0.0, FAR)
        self.kept = (dcol == before).astype(F32)
        self.kept_dev = (dcol == before_dev).astype(F32)
        self.carry_dev = (before == before_dev).astype(F32)
        self.dt_in = dtr + dtb
        self.dt = softplus(self.dt_in)
        decay = self.dt * rate
        tri = (
            lax.broadcasted_iota(jnp.int32, (q, q), 0) >= lax.broadcasted_iota(jnp.int32, (q, q), 1)
        ).astype(F32)
        self.tri = tri
        self.cum = mm(tri, decay, precision=PRECISE)
        self.cum_t = self.cum.T
        self.lead = jnp.exp(self.cum) * self.kept
        end = self.cum[q - 1 : q, :]
        self.tail = jnp.exp(end - self.cum) * (dcol == last).astype(F32)
        self.end = end

    def fade(self, head):
        return jnp.exp(self.cum[:, head : head + 1] - self.cum_t[head : head + 1, :] + self.far)


def conv_block(pre, halo, cw, cb, match):
    taps = len(match) + 1
    ext = jnp.concatenate([halo, pre], axis=0)
    shifted = [
        pltpu.roll(ext, taps - 1 - k, 0)[8:] * match[k] for k in range(taps - 1)
    ] + [pre]
    conv = cb
    for k in range(taps):
        conv = conv + cw[k : k + 1] * shifted[k]
    return conv, shifted


def scan_kernel(dims, off, pos, *refs):
    scan_chunk(dims, pl.program_id(0), pl.program_id(1), off, pos[0], *refs)


def scan_chunk(dims, b, c, off, first, pre, rim, dtr, cw, cb, dtb, rate, dsk, y, rd, lead, st, lead0, fin, halo, state, run):
    q, inner, width, n = dims

    @pl.when(c == 0)
    def _():
        halo[...] = rim[0]
        state[...] = jnp.zeros_like(state)
        run[...] = jnp.zeros_like(run)

    taps = cw.shape[0]
    sp = Span(off, first, b, c * q, q, dtr[0], dtb[...], rate[...], taps)
    total = run[...] + sp.cum
    lead[0] = jnp.exp(total) * sp.kept_dev
    lead0[0, 0] = jnp.broadcast_to(jnp.exp(run[...]) * sp.carry_dev, (8, LANES))
    run[...] = total[q - 1 : q]

    def act(lo, hi):
        conv, _ = conv_block(
            pre[0, :, lo:hi].astype(F32), halo[:, lo:hi], cw[:, lo:hi], cb[:, lo:hi], sp.match
        )
        return conv * jax.nn.sigmoid(conv)

    write = act(inner, inner + n).astype(BF16)
    read = act(inner + n, inner + 2 * n).astype(BF16)
    rd[0] = read
    scores = mm(read, write, NT)
    write_t = write.astype(F32).T.astype(BF16)
    lane = lax.broadcasted_iota(jnp.int32, (1, LANES), 1)
    per = LANES // width
    for j in range(inner // LANES):
        lo, hi = j * LANES, (j + 1) * LANES
        h = j * per
        xs = act(lo, hi)
        xdt = xs * widen(sp.dt, h, lane, width)
        xdt_low = xdt.astype(BF16)
        mixed = None
        for i in range(per):
            part = mm((sp.fade(h + i) * scores).astype(BF16), xdt_low)
            mixed = part if mixed is None else jnp.where(lane >= i * width, part, mixed)
        old = state[:, lo:hi]
        st[0, 0, :, lo:hi] = old
        mixed = mixed + widen(sp.lead, h, lane, width) * mm(read, old.astype(BF16))
        y[0, :, lo:hi] = mixed + dsk[:, lo:hi] * xs
        fresh = mm(write_t, (xdt * widen(sp.tail, h, lane, width)).astype(BF16))
        new = widen(sp.lead[q - 1 : q], h, lane, width) * old + fresh
        state[:, lo:hi] = new
        fin[0, :, lo:hi] = new
    halo[...] = pre[0, q - 8 : q].astype(F32)


def gate_kernel(dims, y_in, rd, lead, lead0, st, s_in, z, gain, y, ygg, sq, st_full):
    q, inner, width, n = dims
    lane = lax.broadcasted_iota(jnp.int32, (1, LANES), 1)
    per = LANES // width
    total = jnp.zeros((q, LANES), F32)
    for j in range(inner // LANES):
        lo, hi = j * LANES, (j + 1) * LANES
        h = j * per
        came = s_in[0, :, lo:hi].astype(F32)
        st_full[0, 0, :, lo:hi] = st[0, 0, :, lo:hi] + widen(lead0[0, 0, 0:1], h, lane, width) * came
        val = y_in[0, :, lo:hi] + widen(lead[0], h, lane, width) * mm(rd[0], came.astype(BF16))
        y[0, :, lo:hi] = val
        gate = z[0, :, lo:hi]
        gated = val * gate * jax.nn.sigmoid(gate)
        total = total + gated * gated
        ygg[0, :, lo:hi] = (gated * gain[:, lo:hi]).astype(BF16)
    sq[0] = jnp.broadcast_to(jnp.sum(total, axis=1, keepdims=True), (q, LANES))


def ungate_kernel(dims, count, dyn, y, z, stat, gain, rd, lead, dy, dz, yn, g_gain, g_state):
    q, inner, width, n = dims
    b, c = pl.program_id(0), pl.program_id(1)

    @pl.when((b == 0) & (c == 0))
    def _():
        g_gain[...] = jnp.zeros_like(g_gain)

    @pl.when(c == 0)
    def _():
        g_state[...] = jnp.zeros_like(g_state)

    lane = lax.broadcasted_iota(jnp.int32, (1, LANES), 1)
    per = LANES // width
    r2 = stat[0, :, 0:1]
    coef = r2 * r2 * r2 * stat[0, :, 1:2] * (1.0 / count)
    read_t = rd[0].astype(F32).T.astype(BF16)
    for j in range(inner // LANES):
        lo, hi = j * LANES, (j + 1) * LANES
        h = j * per
        gate = z[0, :, lo:hi]
        sig = jax.nn.sigmoid(gate)
        act = gate * sig
        val = y[0, :, lo:hi]
        gated = val * act
        dn = dyn[0, :, lo:hi]
        g = gain[:, lo:hi]
        norm = gated * r2
        g_gain[0:1, lo:hi] += jnp.sum(dn * norm, axis=0, keepdims=True)
        yn[0, :, lo:hi] = (norm * g).astype(BF16)
        d_gated = r2 * (dn * g) - gated * coef
        d_core = d_gated * act
        dy[0, :, lo:hi] = d_core
        dz[0, :, lo:hi] = (d_gated * val * silu_slope(gate, sig)).astype(BF16)
        g_state[0, :, lo:hi] += mm(read_t, (d_core * widen(lead[0], h, lane, width)).astype(BF16))


def back_kernel(dims, off, pos, pre, prev, rim, dtr, y, dy, st, d_in, cw, cb, dtb, rate, dsk,
                dcat, ddt_out, edge, rim_grad, acc, acc_head, d_state, carry):
    q, inner, width, n = dims
    b, c = pl.program_id(0), pl.program_id(1)
    chunks = pl.num_programs(1)
    at = chunks - 1 - c

    @pl.when((b == 0) & (c == 0))
    def _():
        acc[...] = jnp.zeros_like(acc)
        acc_head[...] = jnp.zeros_like(acc_head)

    @pl.when(c == 0)
    def _():
        d_state[...] = d_in[0]
        carry[...] = jnp.zeros_like(carry)

    taps = cw.shape[0]
    sp = Span(off, pos[0], b, at * q, q, dtr[0], dtb[...], rate[...], taps)
    lane = lax.broadcasted_iota(jnp.int32, (1, LANES), 1)
    per = LANES // width

    def conv(lo, hi):
        ahead = jnp.where(at == 0, rim[0, :, lo:hi], prev[0, 8:16, lo:hi].astype(F32))
        return conv_block(pre[0, :, lo:hi].astype(F32), ahead, cw[:, lo:hi], cb[:, lo:hi], sp.match)

    def unconv(lo, hi, d_act, out, shifted, sig):
        d_conv = d_act * silu_slope(out, sig)
        acc[taps : taps + 1, lo:hi] += jnp.sum(d_conv, axis=0, keepdims=True)
        d_ext = None
        zeros = jnp.zeros((8, hi - lo), F32)
        for k in range(taps):
            acc[k : k + 1, lo:hi] += jnp.sum(d_conv * shifted[k], axis=0, keepdims=True)
            masked = cw[k : k + 1, lo:hi] * d_conv
            if k < taps - 1:
                masked = masked * sp.match[k]
            part = jnp.concatenate([zeros, masked], axis=0)
            if k < taps - 1:
                part = pltpu.roll(part, q + 8 - (taps - 1 - k), 0)
            d_ext = part if d_ext is None else d_ext + part
        d_pre = jnp.concatenate([d_ext[8:q], d_ext[q:] + carry[:, lo:hi]], axis=0)
        carry[:, lo:hi] = d_ext[0:8]
        rim_grad[0, :, lo:hi] = d_ext[0:8]
        dcat[0, :, lo:hi] = d_pre.astype(BF16)

        @pl.when(c == 0)
        def _():
            edge[0, :, lo:hi] = d_pre[q - 8 : q]

    w_conv, w_shift = conv(inner, inner + n)
    w_sig = jax.nn.sigmoid(w_conv)
    write = (w_conv * w_sig).astype(BF16)
    r_conv, r_shift = conv(inner + n, inner + 2 * n)
    r_sig = jax.nn.sigmoid(r_conv)
    read = (r_conv * r_sig).astype(BF16)
    scores = mm(read, write, NT)
    read_t = read.astype(F32).T.astype(BF16)
    d_scores = jnp.zeros((q, q), F32)
    d_write = jnp.zeros((q, n), F32)
    d_read = jnp.zeros((q, n), F32)
    d_cum = jnp.zeros((q, LANES), F32)
    d_step = jnp.zeros((q, LANES), F32)
    d_end = jnp.zeros((8, LANES), F32)
    for j in range(inner // LANES):
        lo, hi = j * LANES, (j + 1) * LANES
        h = j * per
        x_conv, x_shift = conv(lo, hi)
        x_sig = jax.nn.sigmoid(x_conv)
        xs = x_conv * x_sig
        step = widen(sp.dt, h, lane, width)
        xdt = xs * step
        xdt_low = xdt.astype(BF16)
        grad = dy[0, :, lo:hi]
        grad_low = grad.astype(BF16)
        core = y[0, :, lo:hi] - dsk[:, lo:hi] * xs
        late = d_state[:, lo:hi]
        late_low = late.astype(BF16)
        early = st[0, 0, :, lo:hi]
        tail = widen(sp.tail, h, lane, width)
        lead = widen(sp.lead, h, lane, width)
        u = None
        for i in range(per):
            fade = sp.fade(h + i)
            here = (lane >= i * width) & (lane < (i + 1) * width)
            own = jnp.where(here, grad, 0.0).astype(BF16)
            d_scores = d_scores + mm(own, xdt_low, NT) * fade
            part = mm((fade * scores).astype(BF16), grad_low, TN)
            u = part if u is None else jnp.where(lane >= i * width, part, u)
        from_end = tail * mm(write, late_low)
        inside = u
        u = u + from_end
        weighted = (lead * grad).astype(BF16)
        d_read = d_read + mm(weighted, early.astype(BF16), NT)
        d_write = d_write + mm((xdt * tail).astype(BF16), late_low, NT)
        end_lead = widen(sp.lead[q - 1 : q], h, lane, width)
        d_state[:, lo:hi] = end_lead * late + mm(read_t, weighted)
        head_of = (
            lax.broadcasted_iota(jnp.int32, (LANES, LANES), 0) // width + h
            == lax.broadcasted_iota(jnp.int32, (LANES, LANES), 1)
        ).astype(F32)
        d_cum = d_cum + mm(
            grad_low.astype(F32) * core - xdt_low.astype(F32) * inside - xdt * from_end,
            head_of,
            precision=PRECISE,
        )
        d_step = d_step + mm(xs * u, head_of, precision=PRECISE)
        end_row = end_lead * jnp.sum(late * early, axis=0, keepdims=True) + jnp.sum(
            xdt * from_end, axis=0, keepdims=True
        )
        d_end = d_end + mm(jnp.broadcast_to(end_row, (8, LANES)), head_of, precision=PRECISE)
        acc[taps + 1 : taps + 2, lo:hi] += jnp.sum(grad * xs, axis=0, keepdims=True)
        unconv(lo, hi, step * u + dsk[:, lo:hi] * grad, x_conv, x_shift, x_sig)
    d_low = d_scores.astype(BF16)
    d_read = d_read + mm(d_low, write)
    d_write = d_write + mm(d_low, read, TN)
    unconv(inner, inner + n, d_write, w_conv, w_shift, w_sig)
    unconv(inner + n, inner + 2 * n, d_read, r_conv, r_shift, r_sig)
    d_decay = mm(sp.tri, d_cum, TN, precision=PRECISE) + d_end[0:1]
    acc_head[0:1] += jnp.sum(d_decay * sp.dt, axis=0, keepdims=True) * rate[...]
    d_dt = (d_step + d_decay * rate[...]) * jax.nn.sigmoid(sp.dt_in)
    acc_head[1:2] += jnp.sum(d_dt, axis=0, keepdims=True)
    ddt_out[0] = d_dt.astype(BF16)


def whole(shape):
    return pl.BlockSpec(shape, lambda *_: (0,) * len(shape))


def params():
    return pltpu.CompilerParams(vmem_limit_bytes=48 << 20)


def scan_forward(offs, pos, pre, rim, dtr, cw, cb, dtb, rate, dsk, width, n):
    nb, length, chans = pre.shape
    inner = dsk.shape[1]
    q = min(CHUNK, length)
    chunks = length // q
    dims = (q, inner, width, n)

    def rows(size):
        return pl.BlockSpec((1, q, size), lambda b, c, *_: (b, c, 0))

    return pl.pallas_call(
        functools.partial(scan_kernel, dims),
        grid_spec=pltpu.PrefetchScalarGridSpec(
            num_scalar_prefetch=2,
            grid=(nb, chunks),
            in_specs=[
                rows(chans),
                pl.BlockSpec((1, 8, chans), lambda b, c, *_: (b, 0, 0)),
                rows(LANES),
                whole(cw.shape),
                whole(cb.shape),
                whole(dtb.shape),
                whole(rate.shape),
                whole(dsk.shape),
            ],
            out_specs=[
                rows(inner),
                rows(n),
                rows(LANES),
                pl.BlockSpec((1, 1, n, inner), lambda b, c, *_: (b, c, 0, 0)),
                pl.BlockSpec((1, 1, 8, LANES), lambda b, c, *_: (b, c, 0, 0)),
                pl.BlockSpec((1, n, inner), lambda b, c, *_: (b, 0, 0)),
            ],
            scratch_shapes=[
                pltpu.VMEM((8, chans), F32),
                pltpu.VMEM((n, inner), F32),
                pltpu.VMEM((1, LANES), F32),
            ],
        ),
        out_shape=[
            jax.ShapeDtypeStruct((nb, length, inner), F32),
            jax.ShapeDtypeStruct((nb, length, n), BF16),
            jax.ShapeDtypeStruct((nb, length, LANES), F32),
            jax.ShapeDtypeStruct((nb, chunks, n, inner), F32),
            jax.ShapeDtypeStruct((nb, chunks, 8, LANES), F32),
            jax.ShapeDtypeStruct((nb, n, inner), F32),
        ],
        compiler_params=params(),
        name="scan_forward",
    )(offs, pos, pre, rim, dtr, cw, cb, dtb, rate, dsk)


def gate_forward(y_in, rd, lead, lead0, st, s_in, z, gain, width):
    nb, length, inner = y_in.shape
    chunks, n = st.shape[1], st.shape[2]
    q = length // chunks
    dims = (q, inner, width, n)

    def rows(size):
        return pl.BlockSpec((1, q, size), lambda b, c: (b, c, 0))

    def per_chunk(r, size):
        return pl.BlockSpec((1, 1, r, size), lambda b, c: (b, c, 0, 0))

    return pl.pallas_call(
        functools.partial(gate_kernel, dims),
        grid=(nb, chunks),
        in_specs=[
            rows(inner),
            rows(n),
            rows(LANES),
            per_chunk(8, LANES),
            per_chunk(n, inner),
            pl.BlockSpec((1, n, inner), lambda b, c: (b, 0, 0)),
            rows(inner),
            whole(gain.shape),
        ],
        out_specs=[rows(inner), rows(inner), rows(LANES), per_chunk(n, inner)],
        out_shape=[
            jax.ShapeDtypeStruct((nb, length, inner), F32),
            jax.ShapeDtypeStruct((nb, length, inner), BF16),
            jax.ShapeDtypeStruct((nb, length, LANES), F32),
            jax.ShapeDtypeStruct(st.shape, F32),
        ],
        compiler_params=params(),
        name="gate_forward",
    )(y_in, rd, lead, lead0, st, s_in, z, gain)


def gate_backward(dyn, y, z, stat, gain, rd, lead, width, count):
    nb, length, inner = y.shape
    n = rd.shape[2]
    q = min(CHUNK, length)
    chunks = length // q
    dims = (q, inner, width, n)

    def rows(size):
        return pl.BlockSpec((1, q, size), lambda b, c: (b, c, 0))

    return pl.pallas_call(
        functools.partial(ungate_kernel, dims, count),
        grid=(nb, chunks),
        in_specs=[
            rows(inner),
            rows(inner),
            rows(inner),
            rows(LANES),
            whole(gain.shape),
            rows(n),
            rows(LANES),
        ],
        out_specs=[
            rows(inner),
            rows(inner),
            rows(inner),
            whole((8, inner)),
            pl.BlockSpec((1, n, inner), lambda b, c: (b, 0, 0)),
        ],
        out_shape=[
            jax.ShapeDtypeStruct((nb, length, inner), F32),
            jax.ShapeDtypeStruct((nb, length, inner), BF16),
            jax.ShapeDtypeStruct((nb, length, inner), BF16),
            jax.ShapeDtypeStruct((8, inner), F32),
            jax.ShapeDtypeStruct((nb, n, inner), F32),
        ],
        compiler_params=params(),
        name="gate_backward",
    )(dyn, y, z, stat, gain, rd, lead)


def scan_backward(offs, pos, pre, rim, dtr, y, dy, st, d_in, cw, cb, dtb, rate, dsk, width):
    nb, length, chans = pre.shape
    inner = dsk.shape[1]
    chunks, n = st.shape[1], st.shape[2]
    q = length // chunks
    dims = (q, inner, width, n)
    per = q // 16

    def rows(size):
        return pl.BlockSpec((1, q, size), lambda b, c, *_: (b, chunks - 1 - c, 0))

    def per_seq(r, size):
        return pl.BlockSpec((1, r, size), lambda b, c, *_: (b, 0, 0))

    return pl.pallas_call(
        functools.partial(back_kernel, dims),
        grid_spec=pltpu.PrefetchScalarGridSpec(
            num_scalar_prefetch=2,
            grid=(nb, chunks),
            in_specs=[
                rows(chans),
                pl.BlockSpec(
                    (1, 16, chans), lambda b, c, *_: (b, jnp.maximum((chunks - 1 - c) * per - 1, 0), 0)
                ),
                per_seq(8, chans),
                rows(LANES),
                rows(inner),
                rows(inner),
                pl.BlockSpec((1, 1, n, inner), lambda b, c, *_: (b, chunks - 1 - c, 0, 0)),
                per_seq(n, inner),
                whole(cw.shape),
                whole(cb.shape),
                whole(dtb.shape),
                whole(rate.shape),
                whole(dsk.shape),
            ],
            out_specs=[
                rows(chans),
                rows(LANES),
                per_seq(8, chans),
                per_seq(8, chans),
                whole((8, chans)),
                whole((8, LANES)),
            ],
            scratch_shapes=[pltpu.VMEM((n, inner), F32), pltpu.VMEM((8, chans), F32)],
        ),
        out_shape=[
            jax.ShapeDtypeStruct((nb, length, chans), BF16),
            jax.ShapeDtypeStruct((nb, length, LANES), BF16),
            jax.ShapeDtypeStruct((nb, 8, chans), F32),
            jax.ShapeDtypeStruct((nb, 8, chans), F32),
            jax.ShapeDtypeStruct((8, chans), F32),
            jax.ShapeDtypeStruct((8, LANES), F32),
        ],
        compiler_params=params(),
        name="scan_backward",
    )(offs, pos, pre, pre, rim, dtr, y, dy, st, d_in, cw, cb, dtb, rate, dsk)


MESH = pl.DeviceIdType.MESH


def remote(src, dst, send, recv, **where):
    return pltpu.make_async_remote_copy(
        src_ref=src, dst_ref=dst, send_sem=send, recv_sem=recv, device_id=where, device_id_type=MESH
    )


class Line:
    def __init__(self, own, full, rows, wide, send, recv):
        self.own, self.full, self.rows, self.wide = own, full, rows, wide
        self.send, self.recv = send, recv
        self.me = lax.axis_index("tp")
        self.peers = lax.axis_size("tp")

    def block(self, slot):
        return self.full.at[self.rows, pl.ds(pl.multiple_of(slot * self.wide, self.wide), self.wide)]

    def parts(self, k):
        for way, step in enumerate((1, -1)):
            slot = self.me - k * step
            there = self.me + step
            held = (slot >= 0) & (slot < self.peers)
            onward = held & (there >= 0) & (there < self.peers)
            slot = jnp.clip(slot, 0, self.peers - 1)
            here = self.own.at[self.rows] if k == 0 else self.block(slot)
            copy = remote(here, self.block(slot), self.send.at[way, k], self.recv.at[slot], tp=there)
            yield held, onward, copy

    def step(self, k):
        for held, onward, copy in self.parts(k):
            if k > 0:

                @pl.when(held)
                def _():
                    copy.wait_recv()

            @pl.when(onward)
            def _():
                copy.start()

    def finish(self):
        for k in range(self.peers - 1):
            for held, onward, copy in self.parts(k):

                @pl.when(onward)
                def _():
                    copy.wait_send()


def front_kernel(
    dims, off, x, cot, wx_in, wz_in, wo_in, wbc, wdt, gain_in, cw, cb, dtb, rate, dsk, gain,
    xn_o, r1_o, pre_o, dtr_o, z_o, y_o, rd_o, lead_o, st_o, fin_o, sq_o, part_o, rim_o, wx_o, wz_o, wo_o, cot_o,
    x_all, xn, r1, pre, dtr, z, y, rd, lead, st, lead0, fin, sq, ygg, part, rim, rim16, came, left,
    wx, wz, wo, halo, state, run,
    xs_send, xs_recv, cs_send, cs_recv, w_send, w_recv, r_send, r_recv, s_send, s_recv, loc, outs,
):
    nb, length, q, inner, width, n, d = dims
    tokens = nb * length
    pair = 2 * n
    ctx, tp, fs = lax.axis_index("ctx"), lax.axis_index("tp"), lax.axis_index("fsdp")
    tps = lax.axis_size("tp")
    wide = d // tps
    deep = wx_in.shape[0]
    mate = fs + 1 - 2 * lax.rem(fs, 2)
    over = lax.rem(fs + 2, 4)
    other = 1 - ctx
    first = ctx * length

    barrier = pltpu.get_barrier_semaphore()
    pl.semaphore_signal(barrier, inc=1, device_id={"fsdp": mate}, device_id_type=MESH)
    pl.semaphore_signal(barrier, inc=1, device_id={"fsdp": over}, device_id_type=MESH)
    pl.semaphore_signal(barrier, inc=1, device_id={"ctx": other}, device_id_type=MESH)
    for there in (tp - 1, tp + 1):

        @pl.when((there >= 0) & (there < tps))
        def _():
            pl.semaphore_signal(barrier, inc=1, device_id={"tp": there}, device_id_type=MESH)

    sides = (tp > 0).astype(jnp.int32) + (tp < tps - 1).astype(jnp.int32)
    pl.semaphore_wait(barrier, 3 + sides)

    def seq(m):
        return pl.ds(m * length, length)

    x_lines = [Line(x, x_all, seq(m), wide, xs_send.at[m], xs_recv.at[m]) for m in range(nb)]
    c_lines = [Line(cot, cot_o, seq(m), wide, cs_send.at[m], cs_recv.at[m]) for m in range(nb)]
    mine = pl.ds(pl.multiple_of(tp * wide, wide), wide)

    def slot(w, at):
        span = pl.ds(pl.multiple_of(at * deep, deep), deep)
        return (wx.at[span], wz.at[span], wo.at[:, span])[w]

    owns = (wx_in, wz_in, wo_in)

    def near(w):
        return remote(owns[w], slot(w, fs), w_send.at[w, 0], w_recv.at[w, fs], fsdp=mate)

    def far(w):
        return remote(owns[w], slot(w, fs), w_send.at[w, 1], w_recv.at[w, fs], fsdp=over)

    def relay(w):
        return remote(slot(w, over), slot(w, over), w_send.at[w, 2], w_recv.at[w, over], fsdp=mate)

    def arrive(w, at):
        remote(slot(w, at), slot(w, at), w_send.at[w, 0], w_recv.at[w, at], fsdp=mate).wait_recv()

    locals_ = [pltpu.make_async_copy(owns[w], slot(w, fs), loc.at[w]) for w in range(3)]
    locals_.append(pltpu.make_async_copy(x, x_all.at[:, mine], loc.at[3]))
    locals_.append(pltpu.make_async_copy(cot, cot_o.at[:, mine], loc.at[4]))

    x_lines[0].step(0)
    far(0).start()
    near(0).start()
    for copy in locals_:
        copy.start()
    far(1).start()
    near(1).start()
    far(2).start()
    near(2).start()
    for k in range(1, tps):
        x_lines[0].step(k)
    x_lines[1].step(0)

    def pass_on(w):
        arrive(w, over)
        relay(w).start()

    def whole_weight(w):
        arrive(w, mate)
        arrive(w, lax.rem(mate + 2, 4))
        locals_[w].wait()

    out_copies = []

    def keep(i, src, dst):
        copy = pltpu.make_async_copy(src, dst, outs.at[i])
        copy.start()
        out_copies.append(copy)

    def norm(m):
        @pl.loop(0, length // q)
        def _(i):
            rows = pl.ds(pl.multiple_of(m * length + i * q, q), q)
            total = jnp.zeros((q, LANES), F32)
            for j in range(d // LANES):
                v = x_all[rows, j * LANES : (j + 1) * LANES].astype(F32)
                total = total + v * v
            inv = lax.rsqrt(jnp.sum(total, axis=1, keepdims=True) * (1.0 / d) + EPSILON)
            r1[rows, :] = jnp.broadcast_to(inv, (q, LANES))
            for j in range(d // LANES):
                cols = slice(j * LANES, (j + 1) * LANES)
                xn[rows, cols] = (x_all[rows, cols].astype(F32) * inv * gain_in[:, cols]).astype(BF16)

    def project_x(m):
        tile = min(2 * LANES, inner)
        for half in (1, 0):
            size = length // 2
            rows = pl.ds(m * length + half * size, size)
            here = pl.ds(half * size, size)
            dtr[m, here, :] = mm(xn[rows, :], wdt[...])
            pre[m, here, inner:] = mm(xn[rows, :], wbc[...]).astype(BF16)

            @pl.loop(0, inner // tile)
            def _(j):
                cols = pl.ds(pl.multiple_of(j * tile, tile), tile)
                pre[m, here, cols] = mm(xn[rows, :], wx[:, cols]).astype(BF16)

            if half == 1:

                @pl.when(ctx == 0)
                def _():
                    rim_copy(m).start()

    def rim_copy(m):
        return remote(pre.at[m, pl.ds(length - 16, 16)], rim16.at[m], r_send.at[m], r_recv.at[m], ctx=other)

    def project_z(m):
        tile = min(2 * LANES, inner)
        rows = seq(m)

        @pl.loop(0, inner // tile)
        def _(j):
            cols = pl.ds(pl.multiple_of(j * tile, tile), tile)
            z[m, :, cols] = mm(xn[rows, :], wz[:, cols])

    def one(ref, m):
        return ref.at[pl.ds(m, 1)]

    def span(ref, m, rows):
        return ref.at[pl.ds(m, 1), rows]

    def get_rim(m):
        @pl.when(ctx == 1)
        def _():
            rim_copy(m).wait_recv()
            rim[m] = rim16[m, 8:16].astype(F32)

        @pl.when(ctx == 0)
        def _():
            rim[m] = jnp.zeros_like(rim[m])

    def scan(m, lo, hi):
        @pl.loop(lo, hi)
        def _(c):
            rows = pl.ds(pl.multiple_of(c * q, q), q)
            scan_chunk(
                (q, inner, width, n), m, c, off, first,
                span(pre, m, rows), one(rim, m), span(dtr, m, rows), cw, cb, dtb, rate, dsk,
                span(y, m, rows), span(rd, m, rows), span(lead, m, rows),
                st.at[pl.ds(m, 1), pl.ds(c, 1)], lead0.at[pl.ds(m, 1), pl.ds(c, 1)], one(fin, m),
                halo, state, run,
            )

    def state_copy(m):
        return remote(left.at[m], came.at[m], s_send.at[m], s_recv.at[m], ctx=other)

    def send_state(m):
        @pl.when(ctx == 0)
        def _():
            left[m] = fin[m].astype(BF16)
            state_copy(m).start()

    def get_state(m):
        @pl.when(ctx == 1)
        def _():
            state_copy(m).wait_recv()

        @pl.when(ctx == 0)
        def _():
            came[m] = jnp.zeros_like(came[m])

    def gate(m):
        @pl.loop(0, length // q)
        def _(c):
            rows = pl.ds(pl.multiple_of(c * q, q), q)
            sts = st.at[pl.ds(m, 1), pl.ds(c, 1)]
            ys = span(y, m, rows)
            gate_kernel(
                (q, inner, width, n), ys, span(rd, m, rows), span(lead, m, rows),
                lead0.at[pl.ds(m, 1), pl.ds(c, 1)], sts, one(came, m), span(z, m, rows), gain,
                ys, span(ygg, m, rows), span(sq, m, rows), sts,
            )

    def project_out(m):
        tile = 2 * LANES

        @pl.loop(0, d // tile)
        def _(j):
            cols = pl.ds(pl.multiple_of(j * tile, tile), tile)
            part[seq(m), cols] = mm(ygg[m], wo[:, cols]).astype(BF16)

    locals_[3].wait()
    pass_on(0)
    norm(0)
    whole_weight(0)
    keep(0, wx, wx_o)
    project_x(0)
    x_lines[1].step(1)
    pass_on(1)
    get_rim(0)
    scan(0, 0, length // q)
    send_state(0)
    x_lines[1].step(2)
    whole_weight(1)
    keep(1, wz, wz_o)
    project_z(0)
    for k in range(3, tps):
        x_lines[1].step(k)
    pass_on(2)
    c_lines[0].step(0)
    norm(1)
    project_x(1)
    keep(2, xn, xn_o)
    keep(3, r1, r1_o)
    keep(4, pre, pre_o)
    keep(5, dtr, dtr_o)
    c_lines[0].step(1)
    get_rim(1)
    keep(6, rim, rim_o)
    scan(1, 0, length // q)
    send_state(1)
    keep(7, rd, rd_o)
    keep(8, lead, lead_o)
    keep(9, fin, fin_o)
    c_lines[0].step(2)
    project_z(1)
    keep(10, z, z_o)
    get_state(0)
    gate(0)
    for k in range(3, tps):
        c_lines[0].step(k)
    c_lines[1].step(0)
    whole_weight(2)
    keep(11, wo, wo_o)
    project_out(0)
    get_state(1)
    c_lines[1].step(1)
    gate(1)
    keep(12, y, y_o)
    keep(13, st, st_o)
    keep(14, sq, sq_o)
    project_out(1)
    keep(15, part, part_o)
    for k in range(2, tps):
        c_lines[1].step(k)
    for line in x_lines + c_lines:
        line.finish()
    for w in range(3):
        near(w).wait_send()
        far(w).wait_send()
        relay(w).wait_send()
    locals_[4].wait()

    @pl.when(ctx == 0)
    def _():
        for m in range(nb):
            rim_copy(m).wait_send()
            state_copy(m).wait_send()

    for copy in out_copies:
        copy.wait()


def front(offs, x, cot, wx, wz, wo, wbc, wdt, gain_in, cw, cb, dtb, rate, dsk, gain, nb, length, width, n, tps):
    tokens, wide = x.shape
    d = wide * tps
    inner = wx.shape[1]
    chans = cw.shape[1]
    q = min(CHUNK, length)
    chunks = length // q
    dims = (nb, length, q, inner, width, n, d)
    sds = jax.ShapeDtypeStruct
    kept = [
        sds((tokens, d), BF16),
        sds((tokens, LANES), F32),
        sds((nb, length, chans), BF16),
        sds((nb, length, LANES), F32),
        sds((nb, length, inner), F32),
        sds((nb, length, inner), F32),
        sds((nb, length, n), BF16),
        sds((nb, length, LANES), F32),
        sds((nb, chunks, n, inner), F32),
        sds((nb, n, inner), F32),
        sds((nb, length, LANES), F32),
        sds((tokens, d), BF16),
        sds((nb, 8, chans), F32),
        sds((d, inner), BF16),
        sds((d, inner), BF16),
        sds((inner, d), BF16),
        sds((tokens, d), BF16),
    ]

    def vm(k):
        return pltpu.VMEM(kept[k].shape, kept[k].dtype)

    scratch = [
        pltpu.VMEM((tokens, d), BF16),
        vm(0), vm(1), vm(2), vm(3), vm(4), vm(5), vm(6), vm(7), vm(8),
        pltpu.VMEM((nb, chunks, 8, LANES), F32),
        vm(9), vm(10),
        pltpu.VMEM((nb, length, inner), BF16),
        vm(11), vm(12),
        pltpu.VMEM((nb, 16, chans), BF16),
        pltpu.VMEM((nb, n, inner), BF16),
        pltpu.VMEM((nb, n, inner), BF16),
        vm(13), vm(14), vm(15),
        pltpu.VMEM((8, chans), F32),
        pltpu.VMEM((n, inner), F32),
        pltpu.VMEM((1, LANES), F32),
        pltpu.SemaphoreType.DMA((nb, 2, tps)),
        pltpu.SemaphoreType.DMA((nb, tps)),
        pltpu.SemaphoreType.DMA((nb, 2, tps)),
        pltpu.SemaphoreType.DMA((nb, tps)),
        pltpu.SemaphoreType.DMA((3, 3)),
        pltpu.SemaphoreType.DMA((3, 4)),
        pltpu.SemaphoreType.DMA((nb,)),
        pltpu.SemaphoreType.DMA((nb,)),
        pltpu.SemaphoreType.DMA((nb,)),
        pltpu.SemaphoreType.DMA((nb,)),
        pltpu.SemaphoreType.DMA((5,)),
        pltpu.SemaphoreType.DMA((16,)),
    ]
    hbm = pl.BlockSpec(memory_space=pl.ANY)
    vmem = pl.BlockSpec(memory_space=pltpu.VMEM)
    return pl.pallas_call(
        functools.partial(front_kernel, dims),
        in_specs=[pl.BlockSpec(memory_space=pltpu.SMEM)] + [hbm] * 5 + [vmem] * 9,
        out_specs=[hbm] * len(kept),
        out_shape=kept,
        scratch_shapes=scratch,
        compiler_params=pltpu.CompilerParams(
            collective_id=0, has_side_effects=True, vmem_limit_bytes=60 << 20
        ),
        name="front",
    )(offs, x, cot, wx, wz, wo, wbc, wdt, gain_in, cw, cb, dtb, rate, dsk, gain)


def shift(arr, axis, by):
    peers = lax.axis_size(axis)
    pairs = [(i, i + by) for i in range(peers) if 0 <= i + by < peers]
    return lax.ppermute(arr, axis, pairs)


def heads_row(vec, width=LANES):
    return jnp.pad(vec[None], ((0, 0), (0, width - vec.shape[0])))


def on_device(
    x_in,
    cotangent,
    offsets,
    in_gain,
    w_z,
    w_x,
    w_dt,
    w_bc,
    conv_w,
    conv_b,
    dt_bias,
    a_log,
    d_skip,
    norm_gain,
    w_out,
):
    batches, seq_count, length, width_dev = x_in.shape
    nb = batches * seq_count
    tokens = nb * length
    tp_rank = lax.axis_index("tp")
    ctx_rank = lax.axis_index("ctx")
    peers = lax.axis_size("ctx")
    inner = w_z.shape[1]
    heads = w_dt.shape[1]
    width = inner // heads
    model = in_gain.shape[0]
    inner_all = norm_gain.shape[0]
    pair = conv_w.shape[1] - inner_all
    n = pair // 2
    taps = conv_w.shape[0]

    def mine(arr, size, axis):
        return lax.dynamic_slice_in_dim(arr, tp_rank * size, size, axis)

    cw = jnp.concatenate([mine(conv_w, inner, 1), conv_w[:, inner_all:]], axis=1)
    cb = jnp.concatenate([mine(conv_b, inner, 0), conv_b[inner_all:]])[None]
    gain = mine(norm_gain, inner, 0)[None]
    gain_in = mine(in_gain, width_dev, 0)
    dtb = heads_row(mine(dt_bias, heads, 0))
    rate = heads_row(-jnp.exp(mine(a_log, heads, 0)))
    dsk = jnp.repeat(mine(d_skip, heads, 0), width)[None]
    pos = (ctx_rank * length).astype(jnp.int32)[None]
    offs = offsets.reshape(nb, offsets.shape[-1])

    x_own = x_in.reshape(tokens, width_dev)
    cot_own = cotangent.reshape(tokens, width_dev)
    tps = lax.axis_size("tp")
    small = jnp.concatenate([w_bc, w_dt], axis=1)
    small = lax.all_gather(small, "fsdp", axis=0, tiled=True)
    wdt = jnp.pad(small[:, pair // tps :], ((0, 0), (0, LANES - heads)))
    wbc = lax.all_gather(small[:, : pair // tps], "tp", axis=1, tiled=True)

    def chained(start, lend, by):
        came = jnp.zeros_like(start)
        for k in range(peers - 1):
            sent = start if k == 0 else start + lend * came
            came = shift(sent.astype(BF16), "ctx", by).astype(F32)
        return came

    def ending(lead):
        return jnp.repeat(lead[:, length - 1, :heads], width, axis=-1)[:, None]

    if peers == 2 and lax.axis_size("fsdp") == 4:
        xn, r1, pre, dtr, z, y, rd, lead, st, _, sq, part, rim, wx, wz, wo, cot_all = front(
            offs, x_own, cot_own, w_x, w_z, w_out, wbc, wdt, in_gain[None], cw, cb, dtb, rate, dsk, gain,
            nb, length, width, n, tps,
        )
        r1 = r1[:, :1]
    else:
        x_all = lax.all_gather(x_own, "tp", axis=1, tiled=True)
        wx = lax.all_gather(w_x, "fsdp", axis=0, tiled=True)
        wz = lax.all_gather(w_z, "fsdp", axis=0, tiled=True)
        wo = lax.all_gather(w_out, "fsdp", axis=1, tiled=True)
        cot_all = lax.all_gather(cot_own, "tp", axis=1, tiled=True)
        resid = x_all.astype(F32)
        r1 = lax.rsqrt(jnp.mean(resid * resid, axis=1, keepdims=True) + EPSILON)
        xn = (resid * r1 * in_gain).astype(BF16)
        pre = jnp.concatenate([mm(xn, wx).astype(BF16), mm(xn, wbc).astype(BF16)], axis=1)
        pre = pre.reshape(nb, length, inner + pair)
        dtr = mm(xn, wdt).reshape(nb, length, LANES)
        z = mm(xn, wz).reshape(nb, length, inner)
        rim = shift(pre[:, length - 8 :], "ctx", 1).astype(F32)
        y, rd, lead, st, lead0, fin = scan_forward(
            offs, pos, pre, rim, dtr, cw, cb, dtb, rate, dsk, width, n
        )
        s_in = chained(fin, ending(lead), 1)
        y, ygg, sq, st = gate_forward(y, rd, lead, lead0, st, s_in, z, gain, width)
        part = mm(ygg.reshape(tokens, inner), wo).astype(BF16)
    lend = ending(lead)
    share = lax.psum_scatter(part, "tp", scatter_dimension=1, tiled=True)
    dyn = mm(cot_all, wo, NT).reshape(nb, length, inner)
    dot = jnp.sum(dyn * gain * y * jax.nn.silu(z), axis=2)
    stat = jnp.stack([sq[..., 0], dot])
    stat = jnp.sum(lax.all_gather(stat, "tp"), axis=0)
    r2 = lax.rsqrt(stat[0] / inner_all + EPSILON)
    out = x_own.astype(F32) + r2.reshape(tokens, 1) * share.astype(F32)
    stat = jnp.pad(jnp.stack([r2, stat[1]], axis=-1), ((0, 0), (0, 0), (0, LANES - 2)))
    dy, dz, yn, g_gain, g_state = gate_backward(dyn, y, z, stat, gain, rd, lead, width, inner_all)
    dz = dz.reshape(tokens, inner)
    yn = yn.reshape(tokens, inner)
    d_in = chained(g_state, lend, -1)
    rows = ("ctx", "fsdp")

    def scattered(grad):
        return lax.psum_scatter(grad.astype(BF16), rows, scatter_dimension=0, tiled=True)

    g_out = scattered(mm(cot_all, yn, TN)).astype(F32).T
    g_z = scattered(mm(xn, dz, TN)).astype(F32)
    dcat, ddt, edge, rim_grad, acc, acc_head = scan_backward(
        offs, pos, pre, rim, dtr, y, dy, st, d_in, cw, cb, dtb, rate, dsk, width
    )
    edge = (edge + shift(rim_grad, "ctx", -1)).astype(BF16)
    dcat = lax.dynamic_update_slice(dcat, edge, (0, length - 8, 0)).reshape(tokens, inner + pair)
    ddt = ddt.reshape(tokens, LANES)
    dxn = mm(dz, wz, NT) + mm(dcat[:, :inner], wx, NT) + mm(dcat[:, inner:], wbc, NT) + mm(ddt, wdt, NT)
    dxn = lax.psum_scatter(dxn.astype(BF16), "tp", scatter_dimension=1, tiled=True).astype(F32)
    g_xbc = scattered(jnp.concatenate([mm(xn, dcat, TN), mm(xn, ddt, TN)[:, :heads]], axis=1))
    g_x = g_xbc[:, :inner].astype(F32)
    g_dt = g_xbc[:, inner + pair :].astype(F32)
    g_bc = lax.psum_scatter(
        g_xbc[:, inner : inner + pair].astype(F32), "tp", scatter_dimension=1, tiled=True
    )
    h_own = x_own.astype(F32)
    scaled = dxn * gain_in
    in_dot = jnp.sum(lax.all_gather(jnp.sum(scaled * h_own, axis=1), "tp"), axis=0)[:, None]
    g_in = jnp.sum(dxn * h_own * r1, axis=0)
    d_x = cot_own.astype(F32) + r1 * scaled - h_own * r1**3 * in_dot / model
    pieces = [
        g_in,
        acc[:taps, :inner].reshape(-1),
        acc[taps, :inner],
        g_gain[0],
        acc_head[1, :heads],
        acc_head[0, :heads],
        acc[taps + 1, :inner].reshape(heads, width).sum(axis=1),
        acc[:taps, inner:].reshape(-1),
        acc[taps, inner:],
    ]
    sizes = [p.shape[0] for p in pieces]
    packed = jnp.sum(lax.all_gather(jnp.concatenate(pieces), rows), axis=0)
    packed = lax.all_gather(packed, "tp")
    parts, start = [], 0
    for size in sizes:
        parts.append(packed[:, start : start + size])
        start += size
    tp = packed.shape[0]
    g_cw = jnp.concatenate(
        [
            parts[1].reshape(tp, taps, inner).transpose(1, 0, 2).reshape(taps, inner_all),
            jnp.sum(parts[7], axis=0).reshape(taps, pair),
        ],
        axis=1,
    )
    g_cb = jnp.concatenate([parts[2].reshape(-1), jnp.sum(parts[8], axis=0)])
    shape = (batches, seq_count, length, width_dev)
    return (
        out.reshape(shape),
        d_x.reshape(shape),
        parts[0].reshape(-1),
        g_z,
        g_x,
        g_dt,
        g_bc,
        g_cw,
        g_cb,
        parts[4].reshape(-1),
        parts[5].reshape(-1),
        parts[6].reshape(-1),
        parts[3].reshape(-1),
        g_out,
    )


def solution(mesh):
    stream = P(None, "fsdp", "ctx", "tp")
    weight = P("fsdp", "tp")
    grad = P(("ctx", "fsdp"), "tp")
    in_specs = (
        (stream, stream, P(None, "fsdp", None), P())
        + (weight,) * 4
        + (P(),) * 6
        + (P("tp", "fsdp"),)
    )
    out_specs = (
        (stream, stream, P()) + (grad,) * 4 + (P(),) * 6 + (P("tp", ("ctx", "fsdp")),)
    )
    return jax.shard_map(
        on_device, mesh=mesh, in_specs=in_specs, out_specs=out_specs, check_vma=False
    )
```

```python
import functools
import types

import jax
import jax.numpy as jnp
from jax import lax
from jax.experimental import pallas as pl
from jax.experimental.pallas import tpu as pltpu
from jax.sharding import PartitionSpec as P

EPSILON = 1e-05
PRECISE = lax.Precision.HIGHEST
LANES = 128
CHUNK = 128
FAR = -1e30
F32 = jnp.float32
BF16 = jnp.bfloat16


def mm(a, b, dims=((1,), (0,)), precision=None):
    return lax.dot_general(a, b, (dims, ((), ())), precision=precision, preferred_element_type=F32)


NN = ((1,), (0,))
NT = ((1,), (1,))
TN = ((0,), (0,))


def softplus(v):
    return jnp.maximum(v, 0.0) + jnp.log1p(jnp.exp(-jnp.abs(v)))


def head_sums(v, head_of):
    high = v.astype(BF16)
    low = (v - high.astype(F32)).astype(BF16)
    return mm(high, head_of) + mm(low, head_of)


def silu_slope(v, sig):
    return sig * (1.0 + v * (1.0 - sig))


def doc_of(off_ref, seq, pos):
    count = jnp.zeros_like(pos)
    for j in range(off_ref.shape[1]):
        count = count + (off_ref[seq, j] <= pos).astype(jnp.int32)
    return count


def widen(cols, head, lane, width):
    out = cols[:, head : head + 1]
    for i in range(1, LANES // width):
        out = jnp.where(lane >= i * width, cols[:, head + i : head + i + 1], out)
    return jnp.broadcast_to(out, (cols.shape[0], LANES))


class Span:
    def __init__(self, off_ref, first, seq, start, q, dtr, dtb, rate, taps):
        at = first + start
        col = at + lax.broadcasted_iota(jnp.int32, (q, 1), 0)
        row = at + lax.broadcasted_iota(jnp.int32, (1, q), 1)
        dcol = doc_of(off_ref, seq, col)
        drow = doc_of(off_ref, seq, row)
        before = doc_of(off_ref, seq, at - 1)
        before_dev = doc_of(off_ref, seq, first - 1)
        last = doc_of(off_ref, seq, at + q - 1)
        self.match = [
            (doc_of(off_ref, seq, col - (taps - 1 - k)) == dcol).astype(F32) for k in range(taps - 1)
        ]
        self.far = jnp.where((dcol == drow) & (col >= row), 0.0, FAR)
        self.kept = (dcol == before).astype(F32)
        self.kept_dev = (dcol == before_dev).astype(F32)
        self.carry_dev = (before == before_dev).astype(F32)
        self.dt_in = dtr + dtb
        self.dt = softplus(self.dt_in)
        decay = self.dt * rate
        tri = (
            lax.broadcasted_iota(jnp.int32, (q, q), 0) >= lax.broadcasted_iota(jnp.int32, (q, q), 1)
        ).astype(F32)
        self.tri = tri
        self.cum = mm(tri, decay, precision=PRECISE)
        self.cum_t = self.cum.T
        self.lead = jnp.exp(self.cum) * self.kept
        end = self.cum[q - 1 : q, :]
        self.tail = jnp.exp(end - self.cum) * (dcol == last).astype(F32)
        self.end = end

    def fade(self, head):
        return jnp.exp(self.cum[:, head : head + 1] - self.cum_t[head : head + 1, :] + self.far)


def conv_block(pre, halo, cw, cb, match):
    taps = len(match) + 1
    ext = jnp.concatenate([halo, pre], axis=0)
    shifted = [
        pltpu.roll(ext, taps - 1 - k, 0)[8:] * match[k] for k in range(taps - 1)
    ] + [pre]
    conv = cb
    for k in range(taps):
        conv = conv + cw[k : k + 1] * shifted[k]
    return conv, shifted


def scan_kernel(dims, off, pos, *refs):
    scan_chunk(dims, pl.program_id(0), pl.program_id(1), off, pos[0], *refs)


def scan_chunk(dims, b, c, off, first, pre, rim, dtr, cw, cb, dtb, rate, dsk, y, rd, lead, st, lead0, fin, halo, state, run):
    q, inner, width, n = dims

    @pl.when(c == 0)
    def _():
        halo[...] = rim[0]
        state[...] = jnp.zeros_like(state)
        run[...] = jnp.zeros_like(run)

    taps = cw.shape[0]
    sp = Span(off, first, b, c * q, q, dtr[0], dtb[...], rate[...], taps)
    total = run[...] + sp.cum
    lead[0] = jnp.exp(total) * sp.kept_dev
    lead0[0, 0] = jnp.broadcast_to(jnp.exp(run[...]) * sp.carry_dev, (8, LANES))
    run[...] = total[q - 1 : q]

    def act(lo, hi):
        conv, _ = conv_block(
            pre[0, :, lo:hi].astype(F32), halo[:, lo:hi], cw[:, lo:hi], cb[:, lo:hi], sp.match
        )
        return conv * jax.nn.sigmoid(conv)

    write = act(inner, inner + n).astype(BF16)
    read = act(inner + n, inner + 2 * n).astype(BF16)
    rd[0] = read
    scores = mm(read, write, NT)
    write_t = write.astype(F32).T.astype(BF16)
    lane = lax.broadcasted_iota(jnp.int32, (1, LANES), 1)
    per = LANES // width
    for j in range(inner // LANES):
        lo, hi = j * LANES, (j + 1) * LANES
        h = j * per
        xs = act(lo, hi)
        xdt = xs * widen(sp.dt, h, lane, width)
        xdt_low = xdt.astype(BF16)
        mixed = None
        for i in range(per):
            part = mm((sp.fade(h + i) * scores).astype(BF16), xdt_low)
            mixed = part if mixed is None else jnp.where(lane >= i * width, part, mixed)
        old = state[:, lo:hi]
        st[0, 0, :, lo:hi] = old.astype(st.dtype)
        mixed = mixed + widen(sp.lead, h, lane, width) * mm(read, old.astype(BF16))
        y[0, :, lo:hi] = mixed + dsk[:, lo:hi] * xs
        fresh = mm(write_t, (xdt * widen(sp.tail, h, lane, width)).astype(BF16))
        new = widen(sp.lead[q - 1 : q], h, lane, width) * old + fresh
        state[:, lo:hi] = new
        fin[0, :, lo:hi] = new
    halo[...] = pre[0, q - 8 : q].astype(F32)


def gate_kernel(dims, y_in, rd, lead, lead0, st, s_in, z, gain, y, ygg, sq, st_full):
    q, inner, width, n = dims
    lane = lax.broadcasted_iota(jnp.int32, (1, LANES), 1)
    per = LANES // width
    total = jnp.zeros((q, LANES), F32)
    for j in range(inner // LANES):
        lo, hi = j * LANES, (j + 1) * LANES
        h = j * per
        came = s_in[0, :, lo:hi].astype(F32)
        full = st[0, 0, :, lo:hi].astype(F32) + widen(lead0[0, 0, 0:1], h, lane, width) * came
        st_full[0, 0, :, lo:hi] = full.astype(st_full.dtype)
        val = y_in[0, :, lo:hi] + widen(lead[0], h, lane, width) * mm(rd[0], came.astype(BF16))
        y[0, :, lo:hi] = val
        gate = z[0, :, lo:hi]
        gated = val * gate * jax.nn.sigmoid(gate)
        total = total + gated * gated
        ygg[0, :, lo:hi] = (gated * gain[:, lo:hi]).astype(BF16)
    sq[0] = jnp.broadcast_to(jnp.sum(total, axis=1, keepdims=True), (q, LANES))


def ungate_kernel(dims, count, dyn, y, z, stat, gain, rd, lead, dy, dz, yn, g_gain, g_state):
    b, c = pl.program_id(0), pl.program_id(1)

    @pl.when((b == 0) & (c == 0))
    def _():
        g_gain[...] = jnp.zeros_like(g_gain)

    @pl.when(c == 0)
    def _():
        g_state[...] = jnp.zeros_like(g_state)

    ungate_chunk(dims, count, dyn, y, z, stat, gain, rd, lead, dy, dz, yn, g_gain, g_state)


def ungate_chunk(dims, count, dyn, y, z, stat, gain, rd, lead, dy, dz, yn, g_gain, g_state):
    q, inner, width, n = dims
    lane = lax.broadcasted_iota(jnp.int32, (1, LANES), 1)
    per = LANES // width
    r2 = stat[0, :, 0:1]
    coef = r2 * r2 * r2 * stat[0, :, 1:2] * (1.0 / count)
    read_t = rd[0].astype(F32).T.astype(BF16)
    for j in range(inner // LANES):
        lo, hi = j * LANES, (j + 1) * LANES
        h = j * per
        gate = z[0, :, lo:hi]
        sig = jax.nn.sigmoid(gate)
        act = gate * sig
        val = y[0, :, lo:hi]
        gated = val * act
        dn = dyn[0, :, lo:hi]
        g = gain[:, lo:hi]
        norm = gated * r2
        g_gain[0:1, lo:hi] += jnp.sum(dn * norm, axis=0, keepdims=True)
        yn[0, :, lo:hi] = (norm * g).astype(BF16)
        d_gated = r2 * (dn * g) - gated * coef
        d_core = d_gated * act
        dy[0, :, lo:hi] = d_core
        dz[0, :, lo:hi] = (d_gated * val * silu_slope(gate, sig)).astype(BF16)
        g_state[0, :, lo:hi] += mm(read_t, (d_core * widen(lead[0], h, lane, width)).astype(BF16))


def back_kernel(dims, off, pos, pre, prev, rim, dtr, y, dy, st, d_in, *refs):
    acc, acc_head, d_state, carry = refs[-4:]
    b, c = pl.program_id(0), pl.program_id(1)
    at = pl.num_programs(1) - 1 - c

    @pl.when((b == 0) & (c == 0))
    def _():
        acc[...] = jnp.zeros_like(acc)
        acc_head[...] = jnp.zeros_like(acc_head)

    @pl.when(c == 0)
    def _():
        d_state[...] = d_in[0]
        carry[...] = jnp.zeros_like(carry)

    back_chunk(dims, b, at, c == 0, off, pos[0], pre, prev, rim, dtr, y, dy, st, *refs)


def back_chunk(dims, b, at, newest, off, first, pre, prev, rim, dtr, y, dy, st, cw, cb, dtb, rate, dsk,
               dcat, ddt_out, edge, rim_grad, acc, acc_head, d_state, carry):
    q, inner, width, n = dims
    taps = cw.shape[0]
    sp = Span(off, first, b, at * q, q, dtr[0], dtb[...], rate[...], taps)
    lane = lax.broadcasted_iota(jnp.int32, (1, LANES), 1)
    per = LANES // width

    def conv(lo, hi):
        ahead = jnp.where(at == 0, rim[0, :, lo:hi], prev[0, 8:16, lo:hi].astype(F32))
        return conv_block(pre[0, :, lo:hi].astype(F32), ahead, cw[:, lo:hi], cb[:, lo:hi], sp.match)

    def unconv(lo, hi, d_act, out, shifted, sig):
        d_conv = d_act * silu_slope(out, sig)
        acc[taps : taps + 1, lo:hi] += jnp.sum(d_conv, axis=0, keepdims=True)
        d_ext = None
        zeros = jnp.zeros((8, hi - lo), F32)
        for k in range(taps):
            acc[k : k + 1, lo:hi] += jnp.sum(d_conv * shifted[k], axis=0, keepdims=True)
            masked = cw[k : k + 1, lo:hi] * d_conv
            if k < taps - 1:
                masked = masked * sp.match[k]
            part = jnp.concatenate([zeros, masked], axis=0)
            if k < taps - 1:
                part = pltpu.roll(part, q + 8 - (taps - 1 - k), 0)
            d_ext = part if d_ext is None else d_ext + part
        d_pre = jnp.concatenate([d_ext[8:q], d_ext[q:] + carry[:, lo:hi]], axis=0)
        carry[:, lo:hi] = d_ext[0:8]
        rim_grad[0, :, lo:hi] = d_ext[0:8]
        dcat[0, :, lo:hi] = d_pre.astype(BF16)

        @pl.when(newest)
        def _():
            edge[0, :, lo:hi] = d_pre[q - 8 : q]

    w_conv, w_shift = conv(inner, inner + n)
    w_sig = jax.nn.sigmoid(w_conv)
    write = (w_conv * w_sig).astype(BF16)
    r_conv, r_shift = conv(inner + n, inner + 2 * n)
    r_sig = jax.nn.sigmoid(r_conv)
    read = (r_conv * r_sig).astype(BF16)
    scores = mm(read, write, NT)
    read_t = read.astype(F32).T.astype(BF16)
    d_scores = jnp.zeros((q, q), F32)
    d_write = jnp.zeros((q, n), F32)
    d_read = jnp.zeros((q, n), F32)
    d_cum = jnp.zeros((q, LANES), F32)
    d_step = jnp.zeros((q, LANES), F32)
    d_end = jnp.zeros((8, LANES), F32)
    for j in range(inner // LANES):
        lo, hi = j * LANES, (j + 1) * LANES
        h = j * per
        x_conv, x_shift = conv(lo, hi)
        x_sig = jax.nn.sigmoid(x_conv)
        xs = x_conv * x_sig
        step = widen(sp.dt, h, lane, width)
        xdt = xs * step
        xdt_low = xdt.astype(BF16)
        grad = dy[0, :, lo:hi]
        grad_low = grad.astype(BF16)
        core = y[0, :, lo:hi] - dsk[:, lo:hi] * xs
        late = d_state[:, lo:hi]
        late_low = late.astype(BF16)
        early = st[0, 0, :, lo:hi].astype(F32)
        tail = widen(sp.tail, h, lane, width)
        lead = widen(sp.lead, h, lane, width)
        u = None
        for i in range(per):
            fade = sp.fade(h + i)
            here = (lane >= i * width) & (lane < (i + 1) * width)
            own = jnp.where(here, grad, 0.0).astype(BF16)
            d_scores = d_scores + mm(own, xdt_low, NT) * fade
            part = mm((fade * scores).astype(BF16), grad_low, TN)
            u = part if u is None else jnp.where(lane >= i * width, part, u)
        from_end = tail * mm(write, late_low)
        inside = u
        u = u + from_end
        weighted = (lead * grad).astype(BF16)
        d_read = d_read + mm(weighted, early.astype(BF16), NT)
        d_write = d_write + mm((xdt * tail).astype(BF16), late_low, NT)
        end_lead = widen(sp.lead[q - 1 : q], h, lane, width)
        d_state[:, lo:hi] = end_lead * late + mm(read_t, weighted)
        head_of = (
            lax.broadcasted_iota(jnp.int32, (LANES, LANES), 0) // width + h
            == lax.broadcasted_iota(jnp.int32, (LANES, LANES), 1)
        ).astype(BF16)
        d_cum = d_cum + head_sums(
            grad_low.astype(F32) * core - xdt_low.astype(F32) * inside - xdt * from_end, head_of
        )
        d_step = d_step + head_sums(xs * u, head_of)
        end_row = end_lead * jnp.sum(late * early, axis=0, keepdims=True) + jnp.sum(
            xdt * from_end, axis=0, keepdims=True
        )
        d_end = d_end + head_sums(jnp.broadcast_to(end_row, (8, LANES)), head_of)
        acc[taps + 1 : taps + 2, lo:hi] += jnp.sum(grad * xs, axis=0, keepdims=True)
        unconv(lo, hi, step * u + dsk[:, lo:hi] * grad, x_conv, x_shift, x_sig)
    d_low = d_scores.astype(BF16)
    d_read = d_read + mm(d_low, write)
    d_write = d_write + mm(d_low, read, TN)
    unconv(inner, inner + n, d_write, w_conv, w_shift, w_sig)
    unconv(inner + n, inner + 2 * n, d_read, r_conv, r_shift, r_sig)
    d_decay = mm(sp.tri, d_cum, TN, precision=PRECISE) + d_end[0:1]
    acc_head[0:1] += jnp.sum(d_decay * sp.dt, axis=0, keepdims=True) * rate[...]
    d_dt = (d_step + d_decay * rate[...]) * jax.nn.sigmoid(sp.dt_in)
    acc_head[1:2] += jnp.sum(d_dt, axis=0, keepdims=True)
    ddt_out[0] = d_dt.astype(BF16)


def whole(shape):
    return pl.BlockSpec(shape, lambda *_: (0,) * len(shape))


def params():
    return pltpu.CompilerParams(vmem_limit_bytes=48 << 20)


def scan_forward(offs, pos, pre, rim, dtr, cw, cb, dtb, rate, dsk, width, n):
    nb, length, chans = pre.shape
    inner = dsk.shape[1]
    q = min(CHUNK, length)
    chunks = length // q
    dims = (q, inner, width, n)

    def rows(size):
        return pl.BlockSpec((1, q, size), lambda b, c, *_: (b, c, 0))

    return pl.pallas_call(
        functools.partial(scan_kernel, dims),
        grid_spec=pltpu.PrefetchScalarGridSpec(
            num_scalar_prefetch=2,
            grid=(nb, chunks),
            in_specs=[
                rows(chans),
                pl.BlockSpec((1, 8, chans), lambda b, c, *_: (b, 0, 0)),
                rows(LANES),
                whole(cw.shape),
                whole(cb.shape),
                whole(dtb.shape),
                whole(rate.shape),
                whole(dsk.shape),
            ],
            out_specs=[
                rows(inner),
                rows(n),
                rows(LANES),
                pl.BlockSpec((1, 1, n, inner), lambda b, c, *_: (b, c, 0, 0)),
                pl.BlockSpec((1, 1, 8, LANES), lambda b, c, *_: (b, c, 0, 0)),
                pl.BlockSpec((1, n, inner), lambda b, c, *_: (b, 0, 0)),
            ],
            scratch_shapes=[
                pltpu.VMEM((8, chans), F32),
                pltpu.VMEM((n, inner), F32),
                pltpu.VMEM((1, LANES), F32),
            ],
        ),
        out_shape=[
            jax.ShapeDtypeStruct((nb, length, inner), F32),
            jax.ShapeDtypeStruct((nb, length, n), BF16),
            jax.ShapeDtypeStruct((nb, length, LANES), F32),
            jax.ShapeDtypeStruct((nb, chunks, n, inner), F32),
            jax.ShapeDtypeStruct((nb, chunks, 8, LANES), F32),
            jax.ShapeDtypeStruct((nb, n, inner), F32),
        ],
        compiler_params=params(),
        name="scan_forward",
    )(offs, pos, pre, rim, dtr, cw, cb, dtb, rate, dsk)


def gate_forward(y_in, rd, lead, lead0, st, s_in, z, gain, width):
    nb, length, inner = y_in.shape
    chunks, n = st.shape[1], st.shape[2]
    q = length // chunks
    dims = (q, inner, width, n)

    def rows(size):
        return pl.BlockSpec((1, q, size), lambda b, c: (b, c, 0))

    def per_chunk(r, size):
        return pl.BlockSpec((1, 1, r, size), lambda b, c: (b, c, 0, 0))

    return pl.pallas_call(
        functools.partial(gate_kernel, dims),
        grid=(nb, chunks),
        in_specs=[
            rows(inner),
            rows(n),
            rows(LANES),
            per_chunk(8, LANES),
            per_chunk(n, inner),
            pl.BlockSpec((1, n, inner), lambda b, c: (b, 0, 0)),
            rows(inner),
            whole(gain.shape),
        ],
        out_specs=[rows(inner), rows(inner), rows(LANES), per_chunk(n, inner)],
        out_shape=[
            jax.ShapeDtypeStruct((nb, length, inner), F32),
            jax.ShapeDtypeStruct((nb, length, inner), BF16),
            jax.ShapeDtypeStruct((nb, length, LANES), F32),
            jax.ShapeDtypeStruct(st.shape, F32),
        ],
        compiler_params=params(),
        name="gate_forward",
    )(y_in, rd, lead, lead0, st, s_in, z, gain)


def gate_backward(dyn, y, z, stat, gain, rd, lead, width, count):
    nb, length, inner = y.shape
    n = rd.shape[2]
    q = min(CHUNK, length)
    chunks = length // q
    dims = (q, inner, width, n)

    def rows(size):
        return pl.BlockSpec((1, q, size), lambda b, c: (b, c, 0))

    return pl.pallas_call(
        functools.partial(ungate_kernel, dims, count),
        grid=(nb, chunks),
        in_specs=[
            rows(inner),
            rows(inner),
            rows(inner),
            rows(LANES),
            whole(gain.shape),
            rows(n),
            rows(LANES),
        ],
        out_specs=[
            rows(inner),
            rows(inner),
            rows(inner),
            whole((8, inner)),
            pl.BlockSpec((1, n, inner), lambda b, c: (b, 0, 0)),
        ],
        out_shape=[
            jax.ShapeDtypeStruct((nb, length, inner), F32),
            jax.ShapeDtypeStruct((nb, length, inner), BF16),
            jax.ShapeDtypeStruct((nb, length, inner), BF16),
            jax.ShapeDtypeStruct((8, inner), F32),
            jax.ShapeDtypeStruct((nb, n, inner), F32),
        ],
        compiler_params=params(),
        name="gate_backward",
    )(dyn, y, z, stat, gain, rd, lead)


def scan_backward(offs, pos, pre, rim, dtr, y, dy, st, d_in, cw, cb, dtb, rate, dsk, width):
    nb, length, chans = pre.shape
    inner = dsk.shape[1]
    chunks, n = st.shape[1], st.shape[2]
    q = length // chunks
    dims = (q, inner, width, n)
    per = q // 16

    def rows(size):
        return pl.BlockSpec((1, q, size), lambda b, c, *_: (b, chunks - 1 - c, 0))

    def per_seq(r, size):
        return pl.BlockSpec((1, r, size), lambda b, c, *_: (b, 0, 0))

    return pl.pallas_call(
        functools.partial(back_kernel, dims),
        grid_spec=pltpu.PrefetchScalarGridSpec(
            num_scalar_prefetch=2,
            grid=(nb, chunks),
            in_specs=[
                rows(chans),
                pl.BlockSpec(
                    (1, 16, chans), lambda b, c, *_: (b, jnp.maximum((chunks - 1 - c) * per - 1, 0), 0)
                ),
                per_seq(8, chans),
                rows(LANES),
                rows(inner),
                rows(inner),
                pl.BlockSpec((1, 1, n, inner), lambda b, c, *_: (b, chunks - 1 - c, 0, 0)),
                per_seq(n, inner),
                whole(cw.shape),
                whole(cb.shape),
                whole(dtb.shape),
                whole(rate.shape),
                whole(dsk.shape),
            ],
            out_specs=[
                rows(chans),
                rows(LANES),
                per_seq(8, chans),
                per_seq(8, chans),
                whole((8, chans)),
                whole((8, LANES)),
            ],
            scratch_shapes=[pltpu.VMEM((n, inner), F32), pltpu.VMEM((8, chans), F32)],
        ),
        out_shape=[
            jax.ShapeDtypeStruct((nb, length, chans), BF16),
            jax.ShapeDtypeStruct((nb, length, LANES), BF16),
            jax.ShapeDtypeStruct((nb, 8, chans), F32),
            jax.ShapeDtypeStruct((nb, 8, chans), F32),
            jax.ShapeDtypeStruct((8, chans), F32),
            jax.ShapeDtypeStruct((8, LANES), F32),
        ],
        compiler_params=params(),
        name="scan_backward",
    )(offs, pos, pre, pre, rim, dtr, y, dy, st, d_in, cw, cb, dtb, rate, dsk)


MESH = pl.DeviceIdType.MESH


def remote(src, dst, send, recv, **where):
    return pltpu.make_async_remote_copy(
        src_ref=src, dst_ref=dst, send_sem=send, recv_sem=recv, device_id=where, device_id_type=MESH
    )


class Line:
    def __init__(self, own, block, send, recv):
        self.own, self.block, self.send, self.recv = own, block, send, recv
        self.me = lax.axis_index("tp")
        self.peers = lax.axis_size("tp")

    def parts(self, k):
        for way, step in enumerate((1, -1)):
            slot = self.me - k * step
            there = self.me + step
            held = (slot >= 0) & (slot < self.peers)
            onward = held & (there >= 0) & (there < self.peers)
            slot = jnp.clip(slot, 0, self.peers - 1)
            here = self.own if k == 0 else self.block(slot)
            copy = remote(here, self.block(slot), self.send.at[way, k], self.recv.at[slot], tp=there)
            yield held, onward, copy

    def step(self, k):
        for held, onward, copy in self.parts(k):
            if k > 0:

                @pl.when(held)
                def _():
                    copy.wait_recv()

            @pl.when(onward)
            def _():
                copy.start()

    def finish(self):
        for k in range(self.peers - 1):
            for held, onward, copy in self.parts(k):

                @pl.when(onward)
                def _():
                    copy.wait_send()


def by_rows_of(size, total, body):
    @pl.loop(0, total // size)
    def _(i):
        body(pl.ds(pl.multiple_of(i * size, size), size))


def into_sum(mine, came):
    def body(rows):
        mine[rows, :] = (mine[rows, :].astype(F32) + came[rows, :].astype(F32)).astype(BF16)

    by_rows_of(32, mine.shape[0], body)


class Drain:
    def __init__(self, part, rows, wide, land, stage, send, recv, load):
        self.part, self.rows, self.wide, self.land, self.stage = part, rows, wide, land, stage
        self.send, self.recv, self.load = send, recv, load
        self.me = lax.axis_index("tp")
        self.peers = lax.axis_size("tp")

    def block(self, slot):
        return self.part.at[self.rows, pl.ds(pl.multiple_of(slot * self.wide, self.wide), self.wide)]

    def copy(self, way, slot):
        there = jnp.clip(self.me + (1, -1)[way], 0, self.peers - 1)
        return remote(
            self.block(slot), self.land.at[way, slot], self.send.at[way, slot], self.recv.at[way, slot], tp=there
        )

    def fetch(self, way, slot):
        return pltpu.make_async_copy(self.land.at[way, slot], self.stage.at[way], self.load.at[way])

    def add(self, way, slot):
        self.fetch(way, slot).wait()
        mine = self.block(slot)

        def body(rows):
            mine[rows, :] = (mine[rows, :].astype(F32) + self.stage[way, rows, :].astype(F32)).astype(BF16)

        by_rows_of(64, mine.shape[0], body)

    def ways(self, j):
        last = self.peers - 1
        for way, rank in ((0, self.me), (1, last - self.me)):
            behind = j - rank
            slot = last - behind if way == 0 else behind
            yield way, jnp.clip(slot, 0, last), behind >= 0, rank > 0

    def begin(self, way, slot, when):
        @pl.when(when)
        def _():
            self.copy(way, slot).wait_recv()
            self.fetch(way, slot).start()

    def round(self, j):
        for way, slot, sends, fed in self.ways(j):
            self.begin(way, slot, sends & fed)
        for way, slot, sends, fed in self.ways(j):

            @pl.when(sends & fed)
            def _():
                self.add(way, slot)

            @pl.when(sends)
            def _():
                self.copy(way, slot).start()

    def close(self):
        fed = (self.me > 0, self.me < self.peers - 1)
        for way in range(2):
            self.begin(way, self.me, fed[way])
        for way in range(2):

            @pl.when(fed[way])
            def _():
                self.add(way, self.me)

    def finish(self):
        for j in range(self.peers - 1):
            for way, slot, sends, _ in self.ways(j):

                @pl.when(sends)
                def _():
                    self.copy(way, slot).wait_send()


class Fold:
    def __init__(self, block, land1, land2, land3, stage, half, send, recv, load):
        self.block, self.land1, self.land2, self.land3 = block, land1, land2, land3
        self.stage, self.half, self.send, self.recv, self.load = stage, half, send, recv, load
        self.ctx, self.fs = lax.axis_index("ctx"), lax.axis_index("fsdp")
        self.core, self.y = lax.rem(self.fs, 2), self.fs // 2

    def first(self, c, y):
        i = 2 * c + y
        mate = self.fs + 1 - 2 * self.core
        return remote(
            self.block(c, y, 1 - self.core), self.land1.at[i], self.send.at[i], self.recv.at[i], fsdp=mate
        )

    def part(self, ref, way):
        return ref.at[pl.ds(way * self.half, self.half)]

    def second(self, way, i):
        if way == 0:
            src, peer = self.block(i, 1 - self.y, self.core), {"fsdp": lax.rem(self.fs + 2, 4)}
        else:
            src, peer = self.block(1 - self.ctx, i, self.core), {"ctx": 1 - self.ctx}
        k = 4 + 2 * way + i
        return remote(self.part(src, way), self.land2.at[way, i], self.send.at[k], self.recv.at[k], **peer)

    def third(self, way):
        if way == 0:
            src, peer = self.block(1 - self.ctx, self.y, self.core), {"ctx": 1 - self.ctx}
        else:
            src, peer = self.block(self.ctx, 1 - self.y, self.core), {"fsdp": lax.rem(self.fs + 2, 4)}
        k = 8 + way
        return remote(self.part(src, way), self.land3.at[way], self.send.at[k], self.recv.at[k], **peer)

    def gather(self, parts):
        def fetch(i):
            _, land, mine = parts[i]
            stage = self.stage.at[i % 2, pl.ds(0, mine.shape[0]), pl.ds(0, mine.shape[1])]
            return pltpu.make_async_copy(land, stage, self.load.at[i % 2]), stage

        for i in range(len(parts) + 1):
            if i < len(parts):
                parts[i][0].wait_recv()
                fetch(i)[0].start()
            if i:
                copy, stage = fetch(i - 1)
                copy.wait()
                mine = parts[i - 1][2]
                into_sum(mine, stage)

    def one(self):
        self.gather(
            [
                (self.first(c, y), self.land1.at[2 * c + y], self.block(c, y, self.core))
                for c in range(2)
                for y in range(2)
            ]
        )
        for way in range(2):
            for i in range(2):
                self.second(way, i).start()

    def two(self):
        self.gather(
            [
                (self.second(0, i), self.land2.at[0, i], self.part(self.block(i, self.y, self.core), 0))
                for i in range(2)
            ]
            + [
                (self.second(1, i), self.land2.at[1, i], self.part(self.block(self.ctx, i, self.core), 1))
                for i in range(2)
            ]
        )
        for way in range(2):
            self.third(way).start()

    def three(self):
        own = self.block(self.ctx, self.y, self.core)
        self.gather([(self.third(way), self.land3.at[way], self.part(own, way)) for way in range(2)])
        return own

    def finish(self):
        for i in range(2):
            for y in range(2):
                self.first(i, y).wait_send()
            self.second(0, i).wait_send()
            self.second(1, i).wait_send()
            self.third(i).wait_send()


IN = ["off", "x", "cot", "wx_in", "wz_in", "wo_in", "wbc_in", "wdt_in"]
IN += ["gain_in", "conv_w", "conv_b", "dt_bias", "a_log", "d_skip", "norm_gain"]


def layer_kernel(dims, names, *refs):
    r = types.SimpleNamespace(**dict(zip(names, refs)))
    nb, length, q, inner, width, n, d, inner_all, hpd = dims
    chunks = length // q
    tokens = nb * length
    chans = inner + 2 * n
    extra = 2 * n + LANES
    ctx, tp, fs = lax.axis_index("ctx"), lax.axis_index("tp"), lax.axis_index("fsdp")
    tps = lax.axis_size("tp")
    wide = d // tps
    deep = r.wx_in.shape[0]
    bd = d // 8
    core, yy = lax.rem(fs, 2), fs // 2
    mate = fs + 1 - 2 * core
    over = lax.rem(fs + 2, 4)
    other = 1 - ctx
    first = ctx * length
    small = (q, inner, width, n)
    dims_mode = (r.cw, r.cb, r.dtb, r.rate, r.dsk)

    def greet(**where):
        pl.semaphore_signal(barrier, inc=1, device_id=where, device_id_type=MESH)

    barrier = pltpu.get_barrier_semaphore()
    for step in range(1, tps):
        greet(tp=lax.rem(tp + step, tps))
    for c in range(2):
        for step in range(4):
            if c or step:
                greet(ctx=lax.rem(ctx + c, 2), fsdp=lax.rem(fs + step, 4))
    pl.semaphore_wait(barrier, tps - 1 + 7)

    def seq(m):
        return pl.ds(m * length, length)

    def one(ref, m):
        return ref.at[pl.ds(m, 1)]

    def span(ref, m, rows):
        return ref.at[pl.ds(m, 1), rows]

    def convolved(m, rows):
        return r.pre.at[pl.ds(m, 1), rows, pl.ds(0, chans)]

    def chunk_rows(c):
        return pl.ds(pl.multiple_of(c * q, q), q)

    mine = pl.ds(pl.multiple_of(tp * wide, wide), wide)
    own_pos = pl.ds(pl.multiple_of(fs * deep, deep), deep)
    rows_bc = r.wbc_in.shape[0]
    tight = 2 * n + hpd

    def features(ref, m):
        return lambda at: ref.at[seq(m), pl.ds(pl.multiple_of(at * wide, wide), wide)]

    def own(ref, m):
        return ref.at[seq(m)]

    x_lines = [Line(own(r.x, m), features(r.x_all, m), r.xs_send.at[m], r.xs_recv.at[m]) for m in range(nb)]
    c_lines = [Line(own(r.cot, m), features(r.cot_o, m), r.cs_send.at[m], r.cs_recv.at[m]) for m in range(nb)]
    bc_rows = pl.ds(pl.multiple_of(tp * rows_bc, rows_bc), rows_bc)

    def bc_in_copy(step):
        there = lax.rem(tp + step, tps)
        return remote(
            r.wbc_in, r.wst.at[bc_rows, own_pos], r.v_send.at[step], r.v_recv.at[tp], tp=there
        )

    def bc_in_recv(step):
        there = lax.rem(tp + step, tps)
        rows = pl.ds(pl.multiple_of(there * rows_bc, rows_bc), rows_bc)
        remote(
            r.wbc_in, r.wst.at[rows, own_pos], r.v_send.at[step], r.v_recv.at[there], tp=there
        ).wait_recv()

    def slot(w, at):
        rows = pl.ds(pl.multiple_of(at * deep, deep), deep)
        return (r.wx.at[rows], r.wz.at[rows], r.wo.at[:, rows], r.wst.at[pl.ds(0, tight), rows])[w]

    owns = (r.wx_in, r.wz_in, r.wo_in, slot(3, fs))

    def near(w):
        return remote(owns[w], slot(w, fs), r.w_send.at[w, 0], r.w_recv.at[w, fs], fsdp=mate)

    def far(w):
        return remote(owns[w], slot(w, fs), r.w_send.at[w, 1], r.w_recv.at[w, fs], fsdp=over)

    def relay(w):
        return remote(slot(w, over), slot(w, over), r.w_send.at[w, 2], r.w_recv.at[w, over], fsdp=mate)

    def arrive(w, at):
        remote(slot(w, at), slot(w, at), r.w_send.at[w, 0], r.w_recv.at[w, at], fsdp=mate).wait_recv()

    locals_ = [pltpu.make_async_copy(owns[w], slot(w, fs), r.loc.at[w]) for w in range(3)]
    locals_.append(pltpu.make_async_copy(r.x, r.x_all.at[:, mine], r.loc.at[3]))
    locals_.append(pltpu.make_async_copy(r.cot, r.cot_o.at[:, mine], r.loc.at[4]))
    locals_.append(pltpu.make_async_copy(r.wbc_in, r.wst.at[bc_rows, own_pos], r.loc.at[5 + nb]))
    locals_.append(pltpu.make_async_copy(r.wdt_in, r.wst.at[pl.ds(2 * n, hpd), own_pos], r.loc.at[6 + nb]))

    def pass_on(w):
        arrive(w, over)
        relay(w).start()

    def whole_weight(w):
        arrive(w, mate)
        arrive(w, lax.rem(mate + 2, 4))
        if w < 3:
            locals_[w].wait()

    def prepare():
        lane = lax.broadcasted_iota(jnp.int32, (8, LANES), 1)
        chan = pl.ds(pl.multiple_of(tp * inner, inner), inner)
        r.cw[:, :inner] = r.conv_w[:, chan]
        r.cw[:, inner:] = r.conv_w[:, inner_all:]
        r.cb[:, :inner] = r.conv_b[:, chan]
        r.cb[:, inner:] = r.conv_b[:, inner_all:]
        r.gain[...] = r.norm_gain[:, chan]

        def own_heads(ref):
            wide_row = jnp.concatenate([ref[...], jnp.zeros((1, LANES - ref.shape[1]), F32)], axis=1)
            turned = pltpu.roll(jnp.broadcast_to(wide_row, (8, LANES)), lax.rem(LANES - tp * hpd, LANES), 1)
            return jnp.where(lane < hpd, turned, 0.0)

        r.dtb[...] = own_heads(r.dt_bias)[0:1]
        r.rate[...] = jnp.where(lane < hpd, -jnp.exp(own_heads(r.a_log)), 0.0)[0:1]
        head_of = (
            lax.broadcasted_iota(jnp.int32, (LANES, inner), 0)
            == lax.broadcasted_iota(jnp.int32, (LANES, inner), 1) // width
        ).astype(F32)
        r.dsk[...] = mm(own_heads(r.d_skip), head_of, precision=PRECISE)[0:1]
        r.wst[tight:, :] = jnp.zeros((LANES - hpd, d), BF16)
        for ref in (r.g_gain, r.g_in, r.acc, r.acc_head):
            ref[...] = jnp.zeros_like(ref)

    def norm(m):
        @pl.loop(0, chunks)
        def _(i):
            rows = pl.ds(pl.multiple_of(m * length + i * q, q), q)
            total = jnp.zeros((q, LANES), F32)
            for j in range(d // LANES):
                v = r.x_all[rows, j * LANES : (j + 1) * LANES].astype(F32)
                total = total + v * v
            inv = lax.rsqrt(jnp.sum(total, axis=1, keepdims=True) * (1.0 / d) + EPSILON)
            r.r1[rows, :] = jnp.broadcast_to(inv, (q, LANES))
            for j in range(d // LANES):
                cols = slice(j * LANES, (j + 1) * LANES)
                r.xn[rows, cols] = (r.x_all[rows, cols].astype(F32) * inv * r.gain_in[:, cols]).astype(BF16)

    tile = min(2 * LANES, inner)

    def tiles(total, body, size=tile):
        @pl.loop(0, total // size)
        def _(j):
            body(pl.ds(pl.multiple_of(j * size, size), size))

    def rim_copy(m):
        return remote(
            r.pre.at[m, pl.ds(length - 16, 16), pl.ds(0, chans)], r.rim16.at[m], r.r_send.at[m], r.r_recv.at[m], ctx=other
        )

    def project_x(m):
        for half in (1, 0):
            size = length // 2
            rows = pl.ds(m * length + half * size, size)
            here = pl.ds(half * size, size)
            both = mm(r.xn[rows, :], r.wst[...], NT)
            r.dtr[m, here, :] = both[:, 2 * n :]
            r.pre[m, here, inner:chans] = both[:, : 2 * n].astype(BF16)

            def body(cols):
                r.pre[m, here, cols] = mm(r.xn[rows, :], r.wx[:, cols]).astype(BF16)

            tiles(inner, body)
            if half == 1:

                @pl.when(ctx == 0)
                def _():
                    rim_copy(m).start()

    def project_z(m):
        def body(cols):
            r.z[m, :, cols] = mm(r.xn[seq(m), :], r.wz[:, cols])

        tiles(inner, body)

    def get_rim(m):
        @pl.when(ctx == 1)
        def _():
            rim_copy(m).wait_recv()
            r.rim[m] = r.rim16[m, 8:16].astype(F32)

        @pl.when(ctx == 0)
        def _():
            r.rim[m] = jnp.zeros_like(r.rim[m])

    def scan(m):
        @pl.loop(0, chunks)
        def _(c):
            rows = chunk_rows(c)
            scan_chunk(
                small, m, c, r.off, first,
                convolved(m, rows), one(r.rim, m), span(r.dtr, m, rows), *dims_mode,
                span(r.y, m, rows), span(r.rd, m, rows), span(r.lead, m, rows),
                r.st.at[pl.ds(m, 1), pl.ds(c, 1)], r.lead0.at[pl.ds(m, 1), pl.ds(c, 1)], one(r.fin, 0),
                r.halo, r.state, r.run,
            )

    def state_copy(m, back):
        return remote(
            r.left.at[m], r.came.at[back, m], r.s_send.at[back, m], r.s_recv.at[back, m], ctx=other
        )

    def send_state(m, back):
        @pl.when(ctx == back)
        def _():
            if back == 0:
                rim_copy(m).wait_send()
            r.left[m] = r.fin[0].astype(BF16)
            state_copy(m, back).start()

    def get_state(m, back):
        @pl.when(ctx == 1 - back)
        def _():
            state_copy(m, back).wait_recv()

        @pl.when(ctx == back)
        def _():
            r.came[back, m] = jnp.zeros_like(r.came[back, m])

    def gate(m):
        @pl.loop(0, chunks)
        def _(c):
            rows = chunk_rows(c)
            sts = r.st.at[pl.ds(m, 1), pl.ds(c, 1)]
            ys = span(r.y, m, rows)
            gate_kernel(
                small, ys, span(r.rd, m, rows), span(r.lead, m, rows),
                r.lead0.at[pl.ds(m, 1), pl.ds(c, 1)], sts, r.came.at[0, pl.ds(m, 1)], span(r.z, m, rows), r.gain,
                ys, span(r.yn, m, rows), span(r.sq, m, rows), sts,
            )

    def project_out(m):
        def body(cols):
            r.part[seq(m), cols] = mm(r.yn[m], r.wo[:, cols]).astype(BF16)

        tiles(d, body, 2 * LANES)

    def drains(part, land, send, recv):
        return [
            Drain(part, seq(m), wide, land.at[m], r.stage, send.at[m], recv.at[m], r.load.at[0])
            for m in range(nb)
        ]

    o_drains = drains(r.part, r.o_land, r.od_send, r.od_recv)
    d_drains = drains(r.part, r.d_land, r.dd_send, r.dd_recv)

    def stat_copy(m, kind, there):
        return remote(
            r.stat_out.at[kind, m], r.stat_in.at[kind, m, tp],
            r.t_send.at[kind, m, there], r.t_recv.at[kind, m, tp], tp=there,
        )

    def send_stat(m, kind, columns):
        lane = lax.broadcasted_iota(jnp.int32, (1, LANES), 1)
        both = jnp.where(lane == 0, columns[0], columns[-1])
        rows = both.T[0:8]
        r.stat_out[kind, m] = rows
        r.stat_in[kind, m, tp] = rows
        for step in range(1, tps):
            stat_copy(m, kind, lax.rem(tp + step, tps)).start()

    def get_stat(m, kind):
        for step in range(1, tps):
            there = lax.rem(tp + step, tps)
            remote(
                r.stat_out.at[kind, m], r.stat_in.at[kind, m, there],
                r.t_send.at[kind, m, there], r.t_recv.at[kind, m, there], tp=there,
            ).wait_recv()
        total = r.stat_in[kind, m, 0]
        for i in range(1, tps):
            total = total + r.stat_in[kind, m, i]
        full = jnp.concatenate([total, jnp.zeros((LANES - 8, length), F32)], axis=0)
        return full.T

    def load_cot(m):
        return pltpu.make_async_copy(r.cot_o.at[seq(m)], r.x_all.at[seq(m)], r.loc.at[5 + m])

    def d_gate(m):
        def body(cols):
            r.dyn[0, :, cols] = mm(r.x_all[seq(m), :], r.wo[cols, :], NT)

        tiles(inner, body)

        def dot(rows):
            total = jnp.zeros((64, LANES), F32)
            for lo in range(0, inner, LANES):
                cols = slice(lo, lo + LANES)
                gate_in = r.z[m, rows, cols]
                gated = r.y[m, rows, cols] * gate_in * jax.nn.sigmoid(gate_in)
                total = total + r.dyn[0, rows, cols] * r.gain[:, cols] * gated
            r.dots[rows, :] = jnp.broadcast_to(jnp.sum(total, axis=1, keepdims=True), (64, LANES))

        by_rows_of(64, length, dot)
        send_stat(m, 0, [r.sq[m], r.dots[...]])

    def ungate(m):
        full = get_stat(m, 0)
        lane = lax.broadcasted_iota(jnp.int32, (1, LANES), 1)
        r.sq[m] = jnp.where(lane == 0, lax.rsqrt(full * (1.0 / inner_all) + EPSILON), full)
        r.fin[...] = jnp.zeros_like(r.fin)

        @pl.loop(0, chunks)
        def _(c):
            rows = chunk_rows(c)
            zs = span(r.z, m, rows)
            ungate_chunk(
                small, inner_all, r.dyn.at[:, rows], span(r.y, m, rows), zs, span(r.sq, m, rows), r.gain,
                span(r.rd, m, rows), span(r.lead, m, rows),
                zs, span(r.dz, m, rows), span(r.yn, m, rows), r.g_gain, one(r.fin, 0),
            )

        send_state(m, 1)

    def back(m, after):
        r.d_state[...] = r.came[1, m].astype(F32)
        r.carry[...] = jnp.zeros_like(r.carry)

        @pl.loop(0, chunks)
        def _(c):
            at = chunks - 1 - c
            rows = chunk_rows(at)
            ahead = pl.ds(pl.multiple_of(jnp.maximum(at * q - 16, 0), 16), 16)
            here = convolved(m, rows)
            back_chunk(
                small, m, at, c == 0, r.off, first, here, convolved(m, ahead), one(r.rim, m),
                span(r.dtr, m, rows), span(r.y, m, rows), span(r.z, m, rows),
                r.st.at[pl.ds(m, 1), pl.ds(at, 1)], *dims_mode,
                here, r.pre.at[pl.ds(m, 1), rows, pl.ds(chans, LANES)], one(r.edge, m), one(r.rim_out, m),
                r.acc, r.acc_head, r.d_state, r.carry,
            )
            for k, hook in after.items():
                pl.when(c == k)(hook)

        @pl.when(ctx == 1)
        def _():
            edge_copy(m).start()

    def edge_copy(m):
        return remote(r.rim_out.at[m], r.rim_in.at[m], r.e_send.at[m], r.e_recv.at[m], ctx=other)

    def patch(m):
        @pl.when(ctx == 0)
        def _():
            edge_copy(m).wait_recv()
            rows = pl.ds(length - 16, 16)
            late = (r.edge[m] + r.rim_in[m]).astype(BF16).astype(F32)
            both = jnp.concatenate([r.pre[m, rows, :chans].astype(F32)[0:8], late], axis=0)
            r.pre[m, rows, :chans] = both.astype(BF16)

    def d_norm(m, at):
        size = min(2 * LANES, wide)

        @pl.loop(0, wide // size)
        def _(j):
            cols = pl.ds(pl.multiple_of(at * wide + j * size, size), size)
            total = mm(r.dz[m], r.wz[cols, :], NT) + mm(r.pre[m, :, :inner], r.wx[cols, :], NT)
            total = total + mm(r.pre[m, :, inner:], r.wst[:, cols])
            r.part[seq(m), cols] = total.astype(BF16)
            prod = total * r.xn[seq(m), cols].astype(F32)
            r.g_in[0:1, cols] += jnp.sum(prod, axis=0, keepdims=True)
            lanes = r.dots[...]
            for lo in range(0, size, LANES):
                lanes = lanes + prod[:, lo : lo + LANES]
            r.dots[...] = lanes

    def send_dots(m):
        dot = jnp.sum(r.dots[...], axis=1, keepdims=True)
        send_stat(m, 1, [jnp.broadcast_to(dot, (length, LANES))])

    def rb(c, y, k):
        return 4 * c + 2 * y + k

    def by_rows(ref):
        return lambda c, y, k: ref.at[
            pl.ds(pl.multiple_of((2 * y + k) * bd, bd), bd), pl.ds(c * inner, inner)
        ]

    def folds(i, block, lands):
        return Fold(block, *lands, r.stage_z, bd // 2, r.f_send.at[i], r.f_recv.at[i], r.load.at[1])

    fold_o = folds(0, by_rows(r.wo), (r.o1, r.o2, r.o3))
    fold_z = folds(1, by_rows(r.x_all), (r.z1, r.z2, r.z3))
    fold_x = folds(2, by_rows(r.wo), (r.x1, r.x2, r.x3))
    fold_s = folds(
        3,
        lambda c, y, k: r.yn.at[
            y, pl.ds(pl.multiple_of(k * bd, bd), bd), pl.ds(pl.multiple_of(c * extra, LANES), extra)
        ],
        (r.s1, r.s2, r.s3),
    )

    def xn_cols(c, y, k):
        return r.xn[:, pl.ds(pl.multiple_of(rb(c, y, k) * bd, bd), bd)]

    def grad_o(c, y, k):
        cot = r.x_all[:, pl.ds(pl.multiple_of(rb(c, y, k) * bd, bd), bd)]
        fold_o.block(c, y, k)[...] = mm(cot, r.yn[...].reshape(tokens, inner), TN).astype(BF16)

    def grad_z(c, y, k):
        fold_z.block(c, y, k)[...] = mm(xn_cols(c, y, k), r.dz[...].reshape(tokens, inner), TN).astype(BF16)

    def grad_x(c, y, k):
        left = xn_cols(c, y, k)
        fold_x.block(c, y, k)[...] = mm(left, r.pre[:, :, :inner].reshape(tokens, inner), TN).astype(BF16)
        fold_s.block(c, y, k)[...] = mm(left, r.pre[:, :, inner:].reshape(tokens, extra), TN).astype(BF16)

    def send_grads(make, *fold):
        for c in range(2):
            for y in range(2):
                make(c, y, 1 - core)
                for f in fold:
                    f.first(c, y).start()

    def own_grads(make):
        for c in range(2):
            for y in range(2):
                make(c, y, core)

    out_copies = []

    def keep(pair):
        out_copies.append(pair)
        kept(len(out_copies) - 1).start()

    waited = []

    def settle(i):
        kept(i).wait()
        waited.append(i)

    def kept(i):
        return pltpu.make_async_copy(*out_copies[i](), r.outs.at[i])

    def give_out(m):
        o_drains[m].close()
        keep(lambda: (r.part.at[seq(m), mine], r.out.at[seq(m)]))
        keep(lambda: (r.sq.at[m], r.stat.at[seq(m)]))

    def give_dx(m):
        d_drains[m].close()
        keep(lambda: (r.part.at[seq(m), mine], r.dx.at[seq(m)]))

    def give_dots(m):
        lane = lax.broadcasted_iota(jnp.int32, (1, LANES), 1)
        dot = get_stat(m, 1)[:, 0:1]
        r.lead[m] = jnp.where(lane == 0, r.r1[seq(m), :], dot)
        keep(lambda: (r.lead.at[m], r.stat2.at[seq(m)]))

    def device(j):
        c, s = j // 4, j % 4
        return lax.rem(ctx + c, 2), lax.rem(fs + s, 4)

    def tiny_copy(j):
        c, f = device(j)
        return remote(
            r.tiny.at[:], r.tiny_in.at[4 * ctx + fs], r.y_send.at[j], r.y_recv.at[4 * ctx + fs], ctx=c, fsdp=f
        )

    def tiny_recv(j):
        c, f = device(j)
        at = 4 * c + f
        remote(r.tiny.at[:], r.tiny_in.at[at], r.y_send.at[j], r.y_recv.at[at], ctx=c, fsdp=f).wait_recv()

    def spread_copy(step):
        there = lax.rem(tp + step, tps)
        return remote(r.tiny_sum.at[:], r.tiny_all.at[tp], r.q_send.at[step], r.q_recv.at[tp], tp=there)

    def bc_copy(step):
        there = lax.rem(tp + step, tps)
        return remote(r.bc_sum.at[:], r.bc_all.at[tp], r.b_send.at[step], r.b_recv.at[tp], tp=there)

    x_0, x_1 = x_lines
    c_0, c_1 = c_lines
    o_0, o_1 = o_drains
    d_0, d_1 = d_drains
    last = tps - 1

    def steps(line, lo, hi=tps):
        for k in range(lo, hi):
            line.step(k)

    def rounds(drain, lo, hi=last):
        for j in range(lo, hi):
            drain.round(j)

    for step in range(1, tps):
        bc_in_copy(step).start()
    x_0.step(0)
    far(0).start()
    near(0).start()
    for copy in locals_:
        copy.start()
    prepare()
    for step in range(1, tps):
        bc_in_recv(step)
    locals_[5].wait()
    locals_[6].wait()
    for w in (3, 1, 2):
        far(w).start()
        near(w).start()
    steps(x_0, 1, last)
    pass_on(3)
    pass_on(0)
    steps(x_0, last)
    c_0.step(0)
    locals_[3].wait()
    norm(0)
    whole_weight(0)
    whole_weight(3)
    project_x(0)
    get_rim(0)
    scan(0)
    send_state(0, 0)
    c_0.step(1)
    pass_on(1)
    whole_weight(1)
    project_z(0)
    get_state(0, 0)
    gate(0)
    c_0.step(2)
    pass_on(2)
    whole_weight(2)
    project_out(0)
    steps(c_0, 3)
    locals_[4].wait()
    x_0.finish()
    load_cot(0).start()
    load_cot(0).wait()
    d_gate(0)
    x_1.step(0)
    ungate(0)
    x_1.step(1)
    o_0.round(0)
    get_state(0, 1)

    def middle_0():
        x_1.step(2)
        o_0.round(1)

    def middle_2():
        steps(x_1, 3)
        c_1.step(0)
        norm(1)
        project_x(1)
        get_rim(1)
        c_1.step(1)
        scan(1)
        send_state(1, 0)
        project_z(1)
        c_1.step(2)
        rounds(o_0, 2)
        get_state(1, 0)
        gate(1)
        project_out(1)
        o_1.round(0)

    back(0, {0: middle_0, 2: middle_2})
    steps(c_1, 3)
    x_1.finish()
    load_cot(1).start()
    load_cot(1).wait()
    d_gate(1)
    o_1.round(1)
    ungate(1)
    give_out(0)
    o_0.finish()
    patch(0)
    r.dots[...] = jnp.zeros_like(r.dots)
    settle(0)
    d_norm(0, last)
    d_norm(0, 0)
    rounds(o_1, 2)
    for k in range(1, last):
        d_norm(0, last - k)
    send_dots(0)
    get_state(1, 1)

    def late_0():
        relay(2).wait_send()
        send_grads(grad_o, fold_o)
        d_0.round(0)
        own_grads(grad_o)

    def late_1():
        fold_o.one()
        send_grads(grad_z, fold_z)
        own_grads(grad_z)
        d_0.round(1)

    def late_2():
        fold_z.one()
        fold_o.two()
        give_out(1)
        rounds(d_0, 2)

    back(1, {0: late_0, 1: late_1, 2: late_2})
    fold_o.three()
    keep(lambda: (fold_o.block(ctx, yy, core), r.go))
    o_1.finish()
    fold_z.two()
    fold_o.finish()
    settle(4)
    patch(1)
    send_grads(grad_x, fold_x, fold_s)
    r.dots[...] = jnp.zeros_like(r.dots)
    settle(2)
    d_norm(1, last)
    d_norm(1, 0)
    d_1.round(0)
    own_grads(grad_x)
    fold_s.one()
    fold_x.one()
    for k in range(1, last):
        d_norm(1, last - k)
    d_1.round(1)
    send_dots(1)
    taps = r.cw.shape[0]
    r.tiny[...] = jnp.zeros_like(r.tiny)
    r.tiny[0:8, :chans] = r.acc[...]
    r.tiny[8:9, :inner] = r.g_gain[0:1]
    for i in range(d // inner):
        r.tiny[9 + i : 10 + i, :inner] = r.g_in[0:1, i * inner : (i + 1) * inner]
    heads_at = 9 + d // inner
    r.tiny[heads_at : heads_at + 2, :LANES] = r.acc_head[0:2]
    head_of = (
        lax.broadcasted_iota(jnp.int32, (inner, LANES), 0) // width
        == lax.broadcasted_iota(jnp.int32, (inner, LANES), 1)
    ).astype(F32)
    r.tiny[heads_at + 2 : heads_at + 3, :LANES] = mm(r.acc[:, :inner], head_of, precision=PRECISE)[
        taps + 1 : taps + 2
    ]
    for j in range(1, 8):
        tiny_copy(j).start()
    r.tiny_in[4 * ctx + fs] = r.tiny[...]
    give_dx(0)
    give_dots(0)
    rounds(d_1, 2)
    fold_z.three()
    keep(lambda: (fold_z.block(ctx, yy, core), r.gz))
    fold_s.two()
    fold_x.two()
    for j in range(1, 8):
        tiny_recv(j)
    total = r.tiny_in[0]
    for i in range(1, 8):
        total = total + r.tiny_in[i]
    r.tiny_sum[...] = total
    r.tiny_all[tp] = total
    for step in range(1, tps):
        spread_copy(step).start()
    give_dots(1)
    sums = fold_s.three()
    r.gdt[...] = sums[:, 2 * n :].astype(F32).T[:hpd]
    r.bc_sum[...] = sums[:, : 2 * n]
    r.bc_all[tp] = sums[:, : 2 * n]
    for step in range(1, tps):
        bc_copy(step).start()
    give_dx(1)
    fold_x.three()
    keep(lambda: (fold_x.block(ctx, yy, core), r.gx))
    for step in range(1, tps):
        there = lax.rem(tp + step, tps)
        remote(r.bc_sum.at[:], r.bc_all.at[there], r.b_send.at[step], r.b_recv.at[there], tp=there).wait_recv()
    total = r.bc_all[0].astype(F32)
    for i in range(1, tps):
        total = total + r.bc_all[i].astype(F32)
    total = total.T
    share = jnp.zeros((rows_bc, bd), F32)
    for t in range(tps):
        share = share + jnp.where(tp == t, total[t * rows_bc : (t + 1) * rows_bc], 0.0)
    r.gbc[...] = share
    for step in range(1, tps):
        there = lax.rem(tp + step, tps)
        remote(r.tiny_sum.at[:], r.tiny_all.at[there], r.q_send.at[step], r.q_recv.at[there], tp=there).wait_recv()
    both_w, both_b, both_g, per_head = 0.0, 0.0, 0.0, 0.0
    lane = lax.broadcasted_iota(jnp.int32, (8, LANES), 1)
    for t in range(tps):
        every = r.tiny_all.at[t]
        chan = slice(t * inner, (t + 1) * inner)
        r.g_cw[:, chan] = every[0:taps, :inner]
        r.g_cb[:, chan] = every[taps : taps + 1, :inner]
        r.g_ng[:, chan] = every[8:9, :inner]
        both_w = both_w + every[0:taps, inner:]
        both_b = both_b + every[taps : taps + 1, inner:]
        both_g = both_g + every[9 : 9 + d // inner, :inner]
        heads_t = jnp.where(lane < hpd, every[8:16, :LANES], 0.0)
        per_head = per_head + (pltpu.roll(heads_t, t * hpd, 1) if t else heads_t)
    r.g_cw[:, inner_all:] = both_w
    r.g_cb[:, inner_all:] = both_b
    for i in range(d // inner):
        cols = slice(i * inner, (i + 1) * inner)
        r.g_ig[:, cols] = both_g[i : i + 1] / r.gain_in[:, cols]
    count = r.dt_bias.shape[1]
    at = heads_at - 8
    r.g_al[...] = per_head[at : at + 1, :count]
    r.g_db[...] = per_head[at + 1 : at + 2, :count]
    r.g_ds[...] = per_head[at + 2 : at + 3, :count]

    for step in range(1, tps):
        bc_in_copy(step).wait_send()
    for line in c_lines + d_drains:
        line.finish()
    for fold in (fold_z, fold_x, fold_s):
        fold.finish()
    for w in range(4):
        near(w).wait_send()
        far(w).wait_send()
        if w != 2:
            relay(w).wait_send()
    for m in range(nb):
        for kind in range(2):
            for step in range(1, tps):
                stat_copy(m, kind, lax.rem(tp + step, tps)).wait_send()

        @pl.when(ctx == 0)
        def _():
            state_copy(m, 0).wait_send()

        @pl.when(ctx == 1)
        def _():
            state_copy(m, 1).wait_send()
            edge_copy(m).wait_send()

    for j in range(1, 8):
        tiny_copy(j).wait_send()
    for step in range(1, tps):
        spread_copy(step).wait_send()
        bc_copy(step).wait_send()
    for i in range(len(out_copies)):
        if i not in waited:
            kept(i).wait()


SMALL = ["gdt", "gbc", "g_cw", "g_cb", "g_ng", "g_ig", "g_al", "g_db", "g_ds"]


def layer(args, nb, length, inner_dev_heads, width, n, tps, inner_all):
    offs, x, cot, wx = args[:4]
    hpd = inner_dev_heads
    tokens, wide = x.shape
    d = wide * tps
    inner = wx.shape[1]
    chans = inner + 2 * n
    extra = 2 * n + LANES
    q = min(CHUNK, length)
    chunks = length // q
    bd = d // 8
    dims = (nb, length, q, inner, width, n, d, inner_all, hpd)
    taps = args[9].shape[0]
    sds = jax.ShapeDtypeStruct
    outs = dict(
        out=((tokens, wide), BF16), dx=((tokens, wide), BF16), gz=((bd, inner), BF16), gx=((bd, inner), BF16),
        stat=((tokens, LANES), F32), stat2=((tokens, LANES), F32),
        gdt=((hpd, bd), F32), gbc=((2 * n // tps, bd), F32), go=((bd, inner), BF16),
        g_cw=((taps, inner_all + 2 * n), F32), g_cb=((1, inner_all + 2 * n), F32), g_ng=((1, inner_all), F32),
        g_ig=((1, d), F32), g_al=(args[11].shape, F32), g_db=(args[11].shape, F32), g_ds=(args[11].shape, F32),
        cot_o=((tokens, d), BF16),
        o_land=((nb, 2, tps, length, wide), BF16), d_land=((nb, 2, tps, length, wide), BF16),
        o1=((4, bd, inner), BF16), o2=((2, 2, bd // 2, inner), BF16), o3=((2, bd // 2, inner), BF16),
        z1=((4, bd, inner), BF16), z2=((2, 2, bd // 2, inner), BF16), z3=((2, bd // 2, inner), BF16),
        x1=((4, bd, inner), BF16), x2=((2, 2, bd // 2, inner), BF16), x3=((2, bd // 2, inner), BF16),
        s1=((4, bd, extra), BF16), s2=((2, 2, bd // 2, extra), BF16), s3=((2, bd // 2, extra), BF16),
    )
    vmem = dict(
        x_all=((tokens, d), BF16), xn=((tokens, d), BF16), r1=((tokens, LANES), F32),
        pre=((nb, length, chans + LANES), BF16), dtr=((nb, length, LANES), F32), z=((nb, length, inner), F32),
        y=((nb, length, inner), F32), rd=((nb, length, n), BF16), lead=((nb, length, LANES), F32),
        st=((nb, chunks, n, inner), BF16), lead0=((nb, chunks, 8, LANES), F32), fin=((1, n, inner), F32),
        sq=((nb, length, LANES), F32), yn=((nb, length, inner), BF16), part=((tokens, d), BF16),
        rim=((nb, 8, chans), F32), rim16=((nb, 16, chans), BF16), came=((2, nb, n, inner), BF16),
        left=((nb, n, inner), BF16), wx=((d, inner), BF16), wz=((d, inner), BF16), wo=((inner, d), BF16),
        halo=((8, chans), F32), state=((n, inner), F32), run=((1, LANES), F32),
        dyn=((1, length, inner), F32), dz=((nb, length, inner), BF16),
        dots=((length, LANES), F32), g_gain=((8, inner), F32), g_in=((8, d), F32),
        acc=((8, chans), F32), acc_head=((8, LANES), F32), carry=((8, chans), F32),
        edge=((nb, 8, chans), F32), rim_out=((nb, 8, chans), F32), rim_in=((nb, 8, chans), F32),
        stat_out=((2, nb, 8, length), F32), stat_in=((2, nb, tps, 8, length), F32),
        stage=((2, length, wide), BF16), stage_z=((2, bd, max(inner, extra)), BF16),
        wst=((2 * n + LANES, d), BF16), d_state=((n, inner), F32), cw=((taps, chans), F32), cb=((1, chans), F32),
        gain=((1, inner), F32), dtb=((1, LANES), F32), rate=((1, LANES), F32),
        dsk=((1, inner), F32),

        bc_sum=((bd, 2 * n), BF16),
        bc_all=((tps, bd, 2 * n), BF16), tiny=((16, chans), F32), tiny_in=((8, 16, chans), F32),
        tiny_sum=((16, chans), F32), tiny_all=((tps, 16, chans), F32),
    )
    sems = dict(
        xs_send=(nb, 2, tps), xs_recv=(nb, tps), cs_send=(nb, 2, tps), cs_recv=(nb, tps),
        w_send=(4, 3), w_recv=(4, 4), r_send=(nb,), r_recv=(nb,), s_send=(2, nb), s_recv=(2, nb),
        e_send=(nb,), e_recv=(nb,), od_send=(nb, 2, tps), od_recv=(nb, 2, tps),
        dd_send=(nb, 2, tps), dd_recv=(nb, 2, tps), t_send=(2, nb, tps), t_recv=(2, nb, tps),
        f_send=(4, 10), f_recv=(4, 10), y_send=(8,), y_recv=(8,), q_send=(tps,), q_recv=(tps,),
        b_send=(tps,), b_recv=(tps,), v_send=(tps,), v_recv=(tps,), loc=(9,), load=(3, 2), outs=(16,),
    )
    names = IN + list(outs) + list(vmem) + list(sems)
    hbm = pl.BlockSpec(memory_space=pl.ANY)
    whole_vmem = pl.BlockSpec(memory_space=pltpu.VMEM)
    got = pl.pallas_call(
        functools.partial(layer_kernel, dims, names),
        in_specs=[pl.BlockSpec(memory_space=pltpu.SMEM)] + [hbm] * 7 + [whole_vmem] * (len(IN) - 8),
        out_specs=[whole_vmem if k in SMALL else hbm for k in outs],
        out_shape=[sds(*v) for v in outs.values()],
        scratch_shapes=[pltpu.VMEM(*v) for v in vmem.values()]
        + [pltpu.SemaphoreType.DMA(v) for v in sems.values()],
        compiler_params=pltpu.CompilerParams(
            collective_id=0, has_side_effects=True, vmem_limit_bytes=63 << 20
        ),
        name="layer",
    )(*args)
    return dict(zip(outs, got))


def shift(arr, axis, by):
    peers = lax.axis_size(axis)
    pairs = [(i, i + by) for i in range(peers) if 0 <= i + by < peers]
    return lax.ppermute(arr, axis, pairs)


def heads_row(vec, width=LANES):
    return jnp.pad(vec[None], ((0, 0), (0, width - vec.shape[0])))


def on_device(
    x_in,
    cotangent,
    offsets,
    in_gain,
    w_z,
    w_x,
    w_dt,
    w_bc,
    conv_w,
    conv_b,
    dt_bias,
    a_log,
    d_skip,
    norm_gain,
    w_out,
):
    batches, seq_count, length, width_dev = x_in.shape
    nb = batches * seq_count
    tokens = nb * length
    tp_rank = lax.axis_index("tp")
    ctx_rank = lax.axis_index("ctx")
    peers = lax.axis_size("ctx")
    inner = w_z.shape[1]
    heads = w_dt.shape[1]
    width = inner // heads
    model = in_gain.shape[0]
    inner_all = norm_gain.shape[0]
    pair = conv_w.shape[1] - inner_all
    n = pair // 2
    taps = conv_w.shape[0]

    def mine(arr, size, axis):
        return lax.dynamic_slice_in_dim(arr, tp_rank * size, size, axis)

    cw = jnp.concatenate([mine(conv_w, inner, 1), conv_w[:, inner_all:]], axis=1)
    cb = jnp.concatenate([mine(conv_b, inner, 0), conv_b[inner_all:]])[None]
    gain = mine(norm_gain, inner, 0)[None]
    gain_in = mine(in_gain, width_dev, 0)
    dtb = heads_row(mine(dt_bias, heads, 0))
    rate = heads_row(-jnp.exp(mine(a_log, heads, 0)))
    dsk = jnp.repeat(mine(d_skip, heads, 0), width)[None]
    pos = (ctx_rank * length).astype(jnp.int32)[None]
    offs = offsets.reshape(nb, offsets.shape[-1])

    x_own = x_in.reshape(tokens, width_dev)
    cot_own = cotangent.reshape(tokens, width_dev)
    tps = lax.axis_size("tp")
    def chained(start, lend, by):
        came = jnp.zeros_like(start)
        for k in range(peers - 1):
            sent = start if k == 0 else start + lend * came
            came = shift(sent.astype(BF16), "ctx", by).astype(F32)
        return came

    def ending(lead):
        return jnp.repeat(lead[:, length - 1, :heads], width, axis=-1)[:, None]

    if peers == 2 and lax.axis_size("fsdp") == 4 and nb == 2 and heads % 16 == 0:
        got = layer(
            (offs, x_own, cot_own, w_x, w_z, w_out, w_bc.T, w_dt.T, in_gain[None], conv_w, conv_b[None],
             dt_bias[None], a_log[None], d_skip[None], norm_gain[None]),
            nb, length, heads, width, n, tps, inner_all,
        )
        h = x_own.astype(F32)
        out = h + got["stat"][:, 0:1] * got["out"].astype(F32)
        r1, in_dot = got["stat2"][:, 0:1], got["stat2"][:, 1:2]
        share = r1 * gain_in * got["dx"].astype(F32)
        d_x = cot_own.astype(F32) + share - h * (r1 * r1 * in_dot / model)
        shape = (batches, seq_count, length, width_dev)
        return (
            out.reshape(shape),
            d_x.reshape(shape),
            got["g_ig"][0],
            got["gz"].astype(F32),
            got["gx"].astype(F32),
            got["gdt"].T,
            got["gbc"].T,
            got["g_cw"],
            got["g_cb"][0],
            got["g_db"][0],
            got["g_al"][0],
            got["g_ds"][0],
            got["g_ng"][0],
            got["go"].astype(F32).T,
        )
    small = jnp.concatenate([w_bc, w_dt], axis=1)
    small = lax.all_gather(small, "fsdp", axis=0, tiled=True)
    wdt = jnp.pad(small[:, pair // tps :], ((0, 0), (0, LANES - heads)))
    wbc = lax.all_gather(small[:, : pair // tps], "tp", axis=1, tiled=True)

    x_all = lax.all_gather(x_own, "tp", axis=1, tiled=True)
    wx = lax.all_gather(w_x, "fsdp", axis=0, tiled=True)
    wz = lax.all_gather(w_z, "fsdp", axis=0, tiled=True)
    wo = lax.all_gather(w_out, "fsdp", axis=1, tiled=True)
    cot_all = lax.all_gather(cot_own, "tp", axis=1, tiled=True)
    resid = x_all.astype(F32)
    r1 = lax.rsqrt(jnp.mean(resid * resid, axis=1, keepdims=True) + EPSILON)
    xn = (resid * r1 * in_gain).astype(BF16)
    pre = jnp.concatenate([mm(xn, wx).astype(BF16), mm(xn, wbc).astype(BF16)], axis=1)
    pre = pre.reshape(nb, length, inner + pair)
    dtr = mm(xn, wdt).reshape(nb, length, LANES)
    z = mm(xn, wz).reshape(nb, length, inner)
    rim = shift(pre[:, length - 8 :], "ctx", 1).astype(F32)
    y, rd, lead, st, lead0, fin = scan_forward(
        offs, pos, pre, rim, dtr, cw, cb, dtb, rate, dsk, width, n
    )
    s_in = chained(fin, ending(lead), 1)
    y, ygg, sq, st = gate_forward(y, rd, lead, lead0, st, s_in, z, gain, width)
    part = mm(ygg.reshape(tokens, inner), wo).astype(BF16)
    lend = ending(lead)
    share = lax.psum_scatter(part, "tp", scatter_dimension=1, tiled=True)
    dyn = mm(cot_all, wo, NT).reshape(nb, length, inner)
    dot = jnp.sum(dyn * gain * y * jax.nn.silu(z), axis=2)
    stat = jnp.stack([sq[..., 0], dot])
    stat = jnp.sum(lax.all_gather(stat, "tp"), axis=0)
    r2 = lax.rsqrt(stat[0] / inner_all + EPSILON)
    out = x_own.astype(F32) + r2.reshape(tokens, 1) * share.astype(F32)
    stat = jnp.pad(jnp.stack([r2, stat[1]], axis=-1), ((0, 0), (0, 0), (0, LANES - 2)))
    dy, dz, yn, g_gain, g_state = gate_backward(dyn, y, z, stat, gain, rd, lead, width, inner_all)
    dz = dz.reshape(tokens, inner)
    yn = yn.reshape(tokens, inner)
    d_in = chained(g_state, lend, -1)
    rows = ("ctx", "fsdp")

    def scattered(grad):
        return lax.psum_scatter(grad.astype(BF16), rows, scatter_dimension=0, tiled=True)

    g_out = scattered(mm(cot_all, yn, TN)).astype(F32).T
    g_z = scattered(mm(xn, dz, TN)).astype(F32)
    dcat, ddt, edge, rim_grad, acc, acc_head = scan_backward(
        offs, pos, pre, rim, dtr, y, dy, st, d_in, cw, cb, dtb, rate, dsk, width
    )
    edge = (edge + shift(rim_grad, "ctx", -1)).astype(BF16)
    dcat = lax.dynamic_update_slice(dcat, edge, (0, length - 8, 0)).reshape(tokens, inner + pair)
    ddt = ddt.reshape(tokens, LANES)
    dxn = mm(dz, wz, NT) + mm(dcat[:, :inner], wx, NT) + mm(dcat[:, inner:], wbc, NT) + mm(ddt, wdt, NT)
    dxn = lax.psum_scatter(dxn.astype(BF16), "tp", scatter_dimension=1, tiled=True).astype(F32)
    g_xbc = scattered(jnp.concatenate([mm(xn, dcat, TN), mm(xn, ddt, TN)[:, :heads]], axis=1))
    g_x = g_xbc[:, :inner].astype(F32)
    g_dt = g_xbc[:, inner + pair :].astype(F32)
    g_bc = lax.psum_scatter(
        g_xbc[:, inner : inner + pair].astype(F32), "tp", scatter_dimension=1, tiled=True
    )
    h_own = x_own.astype(F32)
    scaled = dxn * gain_in
    in_dot = jnp.sum(lax.all_gather(jnp.sum(scaled * h_own, axis=1), "tp"), axis=0)[:, None]
    g_in = jnp.sum(dxn * h_own * r1, axis=0)
    d_x = cot_own.astype(F32) + r1 * scaled - h_own * r1**3 * in_dot / model
    pieces = [
        g_in,
        acc[:taps, :inner].reshape(-1),
        acc[taps, :inner],
        g_gain[0],
        acc_head[1, :heads],
        acc_head[0, :heads],
        acc[taps + 1, :inner].reshape(heads, width).sum(axis=1),
        acc[:taps, inner:].reshape(-1),
        acc[taps, inner:],
    ]
    sizes = [p.shape[0] for p in pieces]
    packed = jnp.sum(lax.all_gather(jnp.concatenate(pieces), rows), axis=0)
    packed = lax.all_gather(packed, "tp")
    parts, start = [], 0
    for size in sizes:
        parts.append(packed[:, start : start + size])
        start += size
    tp = packed.shape[0]
    g_cw = jnp.concatenate(
        [
            parts[1].reshape(tp, taps, inner).transpose(1, 0, 2).reshape(taps, inner_all),
            jnp.sum(parts[7], axis=0).reshape(taps, pair),
        ],
        axis=1,
    )
    g_cb = jnp.concatenate([parts[2].reshape(-1), jnp.sum(parts[8], axis=0)])
    shape = (batches, seq_count, length, width_dev)
    return (
        out.reshape(shape),
        d_x.reshape(shape),
        parts[0].reshape(-1),
        g_z,
        g_x,
        g_dt,
        g_bc,
        g_cw,
        g_cb,
        parts[4].reshape(-1),
        parts[5].reshape(-1),
        parts[6].reshape(-1),
        parts[3].reshape(-1),
        g_out,
    )


def solution(mesh):
    stream = P(None, "fsdp", "ctx", "tp")
    weight = P("fsdp", "tp")
    grad = P(("ctx", "fsdp"), "tp")
    in_specs = (
        (stream, stream, P(None, "fsdp", None), P())
        + (weight,) * 4
        + (P(),) * 6
        + (P("tp", "fsdp"),)
    )
    out_specs = (
        (stream, stream, P()) + (grad,) * 4 + (P(),) * 6 + (P("tp", ("ctx", "fsdp")),)
    )
    return jax.shard_map(
        on_device, mesh=mesh, in_specs=in_specs, out_specs=out_specs, check_vma=False
    )
```

```python
import functools
import types

import jax
import jax.numpy as jnp
from jax import lax
from jax.experimental import pallas as pl
from jax.experimental.pallas import tpu as pltpu
from jax.sharding import PartitionSpec as P

EPSILON = 1e-05
PRECISE = lax.Precision.HIGHEST
LANES = 128
CHUNK = 128
FAR = -1e30
F32 = jnp.float32
BF16 = jnp.bfloat16


def mm(a, b, dims=((1,), (0,)), precision=None):
    return lax.dot_general(a, b, (dims, ((), ())), precision=precision, preferred_element_type=F32)


NN = ((1,), (0,))
NT = ((1,), (1,))
TN = ((0,), (0,))


def softplus(v):
    return jnp.maximum(v, 0.0) + jnp.log1p(jnp.exp(-jnp.abs(v)))


def head_sums(v, head_of):
    high = v.astype(BF16)
    low = (v - high.astype(F32)).astype(BF16)
    return mm(high, head_of) + mm(low, head_of)


def silu_slope(v, sig):
    return sig * (1.0 + v * (1.0 - sig))


def doc_of(off_ref, seq, pos):
    count = jnp.zeros_like(pos)
    for j in range(off_ref.shape[1]):
        count = count + (off_ref[seq, j] <= pos).astype(jnp.int32)
    return count


def widen(cols, head, lane, width):
    out = cols[:, head : head + 1]
    for i in range(1, LANES // width):
        out = jnp.where(lane >= i * width, cols[:, head + i : head + i + 1], out)
    return jnp.broadcast_to(out, (cols.shape[0], LANES))


class Span:
    def __init__(self, off_ref, first, seq, start, q, dtr, dtb, rate, taps):
        at = first + start
        col = at + lax.broadcasted_iota(jnp.int32, (q, 1), 0)
        row = at + lax.broadcasted_iota(jnp.int32, (1, q), 1)
        dcol = doc_of(off_ref, seq, col)
        drow = doc_of(off_ref, seq, row)
        before = doc_of(off_ref, seq, at - 1)
        before_dev = doc_of(off_ref, seq, first - 1)
        last = doc_of(off_ref, seq, at + q - 1)
        self.match = [
            (doc_of(off_ref, seq, col - (taps - 1 - k)) == dcol).astype(F32) for k in range(taps - 1)
        ]
        self.far = jnp.where((dcol == drow) & (col >= row), 0.0, FAR)
        self.kept = (dcol == before).astype(F32)
        self.kept_dev = (dcol == before_dev).astype(F32)
        self.carry_dev = (before == before_dev).astype(F32)
        self.dt_in = dtr + dtb
        self.dt = softplus(self.dt_in)
        decay = self.dt * rate
        tri = (
            lax.broadcasted_iota(jnp.int32, (q, q), 0) >= lax.broadcasted_iota(jnp.int32, (q, q), 1)
        ).astype(F32)
        self.tri = tri
        self.cum = mm(tri, decay, precision=PRECISE)
        self.cum_t = self.cum.T
        self.lead = jnp.exp(self.cum) * self.kept
        end = self.cum[q - 1 : q, :]
        self.tail = jnp.exp(end - self.cum) * (dcol == last).astype(F32)
        self.end = end

    def fade(self, head):
        return jnp.exp(self.cum[:, head : head + 1] - self.cum_t[head : head + 1, :] + self.far)


def conv_block(pre, halo, cw, cb, match):
    taps = len(match) + 1
    ext = jnp.concatenate([halo, pre], axis=0)
    shifted = [
        pltpu.roll(ext, taps - 1 - k, 0)[8:] * match[k] for k in range(taps - 1)
    ] + [pre]
    conv = cb
    for k in range(taps):
        conv = conv + cw[k : k + 1] * shifted[k]
    return conv, shifted


def scan_kernel(dims, off, pos, *refs):
    scan_chunk(dims, pl.program_id(0), pl.program_id(1), off, pos[0], *refs)


def scan_chunk(dims, b, c, off, first, pre, rim, dtr, cw, cb, dtb, rate, dsk, y, rd, lead, st, lead0, fin, halo, state, run):
    q, inner, width, n = dims

    @pl.when(c == 0)
    def _():
        halo[...] = rim[0]
        state[...] = jnp.zeros_like(state)
        run[...] = jnp.zeros_like(run)

    taps = cw.shape[0]
    sp = Span(off, first, b, c * q, q, dtr[0], dtb[...], rate[...], taps)
    total = run[...] + sp.cum
    lead[0] = jnp.exp(total) * sp.kept_dev
    lead0[0, 0] = jnp.broadcast_to(jnp.exp(run[...]) * sp.carry_dev, (8, LANES))
    run[...] = total[q - 1 : q]

    def act(lo, hi):
        conv, _ = conv_block(
            pre[0, :, lo:hi].astype(F32), halo[:, lo:hi], cw[:, lo:hi], cb[:, lo:hi], sp.match
        )
        return conv * jax.nn.sigmoid(conv)

    write = act(inner, inner + n).astype(BF16)
    read = act(inner + n, inner + 2 * n).astype(BF16)
    rd[0] = read
    scores = mm(read, write, NT)
    write_t = write.astype(F32).T.astype(BF16)
    lane = lax.broadcasted_iota(jnp.int32, (1, LANES), 1)
    per = LANES // width
    for j in range(inner // LANES):
        lo, hi = j * LANES, (j + 1) * LANES
        h = j * per
        xs = act(lo, hi)
        xdt = xs * widen(sp.dt, h, lane, width)
        xdt_low = xdt.astype(BF16)
        mixed = None
        for i in range(per):
            part = mm((sp.fade(h + i) * scores).astype(BF16), xdt_low)
            mixed = part if mixed is None else jnp.where(lane >= i * width, part, mixed)
        old = state[:, lo:hi]
        st[0, 0, :, lo:hi] = old.astype(st.dtype)
        mixed = mixed + widen(sp.lead, h, lane, width) * mm(read, old.astype(BF16))
        y[0, :, lo:hi] = mixed + dsk[:, lo:hi] * xs
        fresh = mm(write_t, (xdt * widen(sp.tail, h, lane, width)).astype(BF16))
        new = widen(sp.lead[q - 1 : q], h, lane, width) * old + fresh
        state[:, lo:hi] = new
        fin[0, :, lo:hi] = new
    halo[...] = pre[0, q - 8 : q].astype(F32)


def gate_kernel(dims, y_in, rd, lead, lead0, st, s_in, z, gain, y, ygg, sq, st_full):
    q, inner, width, n = dims
    lane = lax.broadcasted_iota(jnp.int32, (1, LANES), 1)
    per = LANES // width
    total = jnp.zeros((q, LANES), F32)
    for j in range(inner // LANES):
        lo, hi = j * LANES, (j + 1) * LANES
        h = j * per
        came = s_in[0, :, lo:hi].astype(F32)
        full = st[0, 0, :, lo:hi].astype(F32) + widen(lead0[0, 0, 0:1], h, lane, width) * came
        st_full[0, 0, :, lo:hi] = full.astype(st_full.dtype)
        val = y_in[0, :, lo:hi] + widen(lead[0], h, lane, width) * mm(rd[0], came.astype(BF16))
        y[0, :, lo:hi] = val
        gate = z[0, :, lo:hi]
        gated = val * gate * jax.nn.sigmoid(gate)
        total = total + gated * gated
        ygg[0, :, lo:hi] = (gated * gain[:, lo:hi]).astype(BF16)
    sq[0] = jnp.broadcast_to(jnp.sum(total, axis=1, keepdims=True), (q, LANES))


def ungate_kernel(dims, count, dyn, y, z, stat, gain, rd, lead, dy, dz, yn, g_gain, g_state):
    b, c = pl.program_id(0), pl.program_id(1)

    @pl.when((b == 0) & (c == 0))
    def _():
        g_gain[...] = jnp.zeros_like(g_gain)

    @pl.when(c == 0)
    def _():
        g_state[...] = jnp.zeros_like(g_state)

    ungate_chunk(dims, count, dyn, y, z, stat, gain, rd, lead, dy, dz, yn, g_gain, g_state)


def ungate_chunk(dims, count, dyn, y, z, stat, gain, rd, lead, dy, dz, yn, g_gain, g_state):
    q, inner, width, n = dims
    lane = lax.broadcasted_iota(jnp.int32, (1, LANES), 1)
    per = LANES // width
    r2 = stat[0, :, 0:1]
    coef = r2 * r2 * r2 * stat[0, :, 1:2] * (1.0 / count)
    read_t = rd[0].astype(F32).T.astype(BF16)
    for j in range(inner // LANES):
        lo, hi = j * LANES, (j + 1) * LANES
        h = j * per
        gate = z[0, :, lo:hi]
        sig = jax.nn.sigmoid(gate)
        act = gate * sig
        val = y[0, :, lo:hi]
        gated = val * act
        dn = dyn[0, :, lo:hi]
        g = gain[:, lo:hi]
        norm = gated * r2
        g_gain[0:1, lo:hi] += jnp.sum(dn * norm, axis=0, keepdims=True)
        yn[0, :, lo:hi] = (norm * g).astype(BF16)
        d_gated = r2 * (dn * g) - gated * coef
        d_core = d_gated * act
        dy[0, :, lo:hi] = d_core
        dz[0, :, lo:hi] = (d_gated * val * silu_slope(gate, sig)).astype(BF16)
        g_state[0, :, lo:hi] += mm(read_t, (d_core * widen(lead[0], h, lane, width)).astype(BF16))


def back_kernel(dims, off, pos, pre, prev, rim, dtr, y, dy, st, d_in, *refs):
    acc, acc_head, d_state, carry = refs[-4:]
    b, c = pl.program_id(0), pl.program_id(1)
    at = pl.num_programs(1) - 1 - c

    @pl.when((b == 0) & (c == 0))
    def _():
        acc[...] = jnp.zeros_like(acc)
        acc_head[...] = jnp.zeros_like(acc_head)

    @pl.when(c == 0)
    def _():
        d_state[...] = d_in[0]
        carry[...] = jnp.zeros_like(carry)

    back_chunk(dims, b, at, c == 0, off, pos[0], pre, prev, rim, dtr, y, dy, st, *refs)


def back_chunk(dims, b, at, newest, off, first, pre, prev, rim, dtr, y, dy, st, cw, cb, dtb, rate, dsk,
               dcat, ddt_out, edge, rim_grad, acc, acc_head, d_state, carry):
    q, inner, width, n = dims
    taps = cw.shape[0]
    sp = Span(off, first, b, at * q, q, dtr[0], dtb[...], rate[...], taps)
    lane = lax.broadcasted_iota(jnp.int32, (1, LANES), 1)
    per = LANES // width

    def conv(lo, hi):
        ahead = jnp.where(at == 0, rim[0, :, lo:hi], prev[0, 8:16, lo:hi].astype(F32))
        return conv_block(pre[0, :, lo:hi].astype(F32), ahead, cw[:, lo:hi], cb[:, lo:hi], sp.match)

    def unconv(lo, hi, d_act, out, shifted, sig):
        d_conv = d_act * silu_slope(out, sig)
        acc[taps : taps + 1, lo:hi] += jnp.sum(d_conv, axis=0, keepdims=True)
        d_ext = None
        zeros = jnp.zeros((8, hi - lo), F32)
        for k in range(taps):
            acc[k : k + 1, lo:hi] += jnp.sum(d_conv * shifted[k], axis=0, keepdims=True)
            masked = cw[k : k + 1, lo:hi] * d_conv
            if k < taps - 1:
                masked = masked * sp.match[k]
            part = jnp.concatenate([zeros, masked], axis=0)
            if k < taps - 1:
                part = pltpu.roll(part, q + 8 - (taps - 1 - k), 0)
            d_ext = part if d_ext is None else d_ext + part
        d_pre = jnp.concatenate([d_ext[8:q], d_ext[q:] + carry[:, lo:hi]], axis=0)
        carry[:, lo:hi] = d_ext[0:8]
        rim_grad[0, :, lo:hi] = d_ext[0:8]
        dcat[0, :, lo:hi] = d_pre.astype(BF16)

        @pl.when(newest)
        def _():
            edge[0, :, lo:hi] = d_pre[q - 8 : q]

    w_conv, w_shift = conv(inner, inner + n)
    w_sig = jax.nn.sigmoid(w_conv)
    write = (w_conv * w_sig).astype(BF16)
    r_conv, r_shift = conv(inner + n, inner + 2 * n)
    r_sig = jax.nn.sigmoid(r_conv)
    read = (r_conv * r_sig).astype(BF16)
    scores = mm(read, write, NT)
    read_t = read.astype(F32).T.astype(BF16)
    d_scores = jnp.zeros((q, q), F32)
    d_write = jnp.zeros((q, n), F32)
    d_read = jnp.zeros((q, n), F32)
    d_cum = jnp.zeros((q, LANES), F32)
    d_step = jnp.zeros((q, LANES), F32)
    d_end = jnp.zeros((8, LANES), F32)
    for j in range(inner // LANES):
        lo, hi = j * LANES, (j + 1) * LANES
        h = j * per
        x_conv, x_shift = conv(lo, hi)
        x_sig = jax.nn.sigmoid(x_conv)
        xs = x_conv * x_sig
        step = widen(sp.dt, h, lane, width)
        xdt = xs * step
        xdt_low = xdt.astype(BF16)
        grad = dy[0, :, lo:hi]
        grad_low = grad.astype(BF16)
        core = y[0, :, lo:hi] - dsk[:, lo:hi] * xs
        late = d_state[:, lo:hi]
        late_low = late.astype(BF16)
        early = st[0, 0, :, lo:hi].astype(F32)
        tail = widen(sp.tail, h, lane, width)
        lead = widen(sp.lead, h, lane, width)
        u = None
        for i in range(per):
            fade = sp.fade(h + i)
            here = (lane >= i * width) & (lane < (i + 1) * width)
            own = jnp.where(here, grad, 0.0).astype(BF16)
            d_scores = d_scores + mm(own, xdt_low, NT) * fade
            part = mm((fade * scores).astype(BF16), grad_low, TN)
            u = part if u is None else jnp.where(lane >= i * width, part, u)
        from_end = tail * mm(write, late_low)
        inside = u
        u = u + from_end
        weighted = (lead * grad).astype(BF16)
        d_read = d_read + mm(weighted, early.astype(BF16), NT)
        d_write = d_write + mm((xdt * tail).astype(BF16), late_low, NT)
        end_lead = widen(sp.lead[q - 1 : q], h, lane, width)
        d_state[:, lo:hi] = end_lead * late + mm(read_t, weighted)
        head_of = (
            lax.broadcasted_iota(jnp.int32, (LANES, LANES), 0) // width + h
            == lax.broadcasted_iota(jnp.int32, (LANES, LANES), 1)
        ).astype(BF16)
        d_cum = d_cum + head_sums(
            grad_low.astype(F32) * core - xdt_low.astype(F32) * inside - xdt * from_end, head_of
        )
        d_step = d_step + head_sums(xs * u, head_of)
        end_row = end_lead * jnp.sum(late * early, axis=0, keepdims=True) + jnp.sum(
            xdt * from_end, axis=0, keepdims=True
        )
        d_end = d_end + head_sums(jnp.broadcast_to(end_row, (8, LANES)), head_of)
        acc[taps + 1 : taps + 2, lo:hi] += jnp.sum(grad * xs, axis=0, keepdims=True)
        unconv(lo, hi, step * u + dsk[:, lo:hi] * grad, x_conv, x_shift, x_sig)
    d_low = d_scores.astype(BF16)
    d_read = d_read + mm(d_low, write)
    d_write = d_write + mm(d_low, read, TN)
    unconv(inner, inner + n, d_write, w_conv, w_shift, w_sig)
    unconv(inner + n, inner + 2 * n, d_read, r_conv, r_shift, r_sig)
    d_decay = mm(sp.tri, d_cum, TN, precision=PRECISE) + d_end[0:1]
    acc_head[0:1] += jnp.sum(d_decay * sp.dt, axis=0, keepdims=True) * rate[...]
    d_dt = (d_step + d_decay * rate[...]) * jax.nn.sigmoid(sp.dt_in)
    acc_head[1:2] += jnp.sum(d_dt, axis=0, keepdims=True)
    ddt_out[0] = d_dt.astype(BF16)


def whole(shape):
    return pl.BlockSpec(shape, lambda *_: (0,) * len(shape))


def params():
    return pltpu.CompilerParams(vmem_limit_bytes=48 << 20)


def scan_forward(offs, pos, pre, rim, dtr, cw, cb, dtb, rate, dsk, width, n):
    nb, length, chans = pre.shape
    inner = dsk.shape[1]
    q = min(CHUNK, length)
    chunks = length // q
    dims = (q, inner, width, n)

    def rows(size):
        return pl.BlockSpec((1, q, size), lambda b, c, *_: (b, c, 0))

    return pl.pallas_call(
        functools.partial(scan_kernel, dims),
        grid_spec=pltpu.PrefetchScalarGridSpec(
            num_scalar_prefetch=2,
            grid=(nb, chunks),
            in_specs=[
                rows(chans),
                pl.BlockSpec((1, 8, chans), lambda b, c, *_: (b, 0, 0)),
                rows(LANES),
                whole(cw.shape),
                whole(cb.shape),
                whole(dtb.shape),
                whole(rate.shape),
                whole(dsk.shape),
            ],
            out_specs=[
                rows(inner),
                rows(n),
                rows(LANES),
                pl.BlockSpec((1, 1, n, inner), lambda b, c, *_: (b, c, 0, 0)),
                pl.BlockSpec((1, 1, 8, LANES), lambda b, c, *_: (b, c, 0, 0)),
                pl.BlockSpec((1, n, inner), lambda b, c, *_: (b, 0, 0)),
            ],
            scratch_shapes=[
                pltpu.VMEM((8, chans), F32),
                pltpu.VMEM((n, inner), F32),
                pltpu.VMEM((1, LANES), F32),
            ],
        ),
        out_shape=[
            jax.ShapeDtypeStruct((nb, length, inner), F32),
            jax.ShapeDtypeStruct((nb, length, n), BF16),
            jax.ShapeDtypeStruct((nb, length, LANES), F32),
            jax.ShapeDtypeStruct((nb, chunks, n, inner), F32),
            jax.ShapeDtypeStruct((nb, chunks, 8, LANES), F32),
            jax.ShapeDtypeStruct((nb, n, inner), F32),
        ],
        compiler_params=params(),
        name="scan_forward",
    )(offs, pos, pre, rim, dtr, cw, cb, dtb, rate, dsk)


def gate_forward(y_in, rd, lead, lead0, st, s_in, z, gain, width):
    nb, length, inner = y_in.shape
    chunks, n = st.shape[1], st.shape[2]
    q = length // chunks
    dims = (q, inner, width, n)

    def rows(size):
        return pl.BlockSpec((1, q, size), lambda b, c: (b, c, 0))

    def per_chunk(r, size):
        return pl.BlockSpec((1, 1, r, size), lambda b, c: (b, c, 0, 0))

    return pl.pallas_call(
        functools.partial(gate_kernel, dims),
        grid=(nb, chunks),
        in_specs=[
            rows(inner),
            rows(n),
            rows(LANES),
            per_chunk(8, LANES),
            per_chunk(n, inner),
            pl.BlockSpec((1, n, inner), lambda b, c: (b, 0, 0)),
            rows(inner),
            whole(gain.shape),
        ],
        out_specs=[rows(inner), rows(inner), rows(LANES), per_chunk(n, inner)],
        out_shape=[
            jax.ShapeDtypeStruct((nb, length, inner), F32),
            jax.ShapeDtypeStruct((nb, length, inner), BF16),
            jax.ShapeDtypeStruct((nb, length, LANES), F32),
            jax.ShapeDtypeStruct(st.shape, F32),
        ],
        compiler_params=params(),
        name="gate_forward",
    )(y_in, rd, lead, lead0, st, s_in, z, gain)


def gate_backward(dyn, y, z, stat, gain, rd, lead, width, count):
    nb, length, inner = y.shape
    n = rd.shape[2]
    q = min(CHUNK, length)
    chunks = length // q
    dims = (q, inner, width, n)

    def rows(size):
        return pl.BlockSpec((1, q, size), lambda b, c: (b, c, 0))

    return pl.pallas_call(
        functools.partial(ungate_kernel, dims, count),
        grid=(nb, chunks),
        in_specs=[
            rows(inner),
            rows(inner),
            rows(inner),
            rows(LANES),
            whole(gain.shape),
            rows(n),
            rows(LANES),
        ],
        out_specs=[
            rows(inner),
            rows(inner),
            rows(inner),
            whole((8, inner)),
            pl.BlockSpec((1, n, inner), lambda b, c: (b, 0, 0)),
        ],
        out_shape=[
            jax.ShapeDtypeStruct((nb, length, inner), F32),
            jax.ShapeDtypeStruct((nb, length, inner), BF16),
            jax.ShapeDtypeStruct((nb, length, inner), BF16),
            jax.ShapeDtypeStruct((8, inner), F32),
            jax.ShapeDtypeStruct((nb, n, inner), F32),
        ],
        compiler_params=params(),
        name="gate_backward",
    )(dyn, y, z, stat, gain, rd, lead)


def scan_backward(offs, pos, pre, rim, dtr, y, dy, st, d_in, cw, cb, dtb, rate, dsk, width):
    nb, length, chans = pre.shape
    inner = dsk.shape[1]
    chunks, n = st.shape[1], st.shape[2]
    q = length // chunks
    dims = (q, inner, width, n)
    per = q // 16

    def rows(size):
        return pl.BlockSpec((1, q, size), lambda b, c, *_: (b, chunks - 1 - c, 0))

    def per_seq(r, size):
        return pl.BlockSpec((1, r, size), lambda b, c, *_: (b, 0, 0))

    return pl.pallas_call(
        functools.partial(back_kernel, dims),
        grid_spec=pltpu.PrefetchScalarGridSpec(
            num_scalar_prefetch=2,
            grid=(nb, chunks),
            in_specs=[
                rows(chans),
                pl.BlockSpec(
                    (1, 16, chans), lambda b, c, *_: (b, jnp.maximum((chunks - 1 - c) * per - 1, 0), 0)
                ),
                per_seq(8, chans),
                rows(LANES),
                rows(inner),
                rows(inner),
                pl.BlockSpec((1, 1, n, inner), lambda b, c, *_: (b, chunks - 1 - c, 0, 0)),
                per_seq(n, inner),
                whole(cw.shape),
                whole(cb.shape),
                whole(dtb.shape),
                whole(rate.shape),
                whole(dsk.shape),
            ],
            out_specs=[
                rows(chans),
                rows(LANES),
                per_seq(8, chans),
                per_seq(8, chans),
                whole((8, chans)),
                whole((8, LANES)),
            ],
            scratch_shapes=[pltpu.VMEM((n, inner), F32), pltpu.VMEM((8, chans), F32)],
        ),
        out_shape=[
            jax.ShapeDtypeStruct((nb, length, chans), BF16),
            jax.ShapeDtypeStruct((nb, length, LANES), BF16),
            jax.ShapeDtypeStruct((nb, 8, chans), F32),
            jax.ShapeDtypeStruct((nb, 8, chans), F32),
            jax.ShapeDtypeStruct((8, chans), F32),
            jax.ShapeDtypeStruct((8, LANES), F32),
        ],
        compiler_params=params(),
        name="scan_backward",
    )(offs, pos, pre, pre, rim, dtr, y, dy, st, d_in, cw, cb, dtb, rate, dsk)


MESH = pl.DeviceIdType.MESH


def remote(src, dst, send, recv, **where):
    return pltpu.make_async_remote_copy(
        src_ref=src, dst_ref=dst, send_sem=send, recv_sem=recv, device_id=where, device_id_type=MESH
    )


class Line:
    def __init__(self, own, block, send, recv):
        self.own, self.block, self.send, self.recv = own, block, send, recv
        self.me = lax.axis_index("tp")
        self.peers = lax.axis_size("tp")

    def holds(self, k):
        for way, step in enumerate((1, -1)):
            slot = self.me - k * step
            held = (slot >= 0) & (slot < self.peers)
            yield held, way, jnp.clip(slot, 0, self.peers - 1)

    def parts(self, k):
        for held, way, slot in self.holds(k):
            there = self.me + (1, -1)[way]
            onward = held & (there >= 0) & (there < self.peers)
            here = self.own if k == 0 else self.block(slot)
            copy = remote(here, self.block(slot), self.send.at[way, k], self.recv.at[slot], tp=there)
            yield held, onward, copy

    def step(self, k):
        for held, onward, copy in self.parts(k):
            if k > 0:

                @pl.when(held)
                def _():
                    copy.wait_recv()

            @pl.when(onward)
            def _():
                copy.start()

    def finish(self):
        for k in range(self.peers - 1):
            for held, onward, copy in self.parts(k):

                @pl.when(onward)
                def _():
                    copy.wait_send()


def by_rows_of(size, total, body):
    @pl.loop(0, total // size)
    def _(i):
        body(pl.ds(pl.multiple_of(i * size, size), size))


def into_sum(mine, came):
    def body(rows):
        mine[rows, :] = (mine[rows, :].astype(F32) + came[rows, :].astype(F32)).astype(BF16)

    by_rows_of(32, mine.shape[0], body)


class Drain:
    def __init__(self, part, rows, wide, land, stage, send, recv, load):
        self.part, self.rows, self.wide, self.land, self.stage = part, rows, wide, land, stage
        self.send, self.recv, self.load = send, recv, load
        self.me = lax.axis_index("tp")
        self.peers = lax.axis_size("tp")

    def block(self, slot):
        return self.part.at[self.rows, pl.ds(pl.multiple_of(slot * self.wide, self.wide), self.wide)]

    def copy(self, way, slot):
        there = jnp.clip(self.me + (1, -1)[way], 0, self.peers - 1)
        return remote(
            self.block(slot), self.land.at[way, slot], self.send.at[way, slot], self.recv.at[way, slot], tp=there
        )

    def fetch(self, way, slot):
        return pltpu.make_async_copy(self.land.at[way, slot], self.stage.at[way], self.load.at[way])

    def add(self, way, slot):
        self.fetch(way, slot).wait()
        mine = self.block(slot)

        def body(rows):
            mine[rows, :] = (mine[rows, :].astype(F32) + self.stage[way, rows, :].astype(F32)).astype(BF16)

        by_rows_of(64, mine.shape[0], body)

    def ways(self, j):
        last = self.peers - 1
        for way, rank in ((0, self.me), (1, last - self.me)):
            behind = j - rank
            slot = last - behind if way == 0 else behind
            yield way, jnp.clip(slot, 0, last), behind >= 0, rank > 0

    def begin(self, way, slot, when):
        @pl.when(when)
        def _():
            self.copy(way, slot).wait_recv()
            self.fetch(way, slot).start()

    def source(self, j):
        for way, slot, sends, fed in self.ways(j):

            @pl.when(sends & jnp.logical_not(fed))
            def _():
                self.copy(way, slot).start()

    def relay(self, j):
        for way, slot, sends, fed in self.ways(j):
            self.begin(way, slot, sends & fed)
        for way, slot, sends, fed in self.ways(j):

            @pl.when(sends & fed)
            def _():
                self.add(way, slot)
                self.copy(way, slot).start()

    def round(self, j):
        self.source(j)
        self.relay(j)

    def close(self):
        fed = (self.me > 0, self.me < self.peers - 1)
        for way in range(2):
            self.begin(way, self.me, fed[way])
        for way in range(2):

            @pl.when(fed[way])
            def _():
                self.add(way, self.me)

    def finish(self):
        for j in range(self.peers - 1):
            for way, slot, sends, _ in self.ways(j):

                @pl.when(sends)
                def _():
                    self.copy(way, slot).wait_send()


class Fold:
    def __init__(self, theirs, block, land1, land2, land3, stage, half, send, recv, load):
        self.theirs, self.block, self.land1, self.land2, self.land3 = theirs, block, land1, land2, land3
        self.stage, self.half, self.send, self.recv, self.load = stage, half, send, recv, load
        self.ctx, self.fs = lax.axis_index("ctx"), lax.axis_index("fsdp")
        self.core, self.y = lax.rem(self.fs, 2), self.fs // 2

    def first(self, c, y):
        i = 2 * c + y
        mate = self.fs + 1 - 2 * self.core
        return remote(
            self.theirs(c, y), self.land1.at[i], self.send.at[i], self.recv.at[i], fsdp=mate
        )

    def part(self, ref, way):
        return ref.at[pl.ds(way * self.half, self.half)]

    def second(self, way, i):
        if way == 0:
            src, peer = self.block(i, 1 - self.y), {"fsdp": lax.rem(self.fs + 2, 4)}
        else:
            src, peer = self.block(1 - self.ctx, i), {"ctx": 1 - self.ctx}
        k = 4 + 2 * way + i
        return remote(self.part(src, way), self.land2.at[way, i], self.send.at[k], self.recv.at[k], **peer)

    def third(self, way):
        if way == 0:
            src, peer = self.block(1 - self.ctx, self.y), {"ctx": 1 - self.ctx}
        else:
            src, peer = self.block(self.ctx, 1 - self.y), {"fsdp": lax.rem(self.fs + 2, 4)}
        k = 8 + way
        return remote(self.part(src, way), self.land3.at[way], self.send.at[k], self.recv.at[k], **peer)

    def gather(self, parts):
        def fetch(i):
            _, land, mine = parts[i]
            stage = self.stage.at[i % 2, pl.ds(0, mine.shape[0]), pl.ds(0, mine.shape[1])]
            return pltpu.make_async_copy(land, stage, self.load.at[i % 2]), stage

        for i in range(len(parts) + 1):
            if i < len(parts):
                parts[i][0].wait_recv()
                fetch(i)[0].start()
            if i:
                copy, stage = fetch(i - 1)
                copy.wait()
                mine = parts[i - 1][2]
                into_sum(mine, stage)

    def one(self):
        self.gather(
            [
                (self.first(c, y), self.land1.at[2 * c + y], self.block(c, y))
                for c in range(2)
                for y in range(2)
            ]
        )
        for way in range(2):
            for i in range(2):
                self.second(way, i).start()

    def two(self):
        self.gather(
            [
                (self.second(0, i), self.land2.at[0, i], self.part(self.block(i, self.y), 0))
                for i in range(2)
            ]
            + [
                (self.second(1, i), self.land2.at[1, i], self.part(self.block(self.ctx, i), 1))
                for i in range(2)
            ]
        )
        for way in range(2):
            self.third(way).start()

    def three(self):
        own = self.block(self.ctx, self.y)
        self.gather([(self.third(way), self.land3.at[way], self.part(own, way)) for way in range(2)])
        return own

    def sent(self):
        for i in range(2):
            for y in range(2):
                self.first(i, y).wait_send()

    def finish(self):
        for i in range(2):
            self.second(0, i).wait_send()
            self.second(1, i).wait_send()
            self.third(i).wait_send()


IN = ["off", "x", "cot", "wx_in", "wz_in", "wo_in", "wbc_in", "wdt_in"]
IN += ["gain_in", "conv_w", "conv_b", "dt_bias", "a_log", "d_skip", "norm_gain"]


def layer_kernel(dims, names, *refs):
    r = types.SimpleNamespace(**dict(zip(names, refs)))
    nb, length, q, inner, width, n, d, inner_all, hpd = dims
    chunks = length // q
    tokens = nb * length
    chans = inner + 2 * n
    extra = 2 * n + LANES
    ctx, tp, fs = lax.axis_index("ctx"), lax.axis_index("tp"), lax.axis_index("fsdp")
    tps = lax.axis_size("tp")
    wide = d // tps
    deep = r.wx_in.shape[0]
    bd = d // 8
    core, yy = lax.rem(fs, 2), fs // 2
    mate = fs + 1 - 2 * core
    over = lax.rem(fs + 2, 4)
    other = 1 - ctx
    first = ctx * length
    small = (q, inner, width, n)
    dims_mode = (r.cw, r.cb, r.dtb, r.rate, r.dsk)

    def greet(**where):
        pl.semaphore_signal(barrier, inc=1, device_id=where, device_id_type=MESH)

    barrier = pltpu.get_barrier_semaphore()
    for step in range(1, tps):
        greet(tp=lax.rem(tp + step, tps))
    for c in range(2):
        for step in range(4):
            if c or step:
                greet(ctx=lax.rem(ctx + c, 2), fsdp=lax.rem(fs + step, 4))
    pl.semaphore_wait(barrier, tps - 1 + 7)

    def seq(m):
        return pl.ds(m * length, length)

    def one(ref, m):
        return ref.at[pl.ds(m, 1)]

    def span(ref, m, rows):
        return ref.at[pl.ds(m, 1), rows]

    def convolved(m, rows):
        return r.pre.at[pl.ds(m, 1), rows, pl.ds(0, chans)]

    def chunk_rows(c):
        return pl.ds(pl.multiple_of(c * q, q), q)

    mine = pl.ds(pl.multiple_of(tp * wide, wide), wide)
    own_pos = pl.ds(pl.multiple_of(fs * deep, deep), deep)
    rows_bc = r.wbc_in.shape[0]
    tight = 2 * n + hpd

    def features(ref, m):
        return lambda at: ref.at[seq(m), pl.ds(pl.multiple_of(at * wide, wide), wide)]

    def own(ref, m):
        return ref.at[seq(m)]

    x_lines = [Line(own(r.x, m), features(r.x_all, m), r.xs_send.at[m], r.xs_recv.at[m]) for m in range(nb)]
    c_lines = [Line(own(r.cot, m), features(r.cot_o, m), r.cs_send.at[m], r.cs_recv.at[m]) for m in range(nb)]
    bc_rows = pl.ds(pl.multiple_of(tp * rows_bc, rows_bc), rows_bc)

    def bc_in_copy(step):
        there = lax.rem(tp + step, tps)
        return remote(
            r.wbc_in, r.wst.at[bc_rows, own_pos], r.v_send.at[step], r.v_recv.at[tp], tp=there
        )

    def bc_in_recv(step):
        there = lax.rem(tp + step, tps)
        rows = pl.ds(pl.multiple_of(there * rows_bc, rows_bc), rows_bc)
        remote(
            r.wbc_in, r.wst.at[rows, own_pos], r.v_send.at[step], r.v_recv.at[there], tp=there
        ).wait_recv()

    def slot(w, at):
        rows = pl.ds(pl.multiple_of(at * deep, deep), deep)
        return (r.wx.at[rows], r.wz.at[rows], r.wo.at[:, rows], r.wst.at[pl.ds(0, tight), rows])[w]

    owns = (r.wx_in, r.wz_in, r.wo_in, slot(3, fs))

    def near(w):
        return remote(owns[w], slot(w, fs), r.w_send.at[w, 0], r.w_recv.at[w, fs], fsdp=mate)

    def far(w):
        return remote(owns[w], slot(w, fs), r.w_send.at[w, 1], r.w_recv.at[w, fs], fsdp=over)

    def relay(w):
        return remote(slot(w, over), slot(w, over), r.w_send.at[w, 2], r.w_recv.at[w, over], fsdp=mate)

    def arrive(w, at):
        remote(slot(w, at), slot(w, at), r.w_send.at[w, 0], r.w_recv.at[w, at], fsdp=mate).wait_recv()

    locals_ = [pltpu.make_async_copy(owns[w], slot(w, fs), r.loc.at[w]) for w in range(3)]
    locals_.append(pltpu.make_async_copy(r.x, r.x_all.at[:, mine], r.loc.at[3]))
    locals_.append(pltpu.make_async_copy(r.cot, r.cot_o.at[:, mine], r.loc.at[4]))
    locals_.append(pltpu.make_async_copy(r.wbc_in, r.wst.at[bc_rows, own_pos], r.loc.at[5 + nb]))
    locals_.append(pltpu.make_async_copy(r.wdt_in, r.wst.at[pl.ds(2 * n, hpd), own_pos], r.loc.at[6 + nb]))

    def pass_on(w):
        arrive(w, over)
        relay(w).start()

    def whole_weight(w):
        arrive(w, mate)
        arrive(w, lax.rem(mate + 2, 4))
        if w < 3:
            locals_[w].wait()

    def prepare():
        lane = lax.broadcasted_iota(jnp.int32, (8, LANES), 1)
        chan = pl.ds(pl.multiple_of(tp * inner, inner), inner)
        r.cw[:, :inner] = r.conv_w[:, chan]
        r.cw[:, inner:] = r.conv_w[:, inner_all:]
        r.cb[:, :inner] = r.conv_b[:, chan]
        r.cb[:, inner:] = r.conv_b[:, inner_all:]
        r.gain[...] = r.norm_gain[:, chan]

        def own_heads(ref):
            wide_row = jnp.concatenate([ref[...], jnp.zeros((1, LANES - ref.shape[1]), F32)], axis=1)
            turned = pltpu.roll(jnp.broadcast_to(wide_row, (8, LANES)), lax.rem(LANES - tp * hpd, LANES), 1)
            return jnp.where(lane < hpd, turned, 0.0)

        r.dtb[...] = own_heads(r.dt_bias)[0:1]
        r.rate[...] = jnp.where(lane < hpd, -jnp.exp(own_heads(r.a_log)), 0.0)[0:1]
        head_of = (
            lax.broadcasted_iota(jnp.int32, (LANES, inner), 0)
            == lax.broadcasted_iota(jnp.int32, (LANES, inner), 1) // width
        ).astype(F32)
        r.dsk[...] = mm(own_heads(r.d_skip), head_of, precision=PRECISE)[0:1]
        r.wst[tight:, :] = jnp.zeros((LANES - hpd, d), BF16)
        for ref in (r.g_gain, r.g_in, r.acc, r.acc_head):
            ref[...] = jnp.zeros_like(ref)

    def norm(m):
        @pl.loop(0, chunks)
        def _(i):
            rows = pl.ds(pl.multiple_of(m * length + i * q, q), q)
            total = jnp.zeros((q, LANES), F32)
            for j in range(d // LANES):
                v = r.x_all[rows, j * LANES : (j + 1) * LANES].astype(F32)
                total = total + v * v
            inv = lax.rsqrt(jnp.sum(total, axis=1, keepdims=True) * (1.0 / d) + EPSILON)
            r.r1[rows, :] = jnp.broadcast_to(inv, (q, LANES))
            for j in range(d // LANES):
                cols = slice(j * LANES, (j + 1) * LANES)
                r.xn[rows, cols] = (r.x_all[rows, cols].astype(F32) * inv * r.gain_in[:, cols]).astype(BF16)

    tile = min(2 * LANES, inner)

    def tiles(total, body, size=tile):
        @pl.loop(0, total // size)
        def _(j):
            body(pl.ds(pl.multiple_of(j * size, size), size))

    def rim_copy(m):
        return remote(
            r.pre.at[m, pl.ds(length - 16, 16), pl.ds(0, chans)], r.rim16.at[m], r.r_send.at[m], r.r_recv.at[m], ctx=other
        )

    def project_x(m):
        for half in (1, 0):
            size = length // 2
            rows = pl.ds(m * length + half * size, size)
            here = pl.ds(half * size, size)
            both = mm(r.xn[rows, :], r.wst[...], NT)
            r.dtr[m, here, :] = both[:, 2 * n :]
            r.pre[m, here, inner:chans] = both[:, : 2 * n].astype(BF16)

            def body(cols):
                r.pre[m, here, cols] = mm(r.xn[rows, :], r.wx[:, cols]).astype(BF16)

            tiles(inner, body)
            if half == 1:

                @pl.when(ctx == 0)
                def _():
                    rim_copy(m).start()

    def project_z(m):
        def body(cols):
            r.z[m, :, cols] = mm(r.xn[seq(m), :], r.wz[:, cols])

        tiles(inner, body)

    def get_rim(m):
        @pl.when(ctx == 1)
        def _():
            rim_copy(m).wait_recv()
            r.rim[m] = r.rim16[m, 8:16].astype(F32)

        @pl.when(ctx == 0)
        def _():
            r.rim[m] = jnp.zeros_like(r.rim[m])

    def scan(m):
        @pl.loop(0, chunks)
        def _(c):
            rows = chunk_rows(c)
            scan_chunk(
                small, m, c, r.off, first,
                convolved(m, rows), one(r.rim, m), span(r.dtr, m, rows), *dims_mode,
                span(r.y, m, rows), span(r.rd, m, rows), span(r.lead, m, rows),
                r.st.at[pl.ds(m, 1), pl.ds(c, 1)], r.lead0.at[pl.ds(m, 1), pl.ds(c, 1)], one(r.fin, 0),
                r.halo, r.state, r.run,
            )

    def state_copy(m, back):
        return remote(
            r.left.at[m], r.came.at[back, m], r.s_send.at[back, m], r.s_recv.at[back, m], ctx=other
        )

    def send_state(m, back):
        @pl.when(ctx == back)
        def _():
            if back == 0:
                rim_copy(m).wait_send()
            r.left[m] = r.fin[0].astype(BF16)
            state_copy(m, back).start()

    def get_state(m, back):
        @pl.when(ctx == 1 - back)
        def _():
            state_copy(m, back).wait_recv()

        @pl.when(ctx == back)
        def _():
            r.came[back, m] = jnp.zeros_like(r.came[back, m])

    def gate(m):
        @pl.loop(0, chunks)
        def _(c):
            rows = chunk_rows(c)
            sts = r.st.at[pl.ds(m, 1), pl.ds(c, 1)]
            ys = span(r.y, m, rows)
            gate_kernel(
                small, ys, span(r.rd, m, rows), span(r.lead, m, rows),
                r.lead0.at[pl.ds(m, 1), pl.ds(c, 1)], sts, r.came.at[0, pl.ds(m, 1)], span(r.z, m, rows), r.gain,
                ys, span(r.yn, m, rows), span(r.sq, m, rows), sts,
            )

    def project_out(m):
        def body(cols):
            r.part[seq(m), cols] = mm(r.yn[m], r.wo[:, cols]).astype(BF16)

        tiles(d, body, 2 * LANES)

    def drains(part, land, send, recv):
        return [
            Drain(part, seq(m), wide, land.at[m], r.stage, send.at[m], recv.at[m], r.load.at[0])
            for m in range(nb)
        ]

    o_drains = drains(r.part, r.o_land, r.od_send, r.od_recv)
    d_drains = drains(r.part, r.d_land, r.dd_send, r.dd_recv)

    def stat_copy(m, kind, there):
        return remote(
            r.stat_out.at[kind, m], r.stat_in.at[kind, m, tp],
            r.t_send.at[kind, m, there], r.t_recv.at[kind, m, tp], tp=there,
        )

    def send_stat(m, kind, columns):
        lane = lax.broadcasted_iota(jnp.int32, (1, LANES), 1)
        both = jnp.where(lane == 0, columns[0], columns[-1])
        rows = both.T[0:8]
        r.stat_out[kind, m] = rows
        r.stat_in[kind, m, tp] = rows
        for step in range(1, tps):
            stat_copy(m, kind, lax.rem(tp + step, tps)).start()

    def get_stat(m, kind):
        for step in range(1, tps):
            there = lax.rem(tp + step, tps)
            remote(
                r.stat_out.at[kind, m], r.stat_in.at[kind, m, there],
                r.t_send.at[kind, m, there], r.t_recv.at[kind, m, there], tp=there,
            ).wait_recv()
        total = r.stat_in[kind, m, 0]
        for i in range(1, tps):
            total = total + r.stat_in[kind, m, i]
        full = jnp.concatenate([total, jnp.zeros((LANES - 8, length), F32)], axis=0)
        return full.T

    def load_cot(m, at):
        cols = pl.ds(pl.multiple_of(at * wide, wide), wide)
        return pltpu.make_async_copy(
            r.cot_o.at[seq(m), cols], r.x_all.at[seq(m), cols], r.cot_load.at[m, at]
        )

    def c_step(m, k):
        c_lines[m].step(k)
        for held, _, slot in c_lines[m].holds(k):

            @pl.when(held)
            def _():
                load_cot(m, slot).start()

    def whole_cot(m):
        for at in range(tps):
            load_cot(m, at).wait()

    def d_gate(m):
        def body(cols):
            r.dyn[0, :, cols] = mm(r.x_all[seq(m), :], r.wo[cols, :], NT)

        tiles(inner, body)

        def dot(rows):
            total = jnp.zeros((64, LANES), F32)
            for lo in range(0, inner, LANES):
                cols = slice(lo, lo + LANES)
                gate_in = r.z[m, rows, cols]
                gated = r.y[m, rows, cols] * gate_in * jax.nn.sigmoid(gate_in)
                total = total + r.dyn[0, rows, cols] * r.gain[:, cols] * gated
            r.dots[rows, :] = jnp.broadcast_to(jnp.sum(total, axis=1, keepdims=True), (64, LANES))

        by_rows_of(64, length, dot)
        send_stat(m, 0, [r.sq[m], r.dots[...]])

    def ungate(m):
        full = get_stat(m, 0)
        lane = lax.broadcasted_iota(jnp.int32, (1, LANES), 1)
        r.sq[m] = jnp.where(lane == 0, lax.rsqrt(full * (1.0 / inner_all) + EPSILON), full)
        r.fin[...] = jnp.zeros_like(r.fin)

        @pl.loop(0, chunks)
        def _(c):
            rows = chunk_rows(c)
            zs = span(r.z, m, rows)
            ungate_chunk(
                small, inner_all, r.dyn.at[:, rows], span(r.y, m, rows), zs, span(r.sq, m, rows), r.gain,
                span(r.rd, m, rows), span(r.lead, m, rows),
                zs, span(r.dz, m, rows), span(r.yn, m, rows), r.g_gain, one(r.fin, 0),
            )

        send_state(m, 1)

    def back(m, after):
        r.d_state[...] = r.came[1, m].astype(F32)
        r.carry[...] = jnp.zeros_like(r.carry)

        @pl.loop(0, chunks)
        def _(c):
            at = chunks - 1 - c
            rows = chunk_rows(at)
            ahead = pl.ds(pl.multiple_of(jnp.maximum(at * q - 16, 0), 16), 16)
            here = convolved(m, rows)
            back_chunk(
                small, m, at, c == 0, r.off, first, here, convolved(m, ahead), one(r.rim, m),
                span(r.dtr, m, rows), span(r.y, m, rows), span(r.z, m, rows),
                r.st.at[pl.ds(m, 1), pl.ds(at, 1)], *dims_mode,
                here, r.pre.at[pl.ds(m, 1), rows, pl.ds(chans, LANES)], one(r.edge, m), one(r.rim_out, m),
                r.acc, r.acc_head, r.d_state, r.carry,
            )
            for k, hook in after.items():
                pl.when(c == k)(hook)

        @pl.when(ctx == 1)
        def _():
            edge_copy(m).start()

    def edge_copy(m):
        return remote(r.rim_out.at[m], r.rim_in.at[m], r.e_send.at[m], r.e_recv.at[m], ctx=other)

    def patch(m):
        @pl.when(ctx == 0)
        def _():
            edge_copy(m).wait_recv()
            rows = pl.ds(length - 16, 16)
            late = (r.edge[m] + r.rim_in[m]).astype(BF16).astype(F32)
            both = jnp.concatenate([r.pre[m, rows, :chans].astype(F32)[0:8], late], axis=0)
            r.pre[m, rows, :chans] = both.astype(BF16)

    def d_norm(m, at):
        size = min(2 * LANES, wide)

        @pl.loop(0, wide // size)
        def _(j):
            cols = pl.ds(pl.multiple_of(at * wide + j * size, size), size)
            total = mm(r.dz[m], r.wz[cols, :], NT) + mm(r.pre[m, :, :inner], r.wx[cols, :], NT)
            total = total + mm(r.pre[m, :, inner:], r.wst[:, cols])
            r.part[seq(m), cols] = total.astype(BF16)
            prod = total * r.xn[seq(m), cols].astype(F32)
            r.g_in[0:1, cols] += jnp.sum(prod, axis=0, keepdims=True)
            lanes = r.dots[...]
            for lo in range(0, size, LANES):
                lanes = lanes + prod[:, lo : lo + LANES]
            r.dots[...] = lanes

    def send_dots(m):
        dot = jnp.sum(r.dots[...], axis=1, keepdims=True)
        send_stat(m, 1, [jnp.broadcast_to(dot, (length, LANES))])

    def rb(c, y, k):
        return 4 * c + 2 * y + k

    def by_rows(ref, k):
        return lambda c, y: ref.at[pl.ds(pl.multiple_of((2 * y + k) * bd, bd), bd), pl.ds(c * inner, inner)]

    def folds(i, theirs, block, lands):
        return Fold(theirs, block, *lands, r.stage_z, bd // 2, r.f_send.at[i], r.f_recv.at[i], r.load.at[1])

    fold_o = folds(0, by_rows(r.wo, 1 - core), by_rows(r.wo, core), (r.o1, r.o2, r.o3))
    fold_z = folds(1, by_rows(r.x_all, 1 - core), by_rows(r.x_all, core), (r.z1, r.z2, r.z3))
    fold_x = folds(
        2,
        by_rows(r.wo, 1 - core),
        lambda c, y: r.yn.at[c, pl.ds(pl.multiple_of(y * bd, bd), bd)],
        (r.x1, r.x2, r.x3),
    )
    fold_s = folds(3, lambda c, y: r.gs.at[c, y, 1], lambda c, y: r.gs.at[c, y, 0], (r.s1, r.s2, r.s3))

    def xn_cols(c, y, k):
        return r.xn[:, pl.ds(pl.multiple_of(rb(c, y, k) * bd, bd), bd)]

    def grad_o(c, y, k, into):
        cot = r.x_all[:, pl.ds(pl.multiple_of(rb(c, y, k) * bd, bd), bd)]
        into[0][...] = mm(cot, r.yn[...].reshape(tokens, inner), TN).astype(BF16)

    def grad_z(c, y, k, into):
        into[0][...] = mm(xn_cols(c, y, k), r.dz[...].reshape(tokens, inner), TN).astype(BF16)

    def grad_x(c, y, k, into):
        left = xn_cols(c, y, k)
        into[0][...] = mm(left, r.pre[:, :, :inner].reshape(tokens, inner), TN).astype(BF16)
        into[1][...] = mm(left, r.pre[:, :, inner:].reshape(tokens, extra), TN).astype(BF16)

    def send_grads(make, *fold):
        for c in range(2):
            for y in range(2):
                make(c, y, 1 - core, [f.theirs(c, y) for f in fold])
                for f in fold:
                    f.first(c, y).start()

    def own_grads(make, *fold):
        for c in range(2):
            for y in range(2):
                make(c, y, core, [f.block(c, y) for f in fold])

    out_copies = []

    def keep(pair):
        out_copies.append(pair)
        kept(len(out_copies) - 1).start()

    waited = []

    def settle(i):
        kept(i).wait()
        waited.append(i)

    def kept(i):
        return pltpu.make_async_copy(*out_copies[i](), r.outs.at[i])

    def give_out(m):
        o_drains[m].close()
        keep(lambda: (r.part.at[seq(m), mine], r.out.at[seq(m)]))
        keep(lambda: (r.sq.at[m], r.stat.at[seq(m)]))

    def give_dx(m):
        d_drains[m].close()
        keep(lambda: (r.part.at[seq(m), mine], r.dx.at[seq(m)]))

    def give_dots(m):
        lane = lax.broadcasted_iota(jnp.int32, (1, LANES), 1)
        dot = get_stat(m, 1)[:, 0:1]
        r.lead[m] = jnp.where(lane == 0, r.r1[seq(m), :], dot)
        keep(lambda: (r.lead.at[m], r.stat2.at[seq(m)]))

    def device(j):
        c, s = j // 4, j % 4
        return lax.rem(ctx + c, 2), lax.rem(fs + s, 4)

    def tiny_copy(j):
        c, f = device(j)
        return remote(
            r.tiny.at[:], r.tiny_in.at[4 * ctx + fs], r.y_send.at[j], r.y_recv.at[4 * ctx + fs], ctx=c, fsdp=f
        )

    def tiny_recv(j):
        c, f = device(j)
        at = 4 * c + f
        remote(r.tiny.at[:], r.tiny_in.at[at], r.y_send.at[j], r.y_recv.at[at], ctx=c, fsdp=f).wait_recv()

    def spread_copy(step):
        there = lax.rem(tp + step, tps)
        return remote(r.tiny_sum.at[:], r.tiny_all.at[tp], r.q_send.at[step], r.q_recv.at[tp], tp=there)

    def bc_copy(step):
        there = lax.rem(tp + step, tps)
        rows = pl.ds(pl.multiple_of(there * rows_bc, rows_bc), rows_bc)
        return remote(r.bc_sum.at[rows], r.bc_all.at[tp], r.b_send.at[step], r.b_recv.at[tp], tp=there)

    x_0, x_1 = x_lines
    c_0, c_1 = c_lines
    o_0, o_1 = o_drains
    d_0, d_1 = d_drains
    last = tps - 1

    def steps(line, lo, hi=tps):
        for k in range(lo, hi):
            line.step(k)

    def rounds(drain, lo, hi=last):
        for j in range(lo, hi):
            drain.round(j)

    for step in range(1, tps):
        bc_in_copy(step).start()
    x_0.step(0)
    far(0).start()
    near(0).start()
    for copy in locals_:
        copy.start()
    prepare()
    for step in range(1, tps):
        bc_in_recv(step)
    locals_[5].wait()
    locals_[6].wait()
    for w in (3, 1, 2):
        far(w).start()
        near(w).start()
    steps(x_0, 1, last)
    pass_on(3)
    pass_on(0)
    steps(x_0, last)
    c_0.step(0)
    locals_[3].wait()
    norm(0)
    whole_weight(0)
    whole_weight(3)
    project_x(0)
    get_rim(0)
    scan(0)
    send_state(0, 0)
    locals_[4].wait()
    x_0.finish()
    load_cot(0, tp).start()
    c_step(0, 1)
    pass_on(1)
    whole_weight(1)
    project_z(0)
    get_state(0, 0)
    gate(0)
    c_step(0, 2)
    pass_on(2)
    whole_weight(2)
    project_out(0)
    for k in range(3, tps):
        c_step(0, k)
    x_1.step(0)
    whole_cot(0)
    d_gate(0)
    x_1.step(1)
    ungate(0)
    o_0.source(0)
    x_1.step(2)
    get_state(0, 1)

    def middle_0():
        o_0.round(1)

    def middle_1():
        steps(x_1, 3)
        c_1.step(0)
        norm(1)
        project_x(1)
        get_rim(1)
        x_1.finish()
        load_cot(1, tp).start()
        scan(1)
        send_state(1, 0)
        c_step(1, 1)
        o_0.source(2)
        project_z(1)
        get_state(1, 0)
        gate(1)
        project_out(1)

    def middle_2():
        c_step(1, 2)
        o_1.source(0)

    back(0, {0: middle_0, 1: middle_1, 2: middle_2})
    for k in range(3, tps):
        c_step(1, k)
    o_0.relay(2)
    whole_cot(1)
    d_gate(1)
    o_1.source(1)
    ungate(1)
    give_out(0)
    o_0.finish()
    patch(0)
    r.dots[...] = jnp.zeros_like(r.dots)
    settle(0)
    o_1.relay(1)
    d_norm(0, last)
    d_norm(0, 0)
    o_1.source(2)
    for k in range(1, last):
        d_norm(0, last - k)
    send_dots(0)
    get_state(1, 1)

    def late_0():
        o_1.relay(2)
        relay(2).wait_send()
        send_grads(grad_o, fold_o)
        d_0.source(0)
        own_grads(grad_o, fold_o)

    def late_1():
        fold_o.one()
        send_grads(grad_z, fold_z)
        own_grads(grad_z, fold_z)
        d_0.source(1)
        d_0.relay(1)
        fold_z.one()

    def late_2():
        d_0.source(2)
        give_out(1)

    back(1, {0: late_0, 1: late_1, 2: late_2})
    d_0.relay(2)
    o_1.finish()
    r.dots[...] = jnp.zeros_like(r.dots)
    settle(2)
    fold_o.sent()
    patch(1)
    d_norm(1, last)
    d_norm(1, 0)
    d_1.round(0)
    send_grads(grad_x, fold_x, fold_s)
    own_grads(grad_x, fold_x, fold_s)
    fold_o.two()
    fold_z.two()
    for k in range(1, last):
        d_norm(1, last - k)
    d_1.round(1)
    fold_s.one()
    fold_x.one()
    send_dots(1)
    fold_o.three()
    keep(lambda: (fold_o.block(ctx, yy), r.go))
    taps = r.cw.shape[0]
    head_of = (
        lax.broadcasted_iota(jnp.int32, (inner, LANES), 0) // width
        == lax.broadcasted_iota(jnp.int32, (inner, LANES), 1)
    ).astype(F32)
    skip = mm(r.acc[:, :inner], head_of, precision=PRECISE)[taps + 1 : taps + 2]
    r.tiny[...] = r.acc[...]
    r.tiny[5:6, :inner] = r.g_gain[0:1]
    for i in range(d // inner):
        r.tiny[6 + i : 7 + i, :inner] = r.g_in[0:1, i * inner : (i + 1) * inner]
    r.tiny[5:7, inner : inner + LANES] = r.acc_head[0:2]
    r.tiny[7:8, inner : inner + LANES] = skip
    for j in range(1, 8):
        tiny_copy(j).start()
    r.tiny_in[4 * ctx + fs] = r.tiny[...]
    rounds(d_1, 2)
    give_dx(0)
    give_dots(0)
    fold_z.three()
    keep(lambda: (fold_z.block(ctx, yy), r.gz))
    fold_s.two()
    fold_x.two()
    for j in range(1, 8):
        tiny_recv(j)
    total = r.tiny_in[0]
    for i in range(1, 8):
        total = total + r.tiny_in[i]
    r.tiny_sum[...] = total
    r.tiny_all[tp] = total
    for step in range(1, tps):
        spread_copy(step).start()
    give_dots(1)
    sums = fold_s.three()
    r.gdt[...] = sums[:, 2 * n :].astype(F32).T[:hpd]
    for lo in range(0, 2 * n, LANES):
        r.bc_sum[lo : lo + LANES, :] = sums[:, lo : lo + LANES].astype(F32).T.astype(BF16)
    r.bc_all[tp] = r.bc_sum[pl.ds(pl.multiple_of(tp * rows_bc, rows_bc), rows_bc), :]
    for step in range(1, tps):
        bc_copy(step).start()
    give_dx(1)
    fold_x.three()
    keep(lambda: (fold_x.block(ctx, yy), r.gx))
    for step in range(1, tps):
        there = lax.rem(tp + step, tps)
        remote(
            r.bc_sum.at[pl.ds(0, rows_bc)], r.bc_all.at[there], r.b_send.at[step], r.b_recv.at[there], tp=there
        ).wait_recv()
    total = r.bc_all[0].astype(F32)
    for i in range(1, tps):
        total = total + r.bc_all[i].astype(F32)
    r.gbc[...] = total
    for step in range(1, tps):
        there = lax.rem(tp + step, tps)
        remote(r.tiny_sum.at[:], r.tiny_all.at[there], r.q_send.at[step], r.q_recv.at[there], tp=there).wait_recv()
    keep(lambda: (r.tiny_all, r.tiny_o))

    for step in range(1, tps):
        bc_in_copy(step).wait_send()
    for line in c_lines + d_drains:
        line.finish()
    fold_o.finish()
    for fold in (fold_z, fold_x, fold_s):
        fold.sent()
        fold.finish()
    for w in range(4):
        near(w).wait_send()
        far(w).wait_send()
        if w != 2:
            relay(w).wait_send()
    for m in range(nb):
        for kind in range(2):
            for step in range(1, tps):
                stat_copy(m, kind, lax.rem(tp + step, tps)).wait_send()

        @pl.when(ctx == 0)
        def _():
            state_copy(m, 0).wait_send()

        @pl.when(ctx == 1)
        def _():
            state_copy(m, 1).wait_send()
            edge_copy(m).wait_send()

    for j in range(1, 8):
        tiny_copy(j).wait_send()
    for step in range(1, tps):
        spread_copy(step).wait_send()
        bc_copy(step).wait_send()
    for i in range(len(out_copies)):
        if i not in waited:
            kept(i).wait()


SMALL = ["gdt", "gbc"]


def layer(args, nb, length, inner_dev_heads, width, n, tps, inner_all):
    offs, x, cot, wx = args[:4]
    hpd = inner_dev_heads
    tokens, wide = x.shape
    d = wide * tps
    inner = wx.shape[1]
    chans = inner + 2 * n
    extra = 2 * n + LANES
    q = min(CHUNK, length)
    chunks = length // q
    bd = d // 8
    dims = (nb, length, q, inner, width, n, d, inner_all, hpd)
    taps = args[9].shape[0]
    sds = jax.ShapeDtypeStruct
    outs = dict(
        out=((tokens, wide), BF16), dx=((tokens, wide), BF16), gz=((bd, inner), BF16), gx=((bd, inner), BF16),
        stat=((tokens, LANES), F32), stat2=((tokens, LANES), F32),
        gdt=((hpd, bd), F32), gbc=((2 * n // tps, bd), F32), go=((bd, inner), BF16),
        tiny_o=((tps, 8, chans), F32),
        cot_o=((tokens, d), BF16),
        o_land=((nb, 2, tps, length, wide), BF16), d_land=((nb, 2, tps, length, wide), BF16),
        o1=((4, bd, inner), BF16), o2=((2, 2, bd // 2, inner), BF16), o3=((2, bd // 2, inner), BF16),
        z1=((4, bd, inner), BF16), z2=((2, 2, bd // 2, inner), BF16), z3=((2, bd // 2, inner), BF16),
        x1=((4, bd, inner), BF16), x2=((2, 2, bd // 2, inner), BF16), x3=((2, bd // 2, inner), BF16),
        s1=((4, bd, extra), BF16), s2=((2, 2, bd // 2, extra), BF16), s3=((2, bd // 2, extra), BF16),
    )
    vmem = dict(
        x_all=((tokens, d), BF16), xn=((tokens, d), BF16), r1=((tokens, LANES), F32),
        pre=((nb, length, chans + LANES), BF16), dtr=((nb, length, LANES), F32), z=((nb, length, inner), F32),
        y=((nb, length, inner), F32), rd=((nb, length, n), BF16), lead=((nb, length, LANES), F32),
        st=((nb, chunks, n, inner), BF16), lead0=((nb, chunks, 8, LANES), F32), fin=((1, n, inner), F32),
        sq=((nb, length, LANES), F32), yn=((nb, length, inner), BF16), part=((tokens, d), BF16),
        rim=((nb, 8, chans), F32), rim16=((nb, 16, chans), BF16), came=((2, nb, n, inner), BF16),
        left=((nb, n, inner), BF16), wx=((d, inner), BF16), wz=((d, inner), BF16), wo=((inner, d), BF16),
        halo=((8, chans), F32), state=((n, inner), F32), run=((1, LANES), F32),
        dyn=((1, length, inner), F32), dz=((nb, length, inner), BF16),
        dots=((length, LANES), F32), g_gain=((8, inner), F32), g_in=((8, d), F32),
        acc=((8, chans), F32), acc_head=((8, LANES), F32), carry=((8, chans), F32),
        edge=((nb, 8, chans), F32), rim_out=((nb, 8, chans), F32), rim_in=((nb, 8, chans), F32),
        stat_out=((2, nb, 8, length), F32), stat_in=((2, nb, tps, 8, length), F32),
        stage=((2, length, wide), BF16), stage_z=((2, bd, max(inner, extra)), BF16), gs=((2, 2, 2, bd, extra), BF16),
        wst=((2 * n + LANES, d), BF16), d_state=((n, inner), F32), cw=((taps, chans), F32), cb=((1, chans), F32),
        gain=((1, inner), F32), dtb=((1, LANES), F32), rate=((1, LANES), F32),
        dsk=((1, inner), F32),

        bc_sum=((2 * n, bd), BF16),
        bc_all=((tps, 2 * n // tps, bd), BF16), tiny=((8, chans), F32), tiny_in=((8, 8, chans), F32),
        tiny_sum=((8, chans), F32), tiny_all=((tps, 8, chans), F32),
    )
    sems = dict(
        cot_load=(nb, tps),
        xs_send=(nb, 2, tps), xs_recv=(nb, tps), cs_send=(nb, 2, tps), cs_recv=(nb, tps),
        w_send=(4, 3), w_recv=(4, 4), r_send=(nb,), r_recv=(nb,), s_send=(2, nb), s_recv=(2, nb),
        e_send=(nb,), e_recv=(nb,), od_send=(nb, 2, tps), od_recv=(nb, 2, tps),
        dd_send=(nb, 2, tps), dd_recv=(nb, 2, tps), t_send=(2, nb, tps), t_recv=(2, nb, tps),
        f_send=(4, 10), f_recv=(4, 10), y_send=(8,), y_recv=(8,), q_send=(tps,), q_recv=(tps,),
        b_send=(tps,), b_recv=(tps,), v_send=(tps,), v_recv=(tps,), loc=(9,), load=(3, 2), outs=(16,),
    )
    names = IN + list(outs) + list(vmem) + list(sems)
    hbm = pl.BlockSpec(memory_space=pl.ANY)
    whole_vmem = pl.BlockSpec(memory_space=pltpu.VMEM)
    got = pl.pallas_call(
        functools.partial(layer_kernel, dims, names),
        in_specs=[pl.BlockSpec(memory_space=pltpu.SMEM)] + [hbm] * 7 + [whole_vmem] * (len(IN) - 8),
        out_specs=[whole_vmem if k in SMALL else hbm for k in outs],
        out_shape=[sds(*v) for v in outs.values()],
        scratch_shapes=[pltpu.VMEM(*v) for v in vmem.values()]
        + [pltpu.SemaphoreType.DMA(v) for v in sems.values()],
        compiler_params=pltpu.CompilerParams(
            collective_id=0, has_side_effects=True, vmem_limit_bytes=63 << 20
        ),
        name="layer",
    )(*args)
    return dict(zip(outs, got))


def ends_kernel(dims, x, cot, o_sum, d_sum, stat, stat2, gain_in, gz_in, gx_in, go_in, gdt_in, gbc_in, tiny,
                out, dx, gz, gx, go, gdt, gbc, g_cw, g_cb, g_ng, g_ig, g_al, g_db, g_ds):
    inner, d, hpd = dims
    wide = x.shape[1]
    tps = d // wide
    tp = lax.axis_index("tp")
    h = x[...].astype(F32)
    out[...] = h + stat[:, 0:1] * o_sum[...].astype(F32)
    inv = stat2[:, 0:1]
    own_gain = gain_in[:, pl.ds(pl.multiple_of(tp * wide, wide), wide)]
    share = inv * own_gain * d_sum[...].astype(F32)
    dx[...] = cot[...].astype(F32) + share - h * (inv * inv * stat2[:, 1:2] * (1.0 / d))
    gz[...] = gz_in[...].astype(F32)
    gx[...] = gx_in[...].astype(F32)
    go[...] = go_in[...].astype(F32).T

    @pl.when(pl.program_id(0) == 0)
    def _():
        gdt[...] = gdt_in[...]
        gbc[...] = gbc_in[...]
        taps = g_cw.shape[0]
        lane = lax.broadcasted_iota(jnp.int32, (8, LANES), 1)
        both, g_norm, heads = 0.0, 0.0, 0.0
        for t in range(tps):
            every = tiny.at[t]
            chan = slice(t * inner, (t + 1) * inner)
            g_cw[:, chan] = every[0:taps, :inner]
            g_cb[:, chan] = every[taps : taps + 1, :inner]
            g_ng[:, chan] = every[5:6, :inner]
            both = both + every[:, inner:]
            g_norm = g_norm + every[:, :inner]
            heads_t = jnp.where(lane < hpd, every[:, inner : inner + LANES], 0.0)
            heads = heads + (pltpu.roll(heads_t, t * hpd, 1) if t else heads_t)
        g_cw[:, tps * inner :] = both[0:taps]
        g_cb[:, tps * inner :] = both[taps : taps + 1]
        for i in range(d // inner):
            cols = slice(i * inner, (i + 1) * inner)
            g_ig[:, cols] = g_norm[6 + i : 7 + i] / gain_in[:, cols]
        count = g_al.shape[1]
        g_al[...] = heads[5:6, :count]
        g_db[...] = heads[6:7, :count]
        g_ds[...] = heads[7:8, :count]


def ends(x, cot, got, gain_in, conv_shape, heads, inner_all, hpd):
    tokens, wide = x.shape
    d = gain_in.shape[1]
    bd, inner = got["gz"].shape
    steps = 2
    rows = tokens // steps

    def by_row(size, width):
        return pl.BlockSpec((size, width), lambda i: (i, 0))

    sds = jax.ShapeDtypeStruct
    shapes = [
        (tokens, wide), (tokens, wide), (bd, inner), (bd, inner), (inner, bd), got["gdt"].shape, got["gbc"].shape,
        conv_shape, (1, conv_shape[1]), (1, inner_all), (1, d), (1, heads), (1, heads), (1, heads),
    ]
    return pl.pallas_call(
        functools.partial(ends_kernel, (inner, d, hpd)),
        grid=(steps,),
        in_specs=[by_row(rows, wide)] * 4
        + [by_row(rows, LANES)] * 2
        + [whole(gain_in.shape)]
        + [by_row(bd // steps, inner)] * 2
        + [pl.BlockSpec((bd, inner // steps), lambda i: (0, i))]
        + [whole(got[k].shape) for k in ("gdt", "gbc", "tiny_o")],
        out_specs=[by_row(rows, wide)] * 2
        + [by_row(bd // steps, inner)] * 2
        + [by_row(inner // steps, bd)]
        + [whole(v) for v in shapes[5:]],
        out_shape=[sds(v, F32) for v in shapes],
        compiler_params=pltpu.CompilerParams(vmem_limit_bytes=63 << 20),
        name="ends",
    )(x, cot, got["out"], got["dx"], got["stat"], got["stat2"], gain_in, got["gz"], got["gx"], got["go"],
      got["gdt"], got["gbc"], got["tiny_o"])


def shift(arr, axis, by):
    peers = lax.axis_size(axis)
    pairs = [(i, i + by) for i in range(peers) if 0 <= i + by < peers]
    return lax.ppermute(arr, axis, pairs)


def heads_row(vec, width=LANES):
    return jnp.pad(vec[None], ((0, 0), (0, width - vec.shape[0])))


def on_device(
    x_in,
    cotangent,
    offsets,
    in_gain,
    w_z,
    w_x,
    w_dt,
    w_bc,
    conv_w,
    conv_b,
    dt_bias,
    a_log,
    d_skip,
    norm_gain,
    w_out,
):
    batches, seq_count, length, width_dev = x_in.shape
    nb = batches * seq_count
    tokens = nb * length
    tp_rank = lax.axis_index("tp")
    ctx_rank = lax.axis_index("ctx")
    peers = lax.axis_size("ctx")
    inner = w_z.shape[1]
    heads = w_dt.shape[1]
    width = inner // heads
    model = in_gain.shape[0]
    inner_all = norm_gain.shape[0]
    pair = conv_w.shape[1] - inner_all
    n = pair // 2
    taps = conv_w.shape[0]

    def mine(arr, size, axis):
        return lax.dynamic_slice_in_dim(arr, tp_rank * size, size, axis)

    cw = jnp.concatenate([mine(conv_w, inner, 1), conv_w[:, inner_all:]], axis=1)
    cb = jnp.concatenate([mine(conv_b, inner, 0), conv_b[inner_all:]])[None]
    gain = mine(norm_gain, inner, 0)[None]
    gain_in = mine(in_gain, width_dev, 0)
    dtb = heads_row(mine(dt_bias, heads, 0))
    rate = heads_row(-jnp.exp(mine(a_log, heads, 0)))
    dsk = jnp.repeat(mine(d_skip, heads, 0), width)[None]
    pos = (ctx_rank * length).astype(jnp.int32)[None]
    offs = offsets.reshape(nb, offsets.shape[-1])

    x_own = x_in.reshape(tokens, width_dev)
    cot_own = cotangent.reshape(tokens, width_dev)
    tps = lax.axis_size("tp")
    def chained(start, lend, by):
        came = jnp.zeros_like(start)
        for k in range(peers - 1):
            sent = start if k == 0 else start + lend * came
            came = shift(sent.astype(BF16), "ctx", by).astype(F32)
        return came

    def ending(lead):
        return jnp.repeat(lead[:, length - 1, :heads], width, axis=-1)[:, None]

    if peers == 2 and lax.axis_size("fsdp") == 4 and nb == 2 and heads % 16 == 0:
        got = layer(
            (offs, x_own, cot_own, w_x, w_z, w_out, w_bc.T, w_dt.T, in_gain[None], conv_w, conv_b[None],
             dt_bias[None], a_log[None], d_skip[None], norm_gain[None]),
            nb, length, heads, width, n, tps, inner_all,
        )
        shape = (batches, seq_count, length, width_dev)
        out, d_x, g_z, g_x, g_out, g_dt, g_bc, g_cw, g_cb, g_ng, g_ig, g_al, g_db, g_ds = ends(
            x_own, cot_own, got, in_gain[None], conv_w.shape, dt_bias.shape[0], inner_all, heads
        )
        return (
            out.reshape(shape),
            d_x.reshape(shape),
            g_ig.reshape(-1),
            g_z,
            g_x,
            g_dt.T,
            g_bc.T,
            g_cw,
            g_cb.reshape(-1),
            g_db.reshape(-1),
            g_al.reshape(-1),
            g_ds.reshape(-1),
            g_ng.reshape(-1),
            g_out,
        )
    small = jnp.concatenate([w_bc, w_dt], axis=1)
    small = lax.all_gather(small, "fsdp", axis=0, tiled=True)
    wdt = jnp.pad(small[:, pair // tps :], ((0, 0), (0, LANES - heads)))
    wbc = lax.all_gather(small[:, : pair // tps], "tp", axis=1, tiled=True)

    x_all = lax.all_gather(x_own, "tp", axis=1, tiled=True)
    wx = lax.all_gather(w_x, "fsdp", axis=0, tiled=True)
    wz = lax.all_gather(w_z, "fsdp", axis=0, tiled=True)
    wo = lax.all_gather(w_out, "fsdp", axis=1, tiled=True)
    cot_all = lax.all_gather(cot_own, "tp", axis=1, tiled=True)
    resid = x_all.astype(F32)
    r1 = lax.rsqrt(jnp.mean(resid * resid, axis=1, keepdims=True) + EPSILON)
    xn = (resid * r1 * in_gain).astype(BF16)
    pre = jnp.concatenate([mm(xn, wx).astype(BF16), mm(xn, wbc).astype(BF16)], axis=1)
    pre = pre.reshape(nb, length, inner + pair)
    dtr = mm(xn, wdt).reshape(nb, length, LANES)
    z = mm(xn, wz).reshape(nb, length, inner)
    rim = shift(pre[:, length - 8 :], "ctx", 1).astype(F32)
    y, rd, lead, st, lead0, fin = scan_forward(
        offs, pos, pre, rim, dtr, cw, cb, dtb, rate, dsk, width, n
    )
    s_in = chained(fin, ending(lead), 1)
    y, ygg, sq, st = gate_forward(y, rd, lead, lead0, st, s_in, z, gain, width)
    part = mm(ygg.reshape(tokens, inner), wo).astype(BF16)
    lend = ending(lead)
    share = lax.psum_scatter(part, "tp", scatter_dimension=1, tiled=True)
    dyn = mm(cot_all, wo, NT).reshape(nb, length, inner)
    dot = jnp.sum(dyn * gain * y * jax.nn.silu(z), axis=2)
    stat = jnp.stack([sq[..., 0], dot])
    stat = jnp.sum(lax.all_gather(stat, "tp"), axis=0)
    r2 = lax.rsqrt(stat[0] / inner_all + EPSILON)
    out = x_own.astype(F32) + r2.reshape(tokens, 1) * share.astype(F32)
    stat = jnp.pad(jnp.stack([r2, stat[1]], axis=-1), ((0, 0), (0, 0), (0, LANES - 2)))
    dy, dz, yn, g_gain, g_state = gate_backward(dyn, y, z, stat, gain, rd, lead, width, inner_all)
    dz = dz.reshape(tokens, inner)
    yn = yn.reshape(tokens, inner)
    d_in = chained(g_state, lend, -1)
    rows = ("ctx", "fsdp")

    def scattered(grad):
        return lax.psum_scatter(grad.astype(BF16), rows, scatter_dimension=0, tiled=True)

    g_out = scattered(mm(cot_all, yn, TN)).astype(F32).T
    g_z = scattered(mm(xn, dz, TN)).astype(F32)
    dcat, ddt, edge, rim_grad, acc, acc_head = scan_backward(
        offs, pos, pre, rim, dtr, y, dy, st, d_in, cw, cb, dtb, rate, dsk, width
    )
    edge = (edge + shift(rim_grad, "ctx", -1)).astype(BF16)
    dcat = lax.dynamic_update_slice(dcat, edge, (0, length - 8, 0)).reshape(tokens, inner + pair)
    ddt = ddt.reshape(tokens, LANES)
    dxn = mm(dz, wz, NT) + mm(dcat[:, :inner], wx, NT) + mm(dcat[:, inner:], wbc, NT) + mm(ddt, wdt, NT)
    dxn = lax.psum_scatter(dxn.astype(BF16), "tp", scatter_dimension=1, tiled=True).astype(F32)
    g_xbc = scattered(jnp.concatenate([mm(xn, dcat, TN), mm(xn, ddt, TN)[:, :heads]], axis=1))
    g_x = g_xbc[:, :inner].astype(F32)
    g_dt = g_xbc[:, inner + pair :].astype(F32)
    g_bc = lax.psum_scatter(
        g_xbc[:, inner : inner + pair].astype(F32), "tp", scatter_dimension=1, tiled=True
    )
    h_own = x_own.astype(F32)
    scaled = dxn * gain_in
    in_dot = jnp.sum(lax.all_gather(jnp.sum(scaled * h_own, axis=1), "tp"), axis=0)[:, None]
    g_in = jnp.sum(dxn * h_own * r1, axis=0)
    d_x = cot_own.astype(F32) + r1 * scaled - h_own * r1**3 * in_dot / model
    pieces = [
        g_in,
        acc[:taps, :inner].reshape(-1),
        acc[taps, :inner],
        g_gain[0],
        acc_head[1, :heads],
        acc_head[0, :heads],
        acc[taps + 1, :inner].reshape(heads, width).sum(axis=1),
        acc[:taps, inner:].reshape(-1),
        acc[taps, inner:],
    ]
    sizes = [p.shape[0] for p in pieces]
    packed = jnp.sum(lax.all_gather(jnp.concatenate(pieces), rows), axis=0)
    packed = lax.all_gather(packed, "tp")
    parts, start = [], 0
    for size in sizes:
        parts.append(packed[:, start : start + size])
        start += size
    tp = packed.shape[0]
    g_cw = jnp.concatenate(
        [
            parts[1].reshape(tp, taps, inner).transpose(1, 0, 2).reshape(taps, inner_all),
            jnp.sum(parts[7], axis=0).reshape(taps, pair),
        ],
        axis=1,
    )
    g_cb = jnp.concatenate([parts[2].reshape(-1), jnp.sum(parts[8], axis=0)])
    shape = (batches, seq_count, length, width_dev)
    return (
        out.reshape(shape),
        d_x.reshape(shape),
        parts[0].reshape(-1),
        g_z,
        g_x,
        g_dt,
        g_bc,
        g_cw,
        g_cb,
        parts[4].reshape(-1),
        parts[5].reshape(-1),
        parts[6].reshape(-1),
        parts[3].reshape(-1),
        g_out,
    )


def solution(mesh):
    stream = P(None, "fsdp", "ctx", "tp")
    weight = P("fsdp", "tp")
    grad = P(("ctx", "fsdp"), "tp")
    in_specs = (
        (stream, stream, P(None, "fsdp", None), P())
        + (weight,) * 4
        + (P(),) * 6
        + (P("tp", "fsdp"),)
    )
    out_specs = (
        (stream, stream, P()) + (grad,) * 4 + (P(),) * 6 + (P("tp", ("ctx", "fsdp")),)
    )
    return jax.shard_map(
        on_device, mesh=mesh, in_specs=in_specs, out_specs=out_specs, check_vma=False
    )
```

```python
import functools
import types

import jax
import jax.numpy as jnp
from jax import lax
from jax.experimental import pallas as pl
from jax.experimental.pallas import tpu as pltpu
from jax.sharding import PartitionSpec as P

EPSILON = 1e-05
PRECISE = lax.Precision.HIGHEST
LANES = 128
CHUNK = 128
FAR = -1e30
F32 = jnp.float32
BF16 = jnp.bfloat16


def mm(a, b, dims=((1,), (0,)), precision=None):
    return lax.dot_general(a, b, (dims, ((), ())), precision=precision, preferred_element_type=F32)


NN = ((1,), (0,))
NT = ((1,), (1,))
TN = ((0,), (0,))


def softplus(v):
    return jnp.maximum(v, 0.0) + jnp.log1p(jnp.exp(-jnp.abs(v)))


def head_sums(v, head_of):
    high = v.astype(BF16)
    low = (v - high.astype(F32)).astype(BF16)
    return mm(high, head_of) + mm(low, head_of)


def silu_slope(v, sig):
    return sig * (1.0 + v * (1.0 - sig))


def doc_of(off_ref, seq, pos):
    count = jnp.zeros_like(pos)
    for j in range(off_ref.shape[1]):
        count = count + (off_ref[seq, j] <= pos).astype(jnp.int32)
    return count


def widen(cols, head, lane, width):
    out = cols[:, head : head + 1]
    for i in range(1, LANES // width):
        out = jnp.where(lane >= i * width, cols[:, head + i : head + i + 1], out)
    return jnp.broadcast_to(out, (cols.shape[0], LANES))


class Span:
    def __init__(self, off_ref, first, seq, start, q, dtr, dtb, rate, taps):
        at = first + start
        col = at + lax.broadcasted_iota(jnp.int32, (q, 1), 0)
        row = at + lax.broadcasted_iota(jnp.int32, (1, q), 1)
        dcol = doc_of(off_ref, seq, col)
        drow = doc_of(off_ref, seq, row)
        before = doc_of(off_ref, seq, at - 1)
        before_dev = doc_of(off_ref, seq, first - 1)
        last = doc_of(off_ref, seq, at + q - 1)
        self.match = [
            (doc_of(off_ref, seq, col - (taps - 1 - k)) == dcol).astype(F32) for k in range(taps - 1)
        ]
        self.far = jnp.where((dcol == drow) & (col >= row), 0.0, FAR)
        self.kept = (dcol == before).astype(F32)
        self.kept_dev = (dcol == before_dev).astype(F32)
        self.carry_dev = (before == before_dev).astype(F32)
        self.dt_in = dtr + dtb
        self.dt = softplus(self.dt_in)
        decay = self.dt * rate
        tri = (
            lax.broadcasted_iota(jnp.int32, (q, q), 0) >= lax.broadcasted_iota(jnp.int32, (q, q), 1)
        ).astype(F32)
        self.tri = tri
        self.cum = mm(tri, decay, precision=PRECISE)
        self.cum_t = self.cum.T
        self.lead = jnp.exp(self.cum) * self.kept
        end = self.cum[q - 1 : q, :]
        self.tail = jnp.exp(end - self.cum) * (dcol == last).astype(F32)
        self.end = end

    def fade(self, head):
        return jnp.exp(self.cum[:, head : head + 1] - self.cum_t[head : head + 1, :] + self.far)


def conv_block(pre, halo, cw, cb, match):
    taps = len(match) + 1
    ext = jnp.concatenate([halo, pre], axis=0)
    shifted = [
        pltpu.roll(ext, taps - 1 - k, 0)[8:] * match[k] for k in range(taps - 1)
    ] + [pre]
    conv = cb
    for k in range(taps):
        conv = conv + cw[k : k + 1] * shifted[k]
    return conv, shifted


def scan_kernel(dims, off, pos, *refs):
    scan_chunk(dims, pl.program_id(0), pl.program_id(1), off, pos[0], *refs)


def scan_chunk(dims, b, c, off, first, pre, rim, dtr, cw, cb, dtb, rate, dsk, y, rd, lead, st, lead0, fin, halo, state, run):
    q, inner, width, n = dims

    @pl.when(c == 0)
    def _():
        halo[...] = rim[0]
        state[...] = jnp.zeros_like(state)
        run[...] = jnp.zeros_like(run)

    taps = cw.shape[0]
    sp = Span(off, first, b, c * q, q, dtr[0], dtb[...], rate[...], taps)
    total = run[...] + sp.cum
    lead[0] = jnp.exp(total) * sp.kept_dev
    lead0[0, 0] = jnp.broadcast_to(jnp.exp(run[...]) * sp.carry_dev, (8, LANES))
    run[...] = total[q - 1 : q]

    def act(lo, hi):
        conv, _ = conv_block(
            pre[0, :, lo:hi].astype(F32), halo[:, lo:hi], cw[:, lo:hi], cb[:, lo:hi], sp.match
        )
        return conv * jax.nn.sigmoid(conv)

    write = act(inner, inner + n).astype(BF16)
    read = act(inner + n, inner + 2 * n).astype(BF16)
    rd[0] = read
    scores = mm(read, write, NT)
    write_t = write.astype(F32).T.astype(BF16)
    lane = lax.broadcasted_iota(jnp.int32, (1, LANES), 1)
    per = LANES // width
    for j in range(inner // LANES):
        lo, hi = j * LANES, (j + 1) * LANES
        h = j * per
        xs = act(lo, hi)
        xdt = xs * widen(sp.dt, h, lane, width)
        xdt_low = xdt.astype(BF16)
        mixed = None
        for i in range(per):
            part = mm((sp.fade(h + i) * scores).astype(BF16), xdt_low)
            mixed = part if mixed is None else jnp.where(lane >= i * width, part, mixed)
        old = state[:, lo:hi]
        st[0, 0, :, lo:hi] = old.astype(st.dtype)
        mixed = mixed + widen(sp.lead, h, lane, width) * mm(read, old.astype(BF16))
        y[0, :, lo:hi] = mixed + dsk[:, lo:hi] * xs
        fresh = mm(write_t, (xdt * widen(sp.tail, h, lane, width)).astype(BF16))
        new = widen(sp.lead[q - 1 : q], h, lane, width) * old + fresh
        state[:, lo:hi] = new
        fin[0, :, lo:hi] = new
    halo[...] = pre[0, q - 8 : q].astype(F32)


def gate_kernel(dims, y_in, rd, lead, lead0, st, s_in, z, gain, y, ygg, sq, st_full):
    q, inner, width, n = dims
    lane = lax.broadcasted_iota(jnp.int32, (1, LANES), 1)
    per = LANES // width
    total = jnp.zeros((q, LANES), F32)
    for j in range(inner // LANES):
        lo, hi = j * LANES, (j + 1) * LANES
        h = j * per
        came = s_in[0, :, lo:hi].astype(F32)
        full = st[0, 0, :, lo:hi].astype(F32) + widen(lead0[0, 0, 0:1], h, lane, width) * came
        st_full[0, 0, :, lo:hi] = full.astype(st_full.dtype)
        val = y_in[0, :, lo:hi] + widen(lead[0], h, lane, width) * mm(rd[0], came.astype(BF16))
        y[0, :, lo:hi] = val
        gate = z[0, :, lo:hi]
        gated = val * gate * jax.nn.sigmoid(gate)
        total = total + gated * gated
        ygg[0, :, lo:hi] = (gated * gain[:, lo:hi]).astype(BF16)
    sq[0] = jnp.broadcast_to(jnp.sum(total, axis=1, keepdims=True), (q, LANES))


def ungate_kernel(dims, count, dyn, y, z, stat, gain, rd, lead, dy, dz, yn, g_gain, g_state):
    b, c = pl.program_id(0), pl.program_id(1)

    @pl.when((b == 0) & (c == 0))
    def _():
        g_gain[...] = jnp.zeros_like(g_gain)

    @pl.when(c == 0)
    def _():
        g_state[...] = jnp.zeros_like(g_state)

    ungate_chunk(dims, count, dyn, y, z, stat, gain, rd, lead, dy, dz, yn, g_gain, g_state)


def ungate_chunk(dims, count, dyn, y, z, stat, gain, rd, lead, dy, dz, yn, g_gain, g_state):
    q, inner, width, n = dims
    lane = lax.broadcasted_iota(jnp.int32, (1, LANES), 1)
    per = LANES // width
    r2 = stat[0, :, 0:1]
    coef = r2 * r2 * r2 * stat[0, :, 1:2] * (1.0 / count)
    read_t = rd[0].astype(F32).T.astype(BF16)
    for j in range(inner // LANES):
        lo, hi = j * LANES, (j + 1) * LANES
        h = j * per
        gate = z[0, :, lo:hi]
        sig = jax.nn.sigmoid(gate)
        act = gate * sig
        val = y[0, :, lo:hi]
        gated = val * act
        dn = dyn[0, :, lo:hi]
        g = gain[:, lo:hi]
        norm = gated * r2
        g_gain[0:1, lo:hi] += jnp.sum(dn * norm, axis=0, keepdims=True)
        yn[0, :, lo:hi] = (norm * g).astype(BF16)
        d_gated = r2 * (dn * g) - gated * coef
        d_core = d_gated * act
        dy[0, :, lo:hi] = d_core
        dz[0, :, lo:hi] = (d_gated * val * silu_slope(gate, sig)).astype(BF16)
        g_state[0, :, lo:hi] += mm(read_t, (d_core * widen(lead[0], h, lane, width)).astype(BF16))


def back_kernel(dims, off, pos, pre, prev, rim, dtr, y, dy, st, d_in, *refs):
    acc, acc_head, d_state, carry = refs[-4:]
    b, c = pl.program_id(0), pl.program_id(1)
    at = pl.num_programs(1) - 1 - c

    @pl.when((b == 0) & (c == 0))
    def _():
        acc[...] = jnp.zeros_like(acc)
        acc_head[...] = jnp.zeros_like(acc_head)

    @pl.when(c == 0)
    def _():
        d_state[...] = d_in[0]
        carry[...] = jnp.zeros_like(carry)

    back_chunk(dims, b, at, c == 0, off, pos[0], pre, prev, rim, dtr, y, dy, st, *refs)


def back_chunk(dims, b, at, newest, off, first, pre, prev, rim, dtr, y, dy, st, cw, cb, dtb, rate, dsk,
               dcat, ddt_out, edge, rim_grad, acc, acc_head, d_state, carry):
    q, inner, width, n = dims
    taps = cw.shape[0]
    sp = Span(off, first, b, at * q, q, dtr[0], dtb[...], rate[...], taps)
    lane = lax.broadcasted_iota(jnp.int32, (1, LANES), 1)
    per = LANES // width

    def conv(lo, hi):
        ahead = jnp.where(at == 0, rim[0, :, lo:hi], prev[0, 8:16, lo:hi].astype(F32))
        return conv_block(pre[0, :, lo:hi].astype(F32), ahead, cw[:, lo:hi], cb[:, lo:hi], sp.match)

    def unconv(lo, hi, d_act, out, shifted, sig):
        d_conv = d_act * silu_slope(out, sig)
        acc[taps : taps + 1, lo:hi] += jnp.sum(d_conv, axis=0, keepdims=True)
        d_ext = None
        zeros = jnp.zeros((8, hi - lo), F32)
        for k in range(taps):
            acc[k : k + 1, lo:hi] += jnp.sum(d_conv * shifted[k], axis=0, keepdims=True)
            masked = cw[k : k + 1, lo:hi] * d_conv
            if k < taps - 1:
                masked = masked * sp.match[k]
            part = jnp.concatenate([zeros, masked], axis=0)
            if k < taps - 1:
                part = pltpu.roll(part, q + 8 - (taps - 1 - k), 0)
            d_ext = part if d_ext is None else d_ext + part
        d_pre = jnp.concatenate([d_ext[8:q], d_ext[q:] + carry[:, lo:hi]], axis=0)
        carry[:, lo:hi] = d_ext[0:8]
        rim_grad[0, :, lo:hi] = d_ext[0:8]
        dcat[0, :, lo:hi] = d_pre.astype(BF16)

        @pl.when(newest)
        def _():
            edge[0, :, lo:hi] = d_pre[q - 8 : q]

    w_conv, w_shift = conv(inner, inner + n)
    w_sig = jax.nn.sigmoid(w_conv)
    write = (w_conv * w_sig).astype(BF16)
    r_conv, r_shift = conv(inner + n, inner + 2 * n)
    r_sig = jax.nn.sigmoid(r_conv)
    read = (r_conv * r_sig).astype(BF16)
    scores = mm(read, write, NT)
    read_t = read.astype(F32).T.astype(BF16)
    d_scores = jnp.zeros((q, q), F32)
    d_write = jnp.zeros((q, n), F32)
    d_read = jnp.zeros((q, n), F32)
    d_cum = jnp.zeros((q, LANES), F32)
    d_step = jnp.zeros((q, LANES), F32)
    d_end = jnp.zeros((8, LANES), F32)
    for j in range(inner // LANES):
        lo, hi = j * LANES, (j + 1) * LANES
        h = j * per
        x_conv, x_shift = conv(lo, hi)
        x_sig = jax.nn.sigmoid(x_conv)
        xs = x_conv * x_sig
        step = widen(sp.dt, h, lane, width)
        xdt = xs * step
        xdt_low = xdt.astype(BF16)
        grad = dy[0, :, lo:hi]
        grad_low = grad.astype(BF16)
        core = y[0, :, lo:hi] - dsk[:, lo:hi] * xs
        late = d_state[:, lo:hi]
        late_low = late.astype(BF16)
        early = st[0, 0, :, lo:hi].astype(F32)
        tail = widen(sp.tail, h, lane, width)
        lead = widen(sp.lead, h, lane, width)
        u = None
        for i in range(per):
            fade = sp.fade(h + i)
            here = (lane >= i * width) & (lane < (i + 1) * width)
            own = jnp.where(here, grad, 0.0).astype(BF16)
            d_scores = d_scores + mm(own, xdt_low, NT) * fade
            part = mm((fade * scores).astype(BF16), grad_low, TN)
            u = part if u is None else jnp.where(lane >= i * width, part, u)
        from_end = tail * mm(write, late_low)
        inside = u
        u = u + from_end
        weighted = (lead * grad).astype(BF16)
        d_read = d_read + mm(weighted, early.astype(BF16), NT)
        d_write = d_write + mm((xdt * tail).astype(BF16), late_low, NT)
        end_lead = widen(sp.lead[q - 1 : q], h, lane, width)
        d_state[:, lo:hi] = end_lead * late + mm(read_t, weighted)
        head_of = (
            lax.broadcasted_iota(jnp.int32, (LANES, LANES), 0) // width + h
            == lax.broadcasted_iota(jnp.int32, (LANES, LANES), 1)
        ).astype(BF16)
        d_cum = d_cum + head_sums(
            grad_low.astype(F32) * core - xdt_low.astype(F32) * inside - xdt * from_end, head_of
        )
        d_step = d_step + head_sums(xs * u, head_of)
        end_row = end_lead * jnp.sum(late * early, axis=0, keepdims=True) + jnp.sum(
            xdt * from_end, axis=0, keepdims=True
        )
        d_end = d_end + head_sums(jnp.broadcast_to(end_row, (8, LANES)), head_of)
        acc[taps + 1 : taps + 2, lo:hi] += jnp.sum(grad * xs, axis=0, keepdims=True)
        unconv(lo, hi, step * u + dsk[:, lo:hi] * grad, x_conv, x_shift, x_sig)
    d_low = d_scores.astype(BF16)
    d_read = d_read + mm(d_low, write)
    d_write = d_write + mm(d_low, read, TN)
    unconv(inner, inner + n, d_write, w_conv, w_shift, w_sig)
    unconv(inner + n, inner + 2 * n, d_read, r_conv, r_shift, r_sig)
    d_decay = mm(sp.tri, d_cum, TN, precision=PRECISE) + d_end[0:1]
    acc_head[0:1] += jnp.sum(d_decay * sp.dt, axis=0, keepdims=True) * rate[...]
    d_dt = (d_step + d_decay * rate[...]) * jax.nn.sigmoid(sp.dt_in)
    acc_head[1:2] += jnp.sum(d_dt, axis=0, keepdims=True)
    ddt_out[0] = d_dt.astype(BF16)


def whole(shape):
    return pl.BlockSpec(shape, lambda *_: (0,) * len(shape))


def params():
    return pltpu.CompilerParams(vmem_limit_bytes=48 << 20)


def scan_forward(offs, pos, pre, rim, dtr, cw, cb, dtb, rate, dsk, width, n):
    nb, length, chans = pre.shape
    inner = dsk.shape[1]
    q = min(CHUNK, length)
    chunks = length // q
    dims = (q, inner, width, n)

    def rows(size):
        return pl.BlockSpec((1, q, size), lambda b, c, *_: (b, c, 0))

    return pl.pallas_call(
        functools.partial(scan_kernel, dims),
        grid_spec=pltpu.PrefetchScalarGridSpec(
            num_scalar_prefetch=2,
            grid=(nb, chunks),
            in_specs=[
                rows(chans),
                pl.BlockSpec((1, 8, chans), lambda b, c, *_: (b, 0, 0)),
                rows(LANES),
                whole(cw.shape),
                whole(cb.shape),
                whole(dtb.shape),
                whole(rate.shape),
                whole(dsk.shape),
            ],
            out_specs=[
                rows(inner),
                rows(n),
                rows(LANES),
                pl.BlockSpec((1, 1, n, inner), lambda b, c, *_: (b, c, 0, 0)),
                pl.BlockSpec((1, 1, 8, LANES), lambda b, c, *_: (b, c, 0, 0)),
                pl.BlockSpec((1, n, inner), lambda b, c, *_: (b, 0, 0)),
            ],
            scratch_shapes=[
                pltpu.VMEM((8, chans), F32),
                pltpu.VMEM((n, inner), F32),
                pltpu.VMEM((1, LANES), F32),
            ],
        ),
        out_shape=[
            jax.ShapeDtypeStruct((nb, length, inner), F32),
            jax.ShapeDtypeStruct((nb, length, n), BF16),
            jax.ShapeDtypeStruct((nb, length, LANES), F32),
            jax.ShapeDtypeStruct((nb, chunks, n, inner), F32),
            jax.ShapeDtypeStruct((nb, chunks, 8, LANES), F32),
            jax.ShapeDtypeStruct((nb, n, inner), F32),
        ],
        compiler_params=params(),
        name="scan_forward",
    )(offs, pos, pre, rim, dtr, cw, cb, dtb, rate, dsk)


def gate_forward(y_in, rd, lead, lead0, st, s_in, z, gain, width):
    nb, length, inner = y_in.shape
    chunks, n = st.shape[1], st.shape[2]
    q = length // chunks
    dims = (q, inner, width, n)

    def rows(size):
        return pl.BlockSpec((1, q, size), lambda b, c: (b, c, 0))

    def per_chunk(r, size):
        return pl.BlockSpec((1, 1, r, size), lambda b, c: (b, c, 0, 0))

    return pl.pallas_call(
        functools.partial(gate_kernel, dims),
        grid=(nb, chunks),
        in_specs=[
            rows(inner),
            rows(n),
            rows(LANES),
            per_chunk(8, LANES),
            per_chunk(n, inner),
            pl.BlockSpec((1, n, inner), lambda b, c: (b, 0, 0)),
            rows(inner),
            whole(gain.shape),
        ],
        out_specs=[rows(inner), rows(inner), rows(LANES), per_chunk(n, inner)],
        out_shape=[
            jax.ShapeDtypeStruct((nb, length, inner), F32),
            jax.ShapeDtypeStruct((nb, length, inner), BF16),
            jax.ShapeDtypeStruct((nb, length, LANES), F32),
            jax.ShapeDtypeStruct(st.shape, F32),
        ],
        compiler_params=params(),
        name="gate_forward",
    )(y_in, rd, lead, lead0, st, s_in, z, gain)


def gate_backward(dyn, y, z, stat, gain, rd, lead, width, count):
    nb, length, inner = y.shape
    n = rd.shape[2]
    q = min(CHUNK, length)
    chunks = length // q
    dims = (q, inner, width, n)

    def rows(size):
        return pl.BlockSpec((1, q, size), lambda b, c: (b, c, 0))

    return pl.pallas_call(
        functools.partial(ungate_kernel, dims, count),
        grid=(nb, chunks),
        in_specs=[
            rows(inner),
            rows(inner),
            rows(inner),
            rows(LANES),
            whole(gain.shape),
            rows(n),
            rows(LANES),
        ],
        out_specs=[
            rows(inner),
            rows(inner),
            rows(inner),
            whole((8, inner)),
            pl.BlockSpec((1, n, inner), lambda b, c: (b, 0, 0)),
        ],
        out_shape=[
            jax.ShapeDtypeStruct((nb, length, inner), F32),
            jax.ShapeDtypeStruct((nb, length, inner), BF16),
            jax.ShapeDtypeStruct((nb, length, inner), BF16),
            jax.ShapeDtypeStruct((8, inner), F32),
            jax.ShapeDtypeStruct((nb, n, inner), F32),
        ],
        compiler_params=params(),
        name="gate_backward",
    )(dyn, y, z, stat, gain, rd, lead)


def scan_backward(offs, pos, pre, rim, dtr, y, dy, st, d_in, cw, cb, dtb, rate, dsk, width):
    nb, length, chans = pre.shape
    inner = dsk.shape[1]
    chunks, n = st.shape[1], st.shape[2]
    q = length // chunks
    dims = (q, inner, width, n)
    per = q // 16

    def rows(size):
        return pl.BlockSpec((1, q, size), lambda b, c, *_: (b, chunks - 1 - c, 0))

    def per_seq(r, size):
        return pl.BlockSpec((1, r, size), lambda b, c, *_: (b, 0, 0))

    return pl.pallas_call(
        functools.partial(back_kernel, dims),
        grid_spec=pltpu.PrefetchScalarGridSpec(
            num_scalar_prefetch=2,
            grid=(nb, chunks),
            in_specs=[
                rows(chans),
                pl.BlockSpec(
                    (1, 16, chans), lambda b, c, *_: (b, jnp.maximum((chunks - 1 - c) * per - 1, 0), 0)
                ),
                per_seq(8, chans),
                rows(LANES),
                rows(inner),
                rows(inner),
                pl.BlockSpec((1, 1, n, inner), lambda b, c, *_: (b, chunks - 1 - c, 0, 0)),
                per_seq(n, inner),
                whole(cw.shape),
                whole(cb.shape),
                whole(dtb.shape),
                whole(rate.shape),
                whole(dsk.shape),
            ],
            out_specs=[
                rows(chans),
                rows(LANES),
                per_seq(8, chans),
                per_seq(8, chans),
                whole((8, chans)),
                whole((8, LANES)),
            ],
            scratch_shapes=[pltpu.VMEM((n, inner), F32), pltpu.VMEM((8, chans), F32)],
        ),
        out_shape=[
            jax.ShapeDtypeStruct((nb, length, chans), BF16),
            jax.ShapeDtypeStruct((nb, length, LANES), BF16),
            jax.ShapeDtypeStruct((nb, 8, chans), F32),
            jax.ShapeDtypeStruct((nb, 8, chans), F32),
            jax.ShapeDtypeStruct((8, chans), F32),
            jax.ShapeDtypeStruct((8, LANES), F32),
        ],
        compiler_params=params(),
        name="scan_backward",
    )(offs, pos, pre, pre, rim, dtr, y, dy, st, d_in, cw, cb, dtb, rate, dsk)


MESH = pl.DeviceIdType.MESH


def remote(src, dst, send, recv, **where):
    return pltpu.make_async_remote_copy(
        src_ref=src, dst_ref=dst, send_sem=send, recv_sem=recv, device_id=where, device_id_type=MESH
    )


class Line:
    def __init__(self, own, block, send, recv):
        self.own, self.block, self.send, self.recv = own, block, send, recv
        self.me = lax.axis_index("tp")
        self.peers = lax.axis_size("tp")

    def holds(self, k):
        for way, step in enumerate((1, -1)):
            slot = self.me - k * step
            held = (slot >= 0) & (slot < self.peers)
            yield held, way, jnp.clip(slot, 0, self.peers - 1)

    def parts(self, k):
        for held, way, slot in self.holds(k):
            there = self.me + (1, -1)[way]
            onward = held & (there >= 0) & (there < self.peers)
            here = self.own if k == 0 else self.block(slot)
            copy = remote(here, self.block(slot), self.send.at[way, k], self.recv.at[slot], tp=there)
            yield held, onward, copy

    def step(self, k):
        for held, onward, copy in self.parts(k):
            if k > 0:

                @pl.when(held)
                def _():
                    copy.wait_recv()

            @pl.when(onward)
            def _():
                copy.start()

    def finish(self):
        for k in range(self.peers - 1):
            for held, onward, copy in self.parts(k):

                @pl.when(onward)
                def _():
                    copy.wait_send()


def by_rows_of(size, total, body):
    @pl.loop(0, total // size)
    def _(i):
        body(pl.ds(pl.multiple_of(i * size, size), size))


def into_sum(mine, came):
    def body(rows):
        mine[rows, :] = (mine[rows, :].astype(F32) + came[rows, :].astype(F32)).astype(BF16)

    by_rows_of(32, mine.shape[0], body)


class Drain:
    def __init__(self, part, rows, wide, land, stage, send, recv, load):
        self.part, self.rows, self.wide, self.land, self.stage = part, rows, wide, land, stage
        self.send, self.recv, self.load = send, recv, load
        self.me = lax.axis_index("tp")
        self.peers = lax.axis_size("tp")

    def block(self, slot):
        return self.part.at[self.rows, pl.ds(pl.multiple_of(slot * self.wide, self.wide), self.wide)]

    def copy(self, way, slot):
        there = jnp.clip(self.me + (1, -1)[way], 0, self.peers - 1)
        return remote(
            self.block(slot), self.land.at[way, slot], self.send.at[way, slot], self.recv.at[way, slot], tp=there
        )

    def fetch(self, way, slot):
        return pltpu.make_async_copy(self.land.at[way, slot], self.stage.at[way], self.load.at[way])

    def add(self, way, slot):
        self.fetch(way, slot).wait()
        mine = self.block(slot)

        def body(rows):
            mine[rows, :] = (mine[rows, :].astype(F32) + self.stage[way, rows, :].astype(F32)).astype(BF16)

        by_rows_of(64, mine.shape[0], body)

    def ways(self, j):
        last = self.peers - 1
        for way, rank in ((0, self.me), (1, last - self.me)):
            behind = j - rank
            slot = last - behind if way == 0 else behind
            yield way, jnp.clip(slot, 0, last), behind >= 0, rank > 0

    def begin(self, way, slot, when):
        @pl.when(when)
        def _():
            self.copy(way, slot).wait_recv()
            self.fetch(way, slot).start()

    def source(self, j):
        for way, slot, sends, fed in self.ways(j):

            @pl.when(sends & jnp.logical_not(fed))
            def _():
                self.copy(way, slot).start()

    def relay(self, j):
        for way, slot, sends, fed in self.ways(j):
            self.begin(way, slot, sends & fed)
        for way, slot, sends, fed in self.ways(j):

            @pl.when(sends & fed)
            def _():
                self.add(way, slot)
                self.copy(way, slot).start()

    def round(self, j):
        self.source(j)
        self.relay(j)

    def close(self):
        fed = (self.me > 0, self.me < self.peers - 1)
        for way in range(2):
            self.begin(way, self.me, fed[way])
        for way in range(2):

            @pl.when(fed[way])
            def _():
                self.add(way, self.me)

    def finish(self):
        for j in range(self.peers - 1):
            for way, slot, sends, _ in self.ways(j):

                @pl.when(sends)
                def _():
                    self.copy(way, slot).wait_send()


class Fold:
    def __init__(self, theirs, block, land1, land2, land3, stage, half, send, recv, load):
        self.theirs, self.block, self.land1, self.land2, self.land3 = theirs, block, land1, land2, land3
        self.stage, self.half, self.send, self.recv, self.load = stage, half, send, recv, load
        self.ctx, self.fs = lax.axis_index("ctx"), lax.axis_index("fsdp")
        self.core, self.y = lax.rem(self.fs, 2), self.fs // 2

    def first(self, c, y):
        i = 2 * c + y
        mate = self.fs + 1 - 2 * self.core
        return remote(
            self.theirs(c, y), self.land1.at[i], self.send.at[i], self.recv.at[i], fsdp=mate
        )

    def part(self, ref, way):
        return ref.at[pl.ds(way * self.half, self.half)]

    def second(self, way, i):
        if way == 0:
            src, peer = self.block(i, 1 - self.y), {"fsdp": lax.rem(self.fs + 2, 4)}
        else:
            src, peer = self.block(1 - self.ctx, i), {"ctx": 1 - self.ctx}
        k = 4 + 2 * way + i
        return remote(self.part(src, way), self.land2.at[way, i], self.send.at[k], self.recv.at[k], **peer)

    def third(self, way):
        if way == 0:
            src, peer = self.block(1 - self.ctx, self.y), {"ctx": 1 - self.ctx}
        else:
            src, peer = self.block(self.ctx, 1 - self.y), {"fsdp": lax.rem(self.fs + 2, 4)}
        k = 8 + way
        return remote(self.part(src, way), self.land3.at[way], self.send.at[k], self.recv.at[k], **peer)

    def gather(self, parts):
        def fetch(i):
            _, land, mine = parts[i]
            stage = self.stage.at[i % 2, pl.ds(0, mine.shape[0]), pl.ds(0, mine.shape[1])]
            return pltpu.make_async_copy(land, stage, self.load.at[i % 2]), stage

        for i in range(len(parts) + 1):
            if i < len(parts):
                parts[i][0].wait_recv()
                fetch(i)[0].start()
            if i:
                copy, stage = fetch(i - 1)
                copy.wait()
                mine = parts[i - 1][2]
                into_sum(mine, stage)

    def one(self):
        self.gather(
            [
                (self.first(c, y), self.land1.at[2 * c + y], self.block(c, y))
                for c in range(2)
                for y in range(2)
            ]
        )
        for way in range(2):
            for i in range(2):
                self.second(way, i).start()

    def two(self):
        self.gather(
            [
                (self.second(0, i), self.land2.at[0, i], self.part(self.block(i, self.y), 0))
                for i in range(2)
            ]
            + [
                (self.second(1, i), self.land2.at[1, i], self.part(self.block(self.ctx, i), 1))
                for i in range(2)
            ]
        )
        for way in range(2):
            self.third(way).start()

    def three(self):
        own = self.block(self.ctx, self.y)
        self.gather([(self.third(way), self.land3.at[way], self.part(own, way)) for way in range(2)])
        return own

    def sent(self):
        for i in range(2):
            for y in range(2):
                self.first(i, y).wait_send()

    def finish(self):
        for i in range(2):
            self.second(0, i).wait_send()
            self.second(1, i).wait_send()
            self.third(i).wait_send()


IN = ["off", "x", "cot", "wx_in", "wz_in", "wo_in", "wbc_in", "wdt_in"]
IN += ["gain_in", "conv_w", "conv_b", "dt_bias", "a_log", "d_skip", "norm_gain"]


def layer_kernel(dims, names, *refs):
    r = types.SimpleNamespace(**dict(zip(names, refs)))
    nb, length, q, inner, width, n, d, inner_all, hpd = dims
    chunks = length // q
    tokens = nb * length
    chans = inner + 2 * n
    extra = 2 * n + LANES
    ctx, tp, fs = lax.axis_index("ctx"), lax.axis_index("tp"), lax.axis_index("fsdp")
    tps = lax.axis_size("tp")
    wide = d // tps
    deep = r.wx_in.shape[0]
    bd = d // 8
    core, yy = lax.rem(fs, 2), fs // 2
    mate = fs + 1 - 2 * core
    over = lax.rem(fs + 2, 4)
    other = 1 - ctx
    first = ctx * length
    small = (q, inner, width, n)
    dims_mode = (r.cw, r.cb, r.dtb, r.rate, r.dsk)

    def greet(**where):
        pl.semaphore_signal(barrier, inc=1, device_id=where, device_id_type=MESH)

    barrier = pltpu.get_barrier_semaphore()
    for step in range(1, tps):
        greet(tp=lax.rem(tp + step, tps))
    for c in range(2):
        for step in range(4):
            if c or step:
                greet(ctx=lax.rem(ctx + c, 2), fsdp=lax.rem(fs + step, 4))
    pl.semaphore_wait(barrier, tps - 1 + 7)

    def seq(m):
        return pl.ds(m * length, length)

    def one(ref, m):
        return ref.at[pl.ds(m, 1)]

    def span(ref, m, rows):
        return ref.at[pl.ds(m, 1), rows]

    def convolved(m, rows):
        return r.pre.at[pl.ds(m, 1), rows, pl.ds(0, chans)]

    def chunk_rows(c):
        return pl.ds(pl.multiple_of(c * q, q), q)

    mine = pl.ds(pl.multiple_of(tp * wide, wide), wide)
    own_pos = pl.ds(pl.multiple_of(fs * deep, deep), deep)
    rows_bc = r.wbc_in.shape[0]
    tight = 2 * n + hpd

    def features(ref, m):
        return lambda at: ref.at[seq(m), pl.ds(pl.multiple_of(at * wide, wide), wide)]

    def own(ref, m):
        return ref.at[seq(m)]

    x_lines = [Line(own(r.x, m), features(r.x_all, m), r.xs_send.at[m], r.xs_recv.at[m]) for m in range(nb)]
    c_lines = [Line(own(r.cot, m), features(r.cot_o, m), r.cs_send.at[m], r.cs_recv.at[m]) for m in range(nb)]
    bc_rows = pl.ds(pl.multiple_of(tp * rows_bc, rows_bc), rows_bc)

    def bc_in_copy(step):
        there = lax.rem(tp + step, tps)
        return remote(
            r.wbc_in, r.wst.at[bc_rows, own_pos], r.v_send.at[step], r.v_recv.at[tp], tp=there
        )

    def bc_in_recv(step):
        there = lax.rem(tp + step, tps)
        rows = pl.ds(pl.multiple_of(there * rows_bc, rows_bc), rows_bc)
        remote(
            r.wbc_in, r.wst.at[rows, own_pos], r.v_send.at[step], r.v_recv.at[there], tp=there
        ).wait_recv()

    def slot(w, at):
        rows = pl.ds(pl.multiple_of(at * deep, deep), deep)
        return (r.wx.at[rows], r.wz.at[rows], r.wo.at[:, rows], r.wst.at[pl.ds(0, tight), rows])[w]

    owns = (r.wx_in, r.wz_in, r.wo_in, slot(3, fs))

    def near(w):
        return remote(owns[w], slot(w, fs), r.w_send.at[w, 0], r.w_recv.at[w, fs], fsdp=mate)

    def far(w):
        return remote(owns[w], slot(w, fs), r.w_send.at[w, 1], r.w_recv.at[w, fs], fsdp=over)

    def relay(w):
        return remote(slot(w, over), slot(w, over), r.w_send.at[w, 2], r.w_recv.at[w, over], fsdp=mate)

    def arrive(w, at):
        remote(slot(w, at), slot(w, at), r.w_send.at[w, 0], r.w_recv.at[w, at], fsdp=mate).wait_recv()

    locals_ = [pltpu.make_async_copy(owns[w], slot(w, fs), r.loc.at[w]) for w in range(3)]
    locals_.append(pltpu.make_async_copy(r.x, r.x_all.at[:, mine], r.loc.at[3]))
    locals_.append(pltpu.make_async_copy(r.cot, r.cot_o.at[:, mine], r.loc.at[4]))
    locals_.append(pltpu.make_async_copy(r.wbc_in, r.wst.at[bc_rows, own_pos], r.loc.at[5 + nb]))
    locals_.append(pltpu.make_async_copy(r.wdt_in, r.wst.at[pl.ds(2 * n, hpd), own_pos], r.loc.at[6 + nb]))

    def pass_on(w):
        arrive(w, over)
        relay(w).start()

    def whole_weight(w):
        arrive(w, mate)
        arrive(w, lax.rem(mate + 2, 4))
        if w < 3:
            locals_[w].wait()

    def prepare():
        lane = lax.broadcasted_iota(jnp.int32, (8, LANES), 1)
        chan = pl.ds(pl.multiple_of(tp * inner, inner), inner)
        r.cw[:, :inner] = r.conv_w[:, chan]
        r.cw[:, inner:] = r.conv_w[:, inner_all:]
        r.cb[:, :inner] = r.conv_b[:, chan]
        r.cb[:, inner:] = r.conv_b[:, inner_all:]
        r.gain[...] = r.norm_gain[:, chan]

        def own_heads(ref):
            wide_row = jnp.concatenate([ref[...], jnp.zeros((1, LANES - ref.shape[1]), F32)], axis=1)
            turned = pltpu.roll(jnp.broadcast_to(wide_row, (8, LANES)), lax.rem(LANES - tp * hpd, LANES), 1)
            return jnp.where(lane < hpd, turned, 0.0)

        r.dtb[...] = own_heads(r.dt_bias)[0:1]
        r.rate[...] = jnp.where(lane < hpd, -jnp.exp(own_heads(r.a_log)), 0.0)[0:1]
        head_of = (
            lax.broadcasted_iota(jnp.int32, (LANES, inner), 0)
            == lax.broadcasted_iota(jnp.int32, (LANES, inner), 1) // width
        ).astype(F32)
        r.dsk[...] = mm(own_heads(r.d_skip), head_of, precision=PRECISE)[0:1]
        r.wst[tight:, :] = jnp.zeros((LANES - hpd, d), BF16)
        for ref in (r.g_gain, r.g_in, r.acc, r.acc_head):
            ref[...] = jnp.zeros_like(ref)

    def norm(m):
        @pl.loop(0, chunks)
        def _(i):
            rows = pl.ds(pl.multiple_of(m * length + i * q, q), q)
            total = jnp.zeros((q, LANES), F32)
            for j in range(d // LANES):
                v = r.x_all[rows, j * LANES : (j + 1) * LANES].astype(F32)
                total = total + v * v
            inv = lax.rsqrt(jnp.sum(total, axis=1, keepdims=True) * (1.0 / d) + EPSILON)
            r.r1[rows, :] = jnp.broadcast_to(inv, (q, LANES))
            for j in range(d // LANES):
                cols = slice(j * LANES, (j + 1) * LANES)
                r.xn[rows, cols] = (r.x_all[rows, cols].astype(F32) * inv * r.gain_in[:, cols]).astype(BF16)

    tile = min(2 * LANES, inner)

    def tiles(total, body, size=tile):
        @pl.loop(0, total // size)
        def _(j):
            body(pl.ds(pl.multiple_of(j * size, size), size))

    def rim_copy(m):
        return remote(
            r.pre.at[m, pl.ds(length - 16, 16), pl.ds(0, chans)], r.rim16.at[m], r.r_send.at[m], r.r_recv.at[m], ctx=other
        )

    def project_x(m):
        for half in (1, 0):
            size = length // 2
            rows = pl.ds(m * length + half * size, size)
            here = pl.ds(half * size, size)
            both = mm(r.xn[rows, :], r.wst[...], NT)
            r.dtr[m, here, :] = both[:, 2 * n :]
            r.pre[m, here, inner:chans] = both[:, : 2 * n].astype(BF16)

            def body(cols):
                r.pre[m, here, cols] = mm(r.xn[rows, :], r.wx[:, cols]).astype(BF16)

            tiles(inner, body)
            if half == 1:

                @pl.when(ctx == 0)
                def _():
                    rim_copy(m).start()

    def project_z(m):
        def body(cols):
            r.z[m, :, cols] = mm(r.xn[seq(m), :], r.wz[:, cols])

        tiles(inner, body)

    def get_rim(m):
        @pl.when(ctx == 1)
        def _():
            rim_copy(m).wait_recv()
            r.rim[m] = r.rim16[m, 8:16].astype(F32)

        @pl.when(ctx == 0)
        def _():
            r.rim[m] = jnp.zeros_like(r.rim[m])

    def scan(m):
        @pl.loop(0, chunks)
        def _(c):
            rows = chunk_rows(c)
            scan_chunk(
                small, m, c, r.off, first,
                convolved(m, rows), one(r.rim, m), span(r.dtr, m, rows), *dims_mode,
                span(r.y, m, rows), span(r.rd, m, rows), span(r.lead, m, rows),
                r.st.at[pl.ds(m, 1), pl.ds(c, 1)], r.lead0.at[pl.ds(m, 1), pl.ds(c, 1)], one(r.fin, 0),
                r.halo, r.state, r.run,
            )

    def state_copy(m, back):
        return remote(
            r.left.at[m], r.came.at[back, m], r.s_send.at[back, m], r.s_recv.at[back, m], ctx=other
        )

    def send_state(m, back):
        @pl.when(ctx == back)
        def _():
            if back == 0:
                rim_copy(m).wait_send()
            r.left[m] = r.fin[0].astype(BF16)
            state_copy(m, back).start()

    def get_state(m, back):
        @pl.when(ctx == 1 - back)
        def _():
            state_copy(m, back).wait_recv()

        @pl.when(ctx == back)
        def _():
            r.came[back, m] = jnp.zeros_like(r.came[back, m])

    def gate(m):
        @pl.loop(0, chunks)
        def _(c):
            rows = chunk_rows(c)
            sts = r.st.at[pl.ds(m, 1), pl.ds(c, 1)]
            ys = span(r.y, m, rows)
            gate_kernel(
                small, ys, span(r.rd, m, rows), span(r.lead, m, rows),
                r.lead0.at[pl.ds(m, 1), pl.ds(c, 1)], sts, r.came.at[0, pl.ds(m, 1)], span(r.z, m, rows), r.gain,
                ys, span(r.yn, m, rows), span(r.sq, m, rows), sts,
            )

    def project_out(m):
        def body(cols):
            r.part[seq(m), cols] = mm(r.yn[m], r.wo[:, cols]).astype(BF16)

        tiles(d, body, 2 * LANES)

    def drains(part, land, send, recv):
        return [
            Drain(part, seq(m), wide, land.at[m], r.stage, send.at[m], recv.at[m], r.load.at[0])
            for m in range(nb)
        ]

    o_drains = drains(r.part, r.o_land, r.od_send, r.od_recv)
    d_drains = drains(r.part, r.d_land, r.dd_send, r.dd_recv)

    def stat_copy(m, kind, there):
        return remote(
            r.stat_out.at[kind, m], r.stat_in.at[kind, m, tp],
            r.t_send.at[kind, m, there], r.t_recv.at[kind, m, tp], tp=there,
        )

    def send_stat(m, kind, columns):
        lane = lax.broadcasted_iota(jnp.int32, (1, LANES), 1)
        both = jnp.where(lane == 0, columns[0], columns[-1])
        rows = both.T[0:8]
        r.stat_out[kind, m] = rows
        r.stat_in[kind, m, tp] = rows
        for step in range(1, tps):
            stat_copy(m, kind, lax.rem(tp + step, tps)).start()

    def get_stat(m, kind):
        for step in range(1, tps):
            there = lax.rem(tp + step, tps)
            remote(
                r.stat_out.at[kind, m], r.stat_in.at[kind, m, there],
                r.t_send.at[kind, m, there], r.t_recv.at[kind, m, there], tp=there,
            ).wait_recv()
        total = r.stat_in[kind, m, 0]
        for i in range(1, tps):
            total = total + r.stat_in[kind, m, i]
        full = jnp.concatenate([total, jnp.zeros((LANES - 8, length), F32)], axis=0)
        return full.T

    def load_cot(m, at):
        cols = pl.ds(pl.multiple_of(at * wide, wide), wide)
        return pltpu.make_async_copy(
            r.cot_o.at[seq(m), cols], r.x_all.at[seq(m), cols], r.cot_load.at[m, at]
        )

    def c_step(m, k):
        c_lines[m].step(k)
        for held, _, slot in c_lines[m].holds(k):

            @pl.when(held)
            def _():
                load_cot(m, slot).start()

    def whole_cot(m):
        for at in range(tps):
            load_cot(m, at).wait()

    def d_gate(m):
        def body(cols):
            r.dyn[0, :, cols] = mm(r.x_all[seq(m), :], r.wo[cols, :], NT)

        tiles(inner, body)

        def dot(rows):
            total = jnp.zeros((64, LANES), F32)
            for lo in range(0, inner, LANES):
                cols = slice(lo, lo + LANES)
                gate_in = r.z[m, rows, cols]
                gated = r.y[m, rows, cols] * gate_in * jax.nn.sigmoid(gate_in)
                total = total + r.dyn[0, rows, cols] * r.gain[:, cols] * gated
            r.dots[rows, :] = jnp.broadcast_to(jnp.sum(total, axis=1, keepdims=True), (64, LANES))

        by_rows_of(64, length, dot)
        send_stat(m, 0, [r.sq[m], r.dots[...]])

    def ungate(m):
        full = get_stat(m, 0)
        lane = lax.broadcasted_iota(jnp.int32, (1, LANES), 1)
        r.sq[m] = jnp.where(lane == 0, lax.rsqrt(full * (1.0 / inner_all) + EPSILON), full)
        r.fin[...] = jnp.zeros_like(r.fin)

        @pl.loop(0, chunks)
        def _(c):
            rows = chunk_rows(c)
            zs = span(r.z, m, rows)
            ungate_chunk(
                small, inner_all, r.dyn.at[:, rows], span(r.y, m, rows), zs, span(r.sq, m, rows), r.gain,
                span(r.rd, m, rows), span(r.lead, m, rows),
                zs, span(r.dz, m, rows), span(r.yn, m, rows), r.g_gain, one(r.fin, 0),
            )

        send_state(m, 1)

    def back(m, after):
        r.d_state[...] = r.came[1, m].astype(F32)
        r.carry[...] = jnp.zeros_like(r.carry)

        @pl.loop(0, chunks)
        def _(c):
            at = chunks - 1 - c
            rows = chunk_rows(at)
            ahead = pl.ds(pl.multiple_of(jnp.maximum(at * q - 16, 0), 16), 16)
            here = convolved(m, rows)
            back_chunk(
                small, m, at, c == 0, r.off, first, here, convolved(m, ahead), one(r.rim, m),
                span(r.dtr, m, rows), span(r.y, m, rows), span(r.z, m, rows),
                r.st.at[pl.ds(m, 1), pl.ds(at, 1)], *dims_mode,
                here, r.pre.at[pl.ds(m, 1), rows, pl.ds(chans, LANES)], one(r.edge, m), one(r.rim_out, m),
                r.acc, r.acc_head, r.d_state, r.carry,
            )
            for k, hook in after.items():
                pl.when(c == k)(hook)

        @pl.when(ctx == 1)
        def _():
            edge_copy(m).start()

    def edge_copy(m):
        return remote(r.rim_out.at[m], r.rim_in.at[m], r.e_send.at[m], r.e_recv.at[m], ctx=other)

    def patch(m):
        @pl.when(ctx == 0)
        def _():
            edge_copy(m).wait_recv()
            rows = pl.ds(length - 16, 16)
            late = (r.edge[m] + r.rim_in[m]).astype(BF16).astype(F32)
            both = jnp.concatenate([r.pre[m, rows, :chans].astype(F32)[0:8], late], axis=0)
            r.pre[m, rows, :chans] = both.astype(BF16)

    def d_norm(m, at):
        size = min(2 * LANES, wide)

        @pl.loop(0, wide // size)
        def _(j):
            cols = pl.ds(pl.multiple_of(at * wide + j * size, size), size)
            total = mm(r.dz[m], r.wz[cols, :], NT) + mm(r.pre[m, :, :inner], r.wx[cols, :], NT)
            total = total + mm(r.pre[m, :, inner:], r.wst[:, cols])
            r.part[seq(m), cols] = total.astype(BF16)
            prod = total * r.xn[seq(m), cols].astype(F32)
            r.g_in[0:1, cols] += jnp.sum(prod, axis=0, keepdims=True)
            lanes = r.dots[...]
            for lo in range(0, size, LANES):
                lanes = lanes + prod[:, lo : lo + LANES]
            r.dots[...] = lanes

    def send_dots(m):
        dot = jnp.sum(r.dots[...], axis=1, keepdims=True)
        send_stat(m, 1, [jnp.broadcast_to(dot, (length, LANES))])

    def rb(c, y, k):
        return 4 * c + 2 * y + k

    def by_rows(ref, k):
        return lambda c, y: ref.at[pl.ds(pl.multiple_of((2 * y + k) * bd, bd), bd), pl.ds(c * inner, inner)]

    def folds(i, theirs, block, lands):
        return Fold(theirs, block, *lands, r.stage_z, bd // 2, r.f_send.at[i], r.f_recv.at[i], r.load.at[1])

    fold_o = folds(0, by_rows(r.wo, 1 - core), by_rows(r.wo, core), (r.o1, r.o2, r.o3))
    fold_z = folds(1, by_rows(r.x_all, 1 - core), by_rows(r.x_all, core), (r.z1, r.z2, r.z3))
    fold_x = folds(
        2,
        by_rows(r.wo, 1 - core),
        lambda c, y: r.yn.at[c, pl.ds(pl.multiple_of(y * bd, bd), bd)],
        (r.x1, r.x2, r.x3),
    )
    fold_s = folds(3, lambda c, y: r.gs.at[c, y, 1], lambda c, y: r.gs.at[c, y, 0], (r.s1, r.s2, r.s3))

    def xn_cols(c, y, k):
        return r.xn[:, pl.ds(pl.multiple_of(rb(c, y, k) * bd, bd), bd)]

    def grad_o(c, y, k, into):
        cot = r.x_all[:, pl.ds(pl.multiple_of(rb(c, y, k) * bd, bd), bd)]
        into[0][...] = mm(cot, r.yn[...].reshape(tokens, inner), TN).astype(BF16)

    def grad_z(c, y, k, into):
        into[0][...] = mm(xn_cols(c, y, k), r.dz[...].reshape(tokens, inner), TN).astype(BF16)

    def grad_x(c, y, k, into):
        left = xn_cols(c, y, k)
        into[0][...] = mm(left, r.pre[:, :, :inner].reshape(tokens, inner), TN).astype(BF16)
        into[1][...] = mm(left, r.pre[:, :, inner:].reshape(tokens, extra), TN).astype(BF16)

    def send_grads(make, *fold):
        for c in range(2):
            for y in range(2):
                make(c, y, 1 - core, [f.theirs(c, y) for f in fold])
                for f in fold:
                    f.first(c, y).start()

    def own_grads(make, *fold):
        for c in range(2):
            for y in range(2):
                make(c, y, core, [f.block(c, y) for f in fold])

    out_copies = []

    def keep(pair):
        out_copies.append(pair)
        kept(len(out_copies) - 1).start()

    waited = []

    def settle(i):
        kept(i).wait()
        waited.append(i)

    def kept(i):
        return pltpu.make_async_copy(*out_copies[i](), r.outs.at[i])

    def give_out(m):
        o_drains[m].close()
        keep(lambda: (r.part.at[seq(m), mine], r.out.at[seq(m)]))
        keep(lambda: (r.sq.at[m], r.stat.at[seq(m)]))

    def give_dx(m):
        d_drains[m].close()
        keep(lambda: (r.part.at[seq(m), mine], r.dx.at[seq(m)]))

    def give_dots(m):
        lane = lax.broadcasted_iota(jnp.int32, (1, LANES), 1)
        dot = get_stat(m, 1)[:, 0:1]
        r.lead[m] = jnp.where(lane == 0, r.r1[seq(m), :], dot)
        keep(lambda: (r.lead.at[m], r.stat2.at[seq(m)]))

    def device(j):
        c, s = j // 4, j % 4
        return lax.rem(ctx + c, 2), lax.rem(fs + s, 4)

    def tiny_copy(j):
        c, f = device(j)
        return remote(
            r.tiny.at[:], r.tiny_in.at[4 * ctx + fs], r.y_send.at[j], r.y_recv.at[4 * ctx + fs], ctx=c, fsdp=f
        )

    def tiny_recv(j):
        c, f = device(j)
        at = 4 * c + f
        remote(r.tiny.at[:], r.tiny_in.at[at], r.y_send.at[j], r.y_recv.at[at], ctx=c, fsdp=f).wait_recv()

    def spread_copy(step):
        there = lax.rem(tp + step, tps)
        return remote(r.tiny_sum.at[:], r.tiny_all.at[tp], r.q_send.at[step], r.q_recv.at[tp], tp=there)

    def bc_copy(step):
        there = lax.rem(tp + step, tps)
        rows = pl.ds(pl.multiple_of(there * rows_bc, rows_bc), rows_bc)
        return remote(r.bc_sum.at[rows], r.bc_all.at[tp], r.b_send.at[step], r.b_recv.at[tp], tp=there)

    x_0, x_1 = x_lines
    c_0, c_1 = c_lines
    o_0, o_1 = o_drains
    d_0, d_1 = d_drains
    last = tps - 1

    def steps(line, lo, hi=tps):
        for k in range(lo, hi):
            line.step(k)

    def rounds(drain, lo, hi=last):
        for j in range(lo, hi):
            drain.round(j)

    for step in range(1, tps):
        bc_in_copy(step).start()
    x_0.step(0)
    far(0).start()
    near(0).start()
    for copy in locals_:
        copy.start()
    prepare()
    for step in range(1, tps):
        bc_in_recv(step)
    locals_[5].wait()
    locals_[6].wait()
    for w in (3, 1, 2):
        far(w).start()
        near(w).start()
    steps(x_0, 1, last)
    pass_on(3)
    pass_on(0)
    c_0.step(0)
    steps(x_0, last)
    locals_[3].wait()
    norm(0)
    whole_weight(0)
    whole_weight(3)
    project_x(0)
    get_rim(0)
    scan(0)
    send_state(0, 0)
    locals_[4].wait()
    x_0.finish()
    load_cot(0, tp).start()
    c_step(0, 1)
    pass_on(1)
    whole_weight(1)
    project_z(0)
    get_state(0, 0)
    gate(0)
    c_step(0, 2)
    x_1.step(0)
    pass_on(2)
    whole_weight(2)
    for k in range(3, tps):
        c_step(0, k)
    whole_cot(0)
    d_gate(0)
    x_1.step(1)
    project_out(0)
    ungate(0)
    o_0.source(0)
    x_1.step(2)
    c_1.step(0)
    get_state(0, 1)

    def middle_0():
        o_0.round(1)

    def middle_1():
        steps(x_1, 3)
        norm(1)
        project_x(1)
        get_rim(1)
        x_1.finish()
        load_cot(1, tp).start()
        c_step(1, 1)
        o_0.source(2)
        scan(1)
        send_state(1, 0)
        project_z(1)
        get_state(1, 0)
        gate(1)
        c_step(1, 2)
        project_out(1)

    def middle_2():
        o_0.relay(2)
        o_1.source(0)

    back(0, {0: middle_0, 1: middle_1, 2: middle_2})
    for k in range(3, tps):
        c_step(1, k)
    whole_cot(1)
    d_gate(1)
    o_1.source(1)
    ungate(1)
    give_out(0)
    o_0.finish()
    patch(0)
    r.dots[...] = jnp.zeros_like(r.dots)
    settle(0)
    o_1.relay(1)
    d_norm(0, last)
    d_norm(0, 0)
    o_1.source(2)
    for k in range(1, last):
        d_norm(0, last - k)
    send_dots(0)
    get_state(1, 1)

    def late_0():
        o_1.relay(2)
        relay(2).wait_send()
        send_grads(grad_o, fold_o)
        d_0.source(0)
        own_grads(grad_o, fold_o)
        fold_o.one()

    def late_1():
        send_grads(grad_z, fold_z)
        own_grads(grad_z, fold_z)
        d_0.source(1)
        d_0.relay(1)
        fold_z.one()

    def late_2():
        d_0.source(2)
        give_out(1)

    back(1, {0: late_0, 1: late_1, 2: late_2})
    d_0.relay(2)
    fold_o.two()
    o_1.finish()
    r.dots[...] = jnp.zeros_like(r.dots)
    settle(2)
    fold_o.sent()
    patch(1)
    d_norm(1, last)
    d_norm(1, 0)
    d_1.round(0)
    send_grads(grad_x, fold_x, fold_s)
    fold_z.two()
    own_grads(grad_x, fold_x, fold_s)
    for k in range(1, last):
        d_norm(1, last - k)
    d_1.round(1)
    fold_s.one()
    fold_x.one()
    send_dots(1)
    fold_o.three()
    keep(lambda: (fold_o.block(ctx, yy), r.go))
    taps = r.cw.shape[0]
    head_of = (
        lax.broadcasted_iota(jnp.int32, (inner, LANES), 0) // width
        == lax.broadcasted_iota(jnp.int32, (inner, LANES), 1)
    ).astype(F32)
    skip = mm(r.acc[:, :inner], head_of, precision=PRECISE)[taps + 1 : taps + 2]
    r.tiny[...] = r.acc[...]
    r.tiny[5:6, :inner] = r.g_gain[0:1]
    for i in range(d // inner):
        r.tiny[6 + i : 7 + i, :inner] = r.g_in[0:1, i * inner : (i + 1) * inner]
    r.tiny[5:7, inner : inner + LANES] = r.acc_head[0:2]
    r.tiny[7:8, inner : inner + LANES] = skip
    for j in range(1, 8):
        tiny_copy(j).start()
    r.tiny_in[4 * ctx + fs] = r.tiny[...]
    rounds(d_1, 2)
    give_dx(0)
    give_dots(0)
    fold_z.three()
    keep(lambda: (fold_z.block(ctx, yy), r.gz))
    fold_s.two()
    fold_x.two()
    for j in range(1, 8):
        tiny_recv(j)
    total = r.tiny_in[0]
    for i in range(1, 8):
        total = total + r.tiny_in[i]
    r.tiny_sum[...] = total
    r.tiny_all[tp] = total
    for step in range(1, tps):
        spread_copy(step).start()
    give_dots(1)
    sums = fold_s.three()
    r.gdt[...] = sums[:, 2 * n :].astype(F32).T[:hpd]
    for lo in range(0, 2 * n, LANES):
        r.bc_sum[lo : lo + LANES, :] = sums[:, lo : lo + LANES].astype(F32).T.astype(BF16)
    r.bc_all[tp] = r.bc_sum[pl.ds(pl.multiple_of(tp * rows_bc, rows_bc), rows_bc), :]
    for step in range(1, tps):
        bc_copy(step).start()
    give_dx(1)
    fold_x.three()
    keep(lambda: (fold_x.block(ctx, yy), r.gx))
    for step in range(1, tps):
        there = lax.rem(tp + step, tps)
        remote(
            r.bc_sum.at[pl.ds(0, rows_bc)], r.bc_all.at[there], r.b_send.at[step], r.b_recv.at[there], tp=there
        ).wait_recv()
    total = r.bc_all[0].astype(F32)
    for i in range(1, tps):
        total = total + r.bc_all[i].astype(F32)
    r.gbc[...] = total
    for step in range(1, tps):
        there = lax.rem(tp + step, tps)
        remote(r.tiny_sum.at[:], r.tiny_all.at[there], r.q_send.at[step], r.q_recv.at[there], tp=there).wait_recv()
    keep(lambda: (r.tiny_all, r.tiny_o))

    for step in range(1, tps):
        bc_in_copy(step).wait_send()
    for line in c_lines + d_drains:
        line.finish()
    fold_o.finish()
    for fold in (fold_z, fold_x, fold_s):
        fold.sent()
        fold.finish()
    for w in range(4):
        near(w).wait_send()
        far(w).wait_send()
        if w != 2:
            relay(w).wait_send()
    for m in range(nb):
        for kind in range(2):
            for step in range(1, tps):
                stat_copy(m, kind, lax.rem(tp + step, tps)).wait_send()

        @pl.when(ctx == 0)
        def _():
            state_copy(m, 0).wait_send()

        @pl.when(ctx == 1)
        def _():
            state_copy(m, 1).wait_send()
            edge_copy(m).wait_send()

    for j in range(1, 8):
        tiny_copy(j).wait_send()
    for step in range(1, tps):
        spread_copy(step).wait_send()
        bc_copy(step).wait_send()
    for i in range(len(out_copies)):
        if i not in waited:
            kept(i).wait()


SMALL = ["gdt", "gbc"]


def layer(args, nb, length, inner_dev_heads, width, n, tps, inner_all):
    offs, x, cot, wx = args[:4]
    hpd = inner_dev_heads
    tokens, wide = x.shape
    d = wide * tps
    inner = wx.shape[1]
    chans = inner + 2 * n
    extra = 2 * n + LANES
    q = min(CHUNK, length)
    chunks = length // q
    bd = d // 8
    dims = (nb, length, q, inner, width, n, d, inner_all, hpd)
    taps = args[9].shape[0]
    sds = jax.ShapeDtypeStruct
    outs = dict(
        out=((tokens, wide), BF16), dx=((tokens, wide), BF16), gz=((bd, inner), BF16), gx=((bd, inner), BF16),
        stat=((tokens, LANES), F32), stat2=((tokens, LANES), F32),
        gdt=((hpd, bd), F32), gbc=((2 * n // tps, bd), F32), go=((bd, inner), BF16),
        tiny_o=((tps, 8, chans), F32),
        cot_o=((tokens, d), BF16),
        o_land=((nb, 2, tps, length, wide), BF16), d_land=((nb, 2, tps, length, wide), BF16),
        o1=((4, bd, inner), BF16), o2=((2, 2, bd // 2, inner), BF16), o3=((2, bd // 2, inner), BF16),
        z1=((4, bd, inner), BF16), z2=((2, 2, bd // 2, inner), BF16), z3=((2, bd // 2, inner), BF16),
        x1=((4, bd, inner), BF16), x2=((2, 2, bd // 2, inner), BF16), x3=((2, bd // 2, inner), BF16),
        s1=((4, bd, extra), BF16), s2=((2, 2, bd // 2, extra), BF16), s3=((2, bd // 2, extra), BF16),
    )
    vmem = dict(
        x_all=((tokens, d), BF16), xn=((tokens, d), BF16), r1=((tokens, LANES), F32),
        pre=((nb, length, chans + LANES), BF16), dtr=((nb, length, LANES), F32), z=((nb, length, inner), F32),
        y=((nb, length, inner), F32), rd=((nb, length, n), BF16), lead=((nb, length, LANES), F32),
        st=((nb, chunks, n, inner), BF16), lead0=((nb, chunks, 8, LANES), F32), fin=((1, n, inner), F32),
        sq=((nb, length, LANES), F32), yn=((nb, length, inner), BF16), part=((tokens, d), BF16),
        rim=((nb, 8, chans), F32), rim16=((nb, 16, chans), BF16), came=((2, nb, n, inner), BF16),
        left=((nb, n, inner), BF16), wx=((d, inner), BF16), wz=((d, inner), BF16), wo=((inner, d), BF16),
        halo=((8, chans), F32), state=((n, inner), F32), run=((1, LANES), F32),
        dyn=((1, length, inner), F32), dz=((nb, length, inner), BF16),
        dots=((length, LANES), F32), g_gain=((8, inner), F32), g_in=((8, d), F32),
        acc=((8, chans), F32), acc_head=((8, LANES), F32), carry=((8, chans), F32),
        edge=((nb, 8, chans), F32), rim_out=((nb, 8, chans), F32), rim_in=((nb, 8, chans), F32),
        stat_out=((2, nb, 8, length), F32), stat_in=((2, nb, tps, 8, length), F32),
        stage=((2, length, wide), BF16), stage_z=((2, bd, max(inner, extra)), BF16), gs=((2, 2, 2, bd, extra), BF16),
        wst=((2 * n + LANES, d), BF16), d_state=((n, inner), F32), cw=((taps, chans), F32), cb=((1, chans), F32),
        gain=((1, inner), F32), dtb=((1, LANES), F32), rate=((1, LANES), F32),
        dsk=((1, inner), F32),

        bc_sum=((2 * n, bd), BF16),
        bc_all=((tps, 2 * n // tps, bd), BF16), tiny=((8, chans), F32), tiny_in=((8, 8, chans), F32),
        tiny_sum=((8, chans), F32), tiny_all=((tps, 8, chans), F32),
    )
    sems = dict(
        cot_load=(nb, tps),
        xs_send=(nb, 2, tps), xs_recv=(nb, tps), cs_send=(nb, 2, tps), cs_recv=(nb, tps),
        w_send=(4, 3), w_recv=(4, 4), r_send=(nb,), r_recv=(nb,), s_send=(2, nb), s_recv=(2, nb),
        e_send=(nb,), e_recv=(nb,), od_send=(nb, 2, tps), od_recv=(nb, 2, tps),
        dd_send=(nb, 2, tps), dd_recv=(nb, 2, tps), t_send=(2, nb, tps), t_recv=(2, nb, tps),
        f_send=(4, 10), f_recv=(4, 10), y_send=(8,), y_recv=(8,), q_send=(tps,), q_recv=(tps,),
        b_send=(tps,), b_recv=(tps,), v_send=(tps,), v_recv=(tps,), loc=(9,), load=(3, 2), outs=(16,),
    )
    names = IN + list(outs) + list(vmem) + list(sems)
    hbm = pl.BlockSpec(memory_space=pl.ANY)
    whole_vmem = pl.BlockSpec(memory_space=pltpu.VMEM)
    got = pl.pallas_call(
        functools.partial(layer_kernel, dims, names),
        in_specs=[pl.BlockSpec(memory_space=pltpu.SMEM)] + [hbm] * 7 + [whole_vmem] * (len(IN) - 8),
        out_specs=[whole_vmem if k in SMALL else hbm for k in outs],
        out_shape=[sds(*v) for v in outs.values()],
        scratch_shapes=[pltpu.VMEM(*v) for v in vmem.values()]
        + [pltpu.SemaphoreType.DMA(v) for v in sems.values()],
        compiler_params=pltpu.CompilerParams(
            collective_id=0, has_side_effects=True, vmem_limit_bytes=63 << 20
        ),
        name="layer",
    )(*args)
    return dict(zip(outs, got))


def ends_kernel(dims, x, cot, o_sum, d_sum, stat, stat2, gain_in, gz_in, gx_in, go_in, gdt_in, gbc_in, tiny,
                out, dx, gz, gx, go, gdt, gbc, g_cw, g_cb, g_ng, g_ig, g_al, g_db, g_ds):
    inner, d, hpd = dims
    wide = x.shape[1]
    tps = d // wide
    tp = lax.axis_index("tp")
    h = x[...].astype(F32)
    out[...] = h + stat[:, 0:1] * o_sum[...].astype(F32)
    inv = stat2[:, 0:1]
    own_gain = gain_in[:, pl.ds(pl.multiple_of(tp * wide, wide), wide)]
    share = inv * own_gain * d_sum[...].astype(F32)
    dx[...] = cot[...].astype(F32) + share - h * (inv * inv * stat2[:, 1:2] * (1.0 / d))
    gz[...] = gz_in[...].astype(F32)
    gx[...] = gx_in[...].astype(F32)
    go[...] = go_in[...].astype(F32).T

    @pl.when(pl.program_id(0) == 0)
    def _():
        gdt[...] = gdt_in[...]
        gbc[...] = gbc_in[...]
        taps = g_cw.shape[0]
        lane = lax.broadcasted_iota(jnp.int32, (8, LANES), 1)
        both, g_norm, heads = 0.0, 0.0, 0.0
        for t in range(tps):
            every = tiny.at[t]
            chan = slice(t * inner, (t + 1) * inner)
            g_cw[:, chan] = every[0:taps, :inner]
            g_cb[:, chan] = every[taps : taps + 1, :inner]
            g_ng[:, chan] = every[5:6, :inner]
            both = both + every[:, inner:]
            g_norm = g_norm + every[:, :inner]
            heads_t = jnp.where(lane < hpd, every[:, inner : inner + LANES], 0.0)
            heads = heads + (pltpu.roll(heads_t, t * hpd, 1) if t else heads_t)
        g_cw[:, tps * inner :] = both[0:taps]
        g_cb[:, tps * inner :] = both[taps : taps + 1]
        for i in range(d // inner):
            cols = slice(i * inner, (i + 1) * inner)
            g_ig[:, cols] = g_norm[6 + i : 7 + i] / gain_in[:, cols]
        count = g_al.shape[1]
        g_al[...] = heads[5:6, :count]
        g_db[...] = heads[6:7, :count]
        g_ds[...] = heads[7:8, :count]


def ends(x, cot, got, gain_in, conv_shape, heads, inner_all, hpd):
    tokens, wide = x.shape
    d = gain_in.shape[1]
    bd, inner = got["gz"].shape
    steps = 2
    rows = tokens // steps

    def by_row(size, width):
        return pl.BlockSpec((size, width), lambda i: (i, 0))

    sds = jax.ShapeDtypeStruct
    shapes = [
        (tokens, wide), (tokens, wide), (bd, inner), (bd, inner), (inner, bd), got["gdt"].shape, got["gbc"].shape,
        conv_shape, (1, conv_shape[1]), (1, inner_all), (1, d), (1, heads), (1, heads), (1, heads),
    ]
    return pl.pallas_call(
        functools.partial(ends_kernel, (inner, d, hpd)),
        grid=(steps,),
        in_specs=[by_row(rows, wide)] * 4
        + [by_row(rows, LANES)] * 2
        + [whole(gain_in.shape)]
        + [by_row(bd // steps, inner)] * 2
        + [pl.BlockSpec((bd, inner // steps), lambda i: (0, i))]
        + [whole(got[k].shape) for k in ("gdt", "gbc", "tiny_o")],
        out_specs=[by_row(rows, wide)] * 2
        + [by_row(bd // steps, inner)] * 2
        + [by_row(inner // steps, bd)]
        + [whole(v) for v in shapes[5:]],
        out_shape=[sds(v, F32) for v in shapes],
        compiler_params=pltpu.CompilerParams(vmem_limit_bytes=63 << 20),
        name="ends",
    )(x, cot, got["out"], got["dx"], got["stat"], got["stat2"], gain_in, got["gz"], got["gx"], got["go"],
      got["gdt"], got["gbc"], got["tiny_o"])


def shift(arr, axis, by):
    peers = lax.axis_size(axis)
    pairs = [(i, i + by) for i in range(peers) if 0 <= i + by < peers]
    return lax.ppermute(arr, axis, pairs)


def heads_row(vec, width=LANES):
    return jnp.pad(vec[None], ((0, 0), (0, width - vec.shape[0])))


def on_device(
    x_in,
    cotangent,
    offsets,
    in_gain,
    w_z,
    w_x,
    w_dt,
    w_bc,
    conv_w,
    conv_b,
    dt_bias,
    a_log,
    d_skip,
    norm_gain,
    w_out,
):
    batches, seq_count, length, width_dev = x_in.shape
    nb = batches * seq_count
    tokens = nb * length
    tp_rank = lax.axis_index("tp")
    ctx_rank = lax.axis_index("ctx")
    peers = lax.axis_size("ctx")
    inner = w_z.shape[1]
    heads = w_dt.shape[1]
    width = inner // heads
    model = in_gain.shape[0]
    inner_all = norm_gain.shape[0]
    pair = conv_w.shape[1] - inner_all
    n = pair // 2
    taps = conv_w.shape[0]

    def mine(arr, size, axis):
        return lax.dynamic_slice_in_dim(arr, tp_rank * size, size, axis)

    cw = jnp.concatenate([mine(conv_w, inner, 1), conv_w[:, inner_all:]], axis=1)
    cb = jnp.concatenate([mine(conv_b, inner, 0), conv_b[inner_all:]])[None]
    gain = mine(norm_gain, inner, 0)[None]
    gain_in = mine(in_gain, width_dev, 0)
    dtb = heads_row(mine(dt_bias, heads, 0))
    rate = heads_row(-jnp.exp(mine(a_log, heads, 0)))
    dsk = jnp.repeat(mine(d_skip, heads, 0), width)[None]
    pos = (ctx_rank * length).astype(jnp.int32)[None]
    offs = offsets.reshape(nb, offsets.shape[-1])

    x_own = x_in.reshape(tokens, width_dev)
    cot_own = cotangent.reshape(tokens, width_dev)
    tps = lax.axis_size("tp")
    def chained(start, lend, by):
        came = jnp.zeros_like(start)
        for k in range(peers - 1):
            sent = start if k == 0 else start + lend * came
            came = shift(sent.astype(BF16), "ctx", by).astype(F32)
        return came

    def ending(lead):
        return jnp.repeat(lead[:, length - 1, :heads], width, axis=-1)[:, None]

    if peers == 2 and lax.axis_size("fsdp") == 4 and nb == 2 and heads % 16 == 0:
        got = layer(
            (offs, x_own, cot_own, w_x, w_z, w_out, w_bc.T, w_dt.T, in_gain[None], conv_w, conv_b[None],
             dt_bias[None], a_log[None], d_skip[None], norm_gain[None]),
            nb, length, heads, width, n, tps, inner_all,
        )
        shape = (batches, seq_count, length, width_dev)
        out, d_x, g_z, g_x, g_out, g_dt, g_bc, g_cw, g_cb, g_ng, g_ig, g_al, g_db, g_ds = ends(
            x_own, cot_own, got, in_gain[None], conv_w.shape, dt_bias.shape[0], inner_all, heads
        )
        return (
            out.reshape(shape),
            d_x.reshape(shape),
            g_ig.reshape(-1),
            g_z,
            g_x,
            g_dt.T,
            g_bc.T,
            g_cw,
            g_cb.reshape(-1),
            g_db.reshape(-1),
            g_al.reshape(-1),
            g_ds.reshape(-1),
            g_ng.reshape(-1),
            g_out,
        )
    small = jnp.concatenate([w_bc, w_dt], axis=1)
    small = lax.all_gather(small, "fsdp", axis=0, tiled=True)
    wdt = jnp.pad(small[:, pair // tps :], ((0, 0), (0, LANES - heads)))
    wbc = lax.all_gather(small[:, : pair // tps], "tp", axis=1, tiled=True)

    x_all = lax.all_gather(x_own, "tp", axis=1, tiled=True)
    wx = lax.all_gather(w_x, "fsdp", axis=0, tiled=True)
    wz = lax.all_gather(w_z, "fsdp", axis=0, tiled=True)
    wo = lax.all_gather(w_out, "fsdp", axis=1, tiled=True)
    cot_all = lax.all_gather(cot_own, "tp", axis=1, tiled=True)
    resid = x_all.astype(F32)
    r1 = lax.rsqrt(jnp.mean(resid * resid, axis=1, keepdims=True) + EPSILON)
    xn = (resid * r1 * in_gain).astype(BF16)
    pre = jnp.concatenate([mm(xn, wx).astype(BF16), mm(xn, wbc).astype(BF16)], axis=1)
    pre = pre.reshape(nb, length, inner + pair)
    dtr = mm(xn, wdt).reshape(nb, length, LANES)
    z = mm(xn, wz).reshape(nb, length, inner)
    rim = shift(pre[:, length - 8 :], "ctx", 1).astype(F32)
    y, rd, lead, st, lead0, fin = scan_forward(
        offs, pos, pre, rim, dtr, cw, cb, dtb, rate, dsk, width, n
    )
    s_in = chained(fin, ending(lead), 1)
    y, ygg, sq, st = gate_forward(y, rd, lead, lead0, st, s_in, z, gain, width)
    part = mm(ygg.reshape(tokens, inner), wo).astype(BF16)
    lend = ending(lead)
    share = lax.psum_scatter(part, "tp", scatter_dimension=1, tiled=True)
    dyn = mm(cot_all, wo, NT).reshape(nb, length, inner)
    dot = jnp.sum(dyn * gain * y * jax.nn.silu(z), axis=2)
    stat = jnp.stack([sq[..., 0], dot])
    stat = jnp.sum(lax.all_gather(stat, "tp"), axis=0)
    r2 = lax.rsqrt(stat[0] / inner_all + EPSILON)
    out = x_own.astype(F32) + r2.reshape(tokens, 1) * share.astype(F32)
    stat = jnp.pad(jnp.stack([r2, stat[1]], axis=-1), ((0, 0), (0, 0), (0, LANES - 2)))
    dy, dz, yn, g_gain, g_state = gate_backward(dyn, y, z, stat, gain, rd, lead, width, inner_all)
    dz = dz.reshape(tokens, inner)
    yn = yn.reshape(tokens, inner)
    d_in = chained(g_state, lend, -1)
    rows = ("ctx", "fsdp")

    def scattered(grad):
        return lax.psum_scatter(grad.astype(BF16), rows, scatter_dimension=0, tiled=True)

    g_out = scattered(mm(cot_all, yn, TN)).astype(F32).T
    g_z = scattered(mm(xn, dz, TN)).astype(F32)
    dcat, ddt, edge, rim_grad, acc, acc_head = scan_backward(
        offs, pos, pre, rim, dtr, y, dy, st, d_in, cw, cb, dtb, rate, dsk, width
    )
    edge = (edge + shift(rim_grad, "ctx", -1)).astype(BF16)
    dcat = lax.dynamic_update_slice(dcat, edge, (0, length - 8, 0)).reshape(tokens, inner + pair)
    ddt = ddt.reshape(tokens, LANES)
    dxn = mm(dz, wz, NT) + mm(dcat[:, :inner], wx, NT) + mm(dcat[:, inner:], wbc, NT) + mm(ddt, wdt, NT)
    dxn = lax.psum_scatter(dxn.astype(BF16), "tp", scatter_dimension=1, tiled=True).astype(F32)
    g_xbc = scattered(jnp.concatenate([mm(xn, dcat, TN), mm(xn, ddt, TN)[:, :heads]], axis=1))
    g_x = g_xbc[:, :inner].astype(F32)
    g_dt = g_xbc[:, inner + pair :].astype(F32)
    g_bc = lax.psum_scatter(
        g_xbc[:, inner : inner + pair].astype(F32), "tp", scatter_dimension=1, tiled=True
    )
    h_own = x_own.astype(F32)
    scaled = dxn * gain_in
    in_dot = jnp.sum(lax.all_gather(jnp.sum(scaled * h_own, axis=1), "tp"), axis=0)[:, None]
    g_in = jnp.sum(dxn * h_own * r1, axis=0)
    d_x = cot_own.astype(F32) + r1 * scaled - h_own * r1**3 * in_dot / model
    pieces = [
        g_in,
        acc[:taps, :inner].reshape(-1),
        acc[taps, :inner],
        g_gain[0],
        acc_head[1, :heads],
        acc_head[0, :heads],
        acc[taps + 1, :inner].reshape(heads, width).sum(axis=1),
        acc[:taps, inner:].reshape(-1),
        acc[taps, inner:],
    ]
    sizes = [p.shape[0] for p in pieces]
    packed = jnp.sum(lax.all_gather(jnp.concatenate(pieces), rows), axis=0)
    packed = lax.all_gather(packed, "tp")
    parts, start = [], 0
    for size in sizes:
        parts.append(packed[:, start : start + size])
        start += size
    tp = packed.shape[0]
    g_cw = jnp.concatenate(
        [
            parts[1].reshape(tp, taps, inner).transpose(1, 0, 2).reshape(taps, inner_all),
            jnp.sum(parts[7], axis=0).reshape(taps, pair),
        ],
        axis=1,
    )
    g_cb = jnp.concatenate([parts[2].reshape(-1), jnp.sum(parts[8], axis=0)])
    shape = (batches, seq_count, length, width_dev)
    return (
        out.reshape(shape),
        d_x.reshape(shape),
        parts[0].reshape(-1),
        g_z,
        g_x,
        g_dt,
        g_bc,
        g_cw,
        g_cb,
        parts[4].reshape(-1),
        parts[5].reshape(-1),
        parts[6].reshape(-1),
        parts[3].reshape(-1),
        g_out,
    )


def solution(mesh):
    stream = P(None, "fsdp", "ctx", "tp")
    weight = P("fsdp", "tp")
    grad = P(("ctx", "fsdp"), "tp")
    in_specs = (
        (stream, stream, P(None, "fsdp", None), P())
        + (weight,) * 4
        + (P(),) * 6
        + (P("tp", "fsdp"),)
    )
    out_specs = (
        (stream, stream, P()) + (grad,) * 4 + (P(),) * 6 + (P("tp", ("ctx", "fsdp")),)
    )
    return jax.shard_map(
        on_device, mesh=mesh, in_specs=in_specs, out_specs=out_specs, check_vma=False
    )
```
